32 devices in a mesh: ctx: 8 (over z, y), hv: 4 (over x, core).
Axes of the slice: x: 2, y: 2, z: 4, core: 2. Of those that a mesh axis runs over, the one named last changes fastest.
Arguments:
- queries: bfloat16 [8192, 8, 256], P(('ctx', 'hv')), may hold values from -6 to 6
- key_vectors: bfloat16 [8192, 8, 256], P(('ctx', 'hv')), may hold values from -6 to 6
- value_vectors: bfloat16 [8192, 8, 512], P(('ctx', 'hv')), may hold values from -6 to 6
- input_gate: bfloat16 [8192, 8], P(('ctx', 'hv')), may hold values from -10 to 240
- forget_gate: bfloat16 [8192, 8], P(('ctx', 'hv')), may hold values from -2 to 16
- doc_ids: int32 [8192], P('ctx'), may hold values from 0 to 3, never falling along the last dimension, each value on 1 to 4096 neighbouring positions
Outputs:
- hidden_states: bfloat16 [8192, 8, 512], P(('ctx', 'hv'))
The draws below stay inside these ranges and needn't reach their ends.
Inputs may be any that keep to these rules, and one draw needn't show every extreme that they name: `doc_ids`: document numbers never fall along the sequence; each of the 4 documents has 1 to 4096 tokens and one has exactly 4096.
All inputs are finite; a program needn't handle non-finite values.
Results may differ from the reference program's by a relative error of at most 0.0034.
Values may be sent and summed in bfloat16 or wider, within the bound.
No kernel may reach another device: no remote copies, remote signals or barrier semaphores. Data moves between devices by JAX's collectives and lax.ppermute only.
A program may use at most 128 MiB of HBM per device.

```python
import math
import jax
import jax.numpy as jnp
import numpy as np
from jax import lax

HEAD_TOTAL = 8
DK = 256
DV = 512
TOK_DEV = 256
DOCS = 4
SEQUENCE_TOKENS = 8192


def draw_forget_gate(key, part):
    every_key = jax.random.split(key, 6)
    slow_share = 0.5
    slow_heads = jax.random.uniform(every_key[0], (HEAD_TOTAL,)) < slow_share
    slow_rate = jnp.exp(jax.random.uniform(every_key[1], (HEAD_TOTAL,), minval=math.log(0.3 / SEQUENCE_TOKENS), maxval=math.log(2.0 / SEQUENCE_TOKENS)))
    fast_rate = jnp.exp(jax.random.uniform(every_key[2], (HEAD_TOTAL,), minval=math.log(1.0 / 50.0), maxval=math.log(1.0 / 20.0)))
    baseline_rate = jnp.where(slow_heads, slow_rate, fast_rate)
    jaggedness = jnp.exp(jax.random.uniform(every_key[3], (SEQUENCE_TOKENS, HEAD_TOTAL), minval=math.log(0.5), maxval=math.log(2.0)))
    spike_events = jax.random.uniform(every_key[4], (SEQUENCE_TOKENS, HEAD_TOTAL)) < 4.0 / SEQUENCE_TOKENS
    spike_rate = jax.random.uniform(every_key[5], (SEQUENCE_TOKENS, HEAD_TOTAL), minval=0.22, maxval=0.69)
    combined_rate = baseline_rate[None, :] * jaggedness + jnp.where(spike_events, spike_rate, 0.0)
    preact = -combined_rate - jnp.log(-jnp.expm1(-combined_rate))
    return preact.astype(jnp.bfloat16)


def draw_input_gate(key, part):
    every_key = jax.random.split(key, 1)
    values_out = jnp.clip(2.0 * jax.random.normal(every_key[0], (SEQUENCE_TOKENS, HEAD_TOTAL)), -10.0, 10.0)
    return values_out.astype(jnp.bfloat16)


def level_of(key, shape, cuts, smallest, high):
    def one(position, blocks):
        draws = jax.random.uniform(jax.random.fold_in(jax.random.fold_in(key, 6), position), (blocks,), jnp.float32, smallest / len(cuts), high / len(cuts))
        return jnp.repeat(jnp.exp(draws), shape[position] // blocks).reshape((-1,) + (1,) * (len(shape) - position - 1))

    loudness = one(*cuts[0])
    for cut in cuts[1:]:
        loudness = loudness * one(*cut)
    return loudness


def split_up(number_of, total, most, slope):
    portions = [(1 << 20) // math.isqrt(rank ** slope) + 1 for rank in range(2, number_of + 1)]
    surplus, counts = total - most - (number_of - 1), [1] * (number_of - 1)
    while surplus > 0:
        candidates = [i for i in range(number_of - 1) if counts[i] < most]
        pool, left = sum([portions[i] for i in candidates]), surplus
        for i in candidates:
            extra = min(most - counts[i], max(1, left * portions[i] // pool), surplus)
            counts[i] = counts[i] + extra
            surplus = surplus - extra
    return np.array([most] + counts)


def uneven_parts(key, number_of, total, limit, slope):
    if number_of == 2:
        one = jax.random.randint(key, (), max(1, total - limit), min(limit, total - 1) + 1)
        return jnp.stack([one, total - one])
    tallies = jnp.asarray(split_up(number_of, total, limit, slope), jnp.int32)
    couples = (number_of - 1) // 2
    giver, receiver = tallies[1:1 + 2 * couples:2], tallies[2:2 + 2 * couples:2]
    margin = jnp.minimum(giver - 1, limit - receiver)
    shifted = jax.random.randint(jax.random.fold_in(key, 1), (couples,), 0, 1 << 20) % (margin + 1)
    tallies = tallies.at[1:1 + 2 * couples:2].set(giver - shifted).at[2:2 + 2 * couples:2].set(receiver + shifted)
    return tallies[jax.random.permutation(jax.random.fold_in(key, 2), number_of)]


def scatter_about(own_key, shape, spread, bound, shards=(), dtype=jnp.bfloat16):
    values = jax.random.normal(own_key, shape, jnp.float32) * spread
    if len(shards) > 0:
        values = level_of(own_key, shape, shards, -0.22, 0.18) * values
    return jnp.clip(values, min=-bound, max=bound).astype(dtype)


def setup_inputs(seed: int = 0) -> dict:
    key_of = jax.random.split(jax.random.key(seed), 7)
    return {
        "queries": scatter_about(key_of[0], (SEQUENCE_TOKENS, HEAD_TOTAL, DK), 1.0, 6.0, ((0, 32),)),
        "key_vectors": scatter_about(key_of[1], (SEQUENCE_TOKENS, HEAD_TOTAL, DK), 1.0, 6.0, ((0, 32),)),
        "value_vectors": scatter_about(key_of[2], (SEQUENCE_TOKENS, HEAD_TOTAL, DV), 1.0, 6.0, ((0, 32),)),
        "input_gate": draw_input_gate(jax.random.fold_in(key_of[6], 71), 0),
        "forget_gate": draw_forget_gate(jax.random.fold_in(key_of[6], 71), 0),
        "doc_ids": jnp.searchsorted(jnp.cumsum(uneven_parts(key_of[5], DOCS, SEQUENCE_TOKENS, SEQUENCE_TOKENS // 2, 0)), jnp.arange(SEQUENCE_TOKENS), side="right").astype(jnp.int32),
    }


FLOOR_NEG = -1e+30
TOP_PRECISION = lax.Precision.HIGHEST

def combine_memory(earlier, later):
    severed_e, decay_e, memory_e, normalizer_e, top_e = earlier
    severed_l, decay_l, memory_l, normalizer_l, top_l = later
    keeping = 1.0 - severed_l
    reached = top_e + decay_l
    stabilizer = jnp.where(severed_l > 0.5, top_l, jnp.maximum(reached, top_l))
    old_factor = keeping * jnp.exp(jnp.minimum(reached - stabilizer, 0.0))
    new_factor = jnp.exp(top_l - stabilizer)
    memory_matrix = old_factor[:, None, None] * memory_e + new_factor[:, None, None] * memory_l
    normalizer = old_factor[:, None] * normalizer_e + new_factor[:, None] * normalizer_l
    return (jnp.maximum(severed_e, severed_l), decay_e + decay_l, memory_matrix, normalizer, stabilizer)

def group_summary(k_group, value_group, gate_in, decay_sum, id_group, alive):
    last_doc = id_group == id_group[-1]
    exponent = decay_sum[-1][None, :] - decay_sum + gate_in
    exponent = jnp.where(last_doc[:, None], exponent, FLOOR_NEG)
    stabilizer = lax.optimization_barrier(jnp.max(exponent, axis=0))
    factor = jnp.exp(exponent - stabilizer[None, :])
    rescaled_values = k_group.astype(jnp.float32) * factor[:, :, None]
    memory_matrix = jnp.einsum('lfj,lfm->fjm', rescaled_values, value_group.astype(jnp.float32), precision=TOP_PRECISION)
    normalizer = lax.optimization_barrier(jnp.sum(rescaled_values, axis=0))
    severed = (1.0 - alive[-1]) * jnp.ones_like(stabilizer)
    return (severed, decay_sum[-1], memory_matrix, normalizer, stabilizer)

def group_output(q_group, k_group, value_group, gate_in, decay_sum, id_group, alive, memory_matrix, normalizer, carried_top):
    length = q_group.shape[0]
    key_scaling = 1.0 / math.sqrt(q_group.shape[2])
    block_len = min(512, length)
    pieces = []
    for offset in range(0, length, block_len):
        finish = offset + block_len
        query_block = q_group[offset:finish].astype(jnp.float32)
        scores = jnp.einsum('bhd,shd->hbs', query_block, k_group[:finish].astype(jnp.float32), precision=TOP_PRECISION) * key_scaling
        query_decay = decay_sum[offset:finish].T
        source_term = (gate_in[:finish] - decay_sum[:finish]).T
        exponent = query_decay[:, :, None] + source_term[:, None, :]
        query_pos = offset + jnp.arange(block_len)
        source_pos = jnp.arange(finish)
        allowed = (source_pos[None, :] <= query_pos[:, None]) & (id_group[offset:finish][:, None] == id_group[:finish][None, :])
        exponent = jnp.where(allowed[None], exponent, FLOOR_NEG)
        carried = jnp.where(alive[offset:finish][None, :] > 0.5, query_decay + carried_top[:, None], FLOOR_NEG)
        stabilizer = jnp.maximum(lax.optimization_barrier(jnp.max(exponent, axis=2)), carried)
        weights = scores * jnp.exp(exponent - stabilizer[:, :, None])
        denominator = lax.optimization_barrier(jnp.sum(weights, axis=2))
        rounded = weights.astype(jnp.bfloat16).astype(jnp.float32)
        upper_term = jnp.einsum('hbs,shv->hbv', rounded, value_group[:finish].astype(jnp.float32), precision=TOP_PRECISION)
        retained_factor = jnp.exp(carried - stabilizer)
        upper_term = upper_term + retained_factor[:, :, None] * key_scaling * jnp.einsum('zsj,sjf->szf', query_block, memory_matrix, precision=TOP_PRECISION)
        denominator = denominator + retained_factor * key_scaling * jnp.einsum('bhk,hk->hb', query_block, normalizer, precision=TOP_PRECISION)
        ratio = upper_term / jnp.maximum(jnp.abs(denominator), 1.0)[:, :, None]
        pieces.append(jnp.transpose(ratio, (1, 0, 2)).astype(jnp.bfloat16))
    return jnp.concatenate(pieces, axis=0)

def reference(queries, key_vectors, value_vectors, input_gate, forget_gate, doc_ids):
    total_len, head_count, key_width = queries.shape
    value_width = value_vectors.shape[2]
    group_len = TOK_DEV
    count = total_len // group_len

    def shape_groups(array_in):
        return array_in.reshape((count, group_len) + array_in.shape[1:])
    log_forget = jax.nn.log_sigmoid(forget_gate.astype(jnp.float32))
    before_ids = jnp.concatenate([jnp.full((1,), -1, jnp.int32), doc_ids[:-1].astype(jnp.int32)])
    inputs = (shape_groups(queries), shape_groups(key_vectors), shape_groups(value_vectors), shape_groups(input_gate.astype(jnp.float32)), shape_groups(log_forget), shape_groups(doc_ids.astype(jnp.int32)), shape_groups(before_ids))
    zero_heads = jnp.zeros((head_count,), jnp.float32)
    initial = (zero_heads, zero_heads, jnp.zeros((head_count, key_width, value_width), jnp.float32), jnp.zeros((head_count, key_width), jnp.float32), jnp.full((head_count,), FLOOR_NEG, jnp.float32))

    def advance(state, element):
        q_c, k_c, v_c, gate_c, forget_c, id_c, before_c = element
        decay_sum = jnp.cumsum(forget_c, axis=0)
        alive = (id_c == before_c[0]).astype(jnp.float32)
        produced = group_output(q_c, k_c, v_c, gate_c, decay_sum, id_c, alive, state[2], state[3], state[4])
        summary = group_summary(k_c, v_c, gate_c, decay_sum, id_c, alive)
        return (combine_memory(state, summary), produced)
    final_state, outputs = lax.scan(advance, initial, inputs)
    return outputs.reshape((total_len, head_count, value_width))
```

```python
import functools

import jax
import jax.numpy as jnp
from jax import lax
from jax.experimental import pallas as pl
from jax.experimental.pallas import tpu as pltpu
from jax.sharding import PartitionSpec as P

AXES = ("ctx", "hv")
FLOOR_NEG = -1e30
META = 16
LANES = 128
F32, BF16 = jnp.float32, jnp.bfloat16

NN = (((1,), (0,)), ((), ()))
NT = (((1,), (1,)), ((), ()))


def dot(a, b, dims=NN):
    return lax.dot_general(a, b, dims, preferred_element_type=F32)


def split3(x):
    hi = x.astype(BF16).astype(F32)
    mid = (x - hi).astype(BF16).astype(F32)
    return hi, mid, (x - hi - mid).astype(BF16).astype(F32)


def iota(shape, dim):
    return lax.broadcasted_iota(jnp.int32, shape, dim)


def meta_rows(normalizer, top, decay, doc):
    line = jnp.concatenate([normalizer, top, decay], axis=1)
    hi, mid, low = split3(line)
    width = line.shape[1]
    doc_line = jnp.concatenate([doc] * (width // LANES), axis=1)
    row = iota((META, width), 0)
    rows = jnp.where(row == 0, hi, jnp.where(row == 1, mid, jnp.where(row == 2, low, 0.0)))
    return jnp.where(row == 3, doc_line, rows).astype(BF16)


def read_meta(ref):
    key_width = ref.shape[0] - META
    rows = ref[key_width:, :].astype(F32)
    line = (rows[2:3] + rows[1:2]) + rows[0:1]
    return (
        line[:, :key_width],
        line[:, key_width : key_width + LANES],
        line[:, key_width + LANES : key_width + 2 * LANES],
        rows[3:4, :LANES],
    )


def weighted(refs, coefs):
    key_width, value_width = refs[0].shape[0] - META, refs[0].shape[1]
    total = None
    for ref, coef in zip(refs, coefs, strict=True):
        wide = jnp.concatenate([coef] * (value_width // LANES), axis=1)
        term = wide * ref[:key_width, :].astype(F32)
        total = term if total is None else total + term
    return total


def gate_rows(core, own_ref, other_ref, heads):
    own, other = own_ref[...].astype(F32), other_ref[...].astype(F32)
    both = jnp.concatenate(
        [jnp.where(core == 0, own, other), jnp.where(core == 0, other, own)], axis=1
    )
    gate_in, forget = both[:heads], both[heads:]
    log_forget = jnp.minimum(forget, 0.0) - jnp.log1p(jnp.exp(-jnp.abs(forget)))
    length = both.shape[1]
    upto = (iota((length, length), 0) <= iota((length, length), 1)).astype(BF16)
    pieces = dot(jnp.concatenate(split3(log_forget), axis=0).astype(BF16), upto)
    decay = (pieces[2 * heads :] + pieces[heads : 2 * heads]) + pieces[:heads]
    return gate_in, decay


def relayout_kernel(half, q_ref, k_ref, v_ref, in_ref, forget_ref, scalars, *outs):
    core = scalars[1]
    q_keep, k_keep, v_keep, q_send, k_send, v_send, gates = outs
    heads = in_ref.shape[0]
    gates[:heads, :] = in_ref[...]
    gates[heads:, :] = forget_ref[...]

    def body(first, second):
        for source, low, high in zip((q_ref, k_ref, v_ref), first, second, strict=True):
            for h in range(half):
                low[h] = source[:, h, :]
                high[h] = source[:, half + h, :]

    keep, send = (q_keep, k_keep, v_keep), (q_send, k_send, v_send)

    @pl.when(core == 0)
    def _():
        body(keep, send)

    @pl.when(core != 0)
    def _():
        body(send, keep)


def state_kernel(
    heads, scalars, k_own, v_own, k_oth, v_oth, g_own, g_oth, ids_ref, *rest
):
    outs, (factors, tops, decays, payload) = rest[:-4], rest[-4:]
    step = pl.program_id(0)
    core = scalars[1]
    half = heads // 2
    tokens = k_own.shape[1]
    key_width, value_width = k_own.shape[2], v_own.shape[2]
    length = 2 * tokens

    @pl.when(step == 0)
    def _():
        gate_in, decay = gate_rows(core, g_own, g_oth, heads)
        ids = ids_ref[...]
        exponent = decay[:, length - 1 :] - decay + gate_in
        exponent = jnp.where(ids == ids[:, length - 1 :], exponent, FLOOR_NEG)
        top = jnp.max(exponent, axis=1, keepdims=True)
        factors[...] = jnp.exp(exponent - top)
        tops[...] = jnp.broadcast_to(top, tops.shape)
        decays[...] = jnp.broadcast_to(decay[:, length - 1 :], decays.shape)

    head = half * core + jnp.bitwise_xor(scalars[0], step)
    row = factors[pl.ds(head, 1), :]
    first, last = row[:, :tokens], row[:, tokens:]
    total, normal = None, None
    for k_ref, v_ref, f in (
        (k_own, v_own, jnp.where(core == 0, first, last)),
        (k_oth, v_oth, jnp.where(core == 0, last, first)),
    ):
        keys, values = k_ref[0], v_ref[0]
        scaled = keys.astype(F32).T * f
        high = scaled.astype(BF16)
        low = (scaled - high.astype(F32)).astype(BF16)
        part = dot(low, values) + dot(high, values)
        pieces = jnp.concatenate(split3(f) + (jnp.zeros((META - 3, tokens), F32),), axis=0)
        sums = dot(pieces.astype(BF16), keys)
        line = (sums[2:3] + sums[1:2]) + sums[0:1]
        total = part if total is None else total + part
        normal = line if normal is None else normal + line
    doc = jnp.broadcast_to(ids_ref[:, length - 1 :].astype(F32) + 1.0, (1, LANES))
    payload[:key_width, :] = total.astype(BF16)
    payload[key_width:, :] = meta_rows(
        normal, tops[pl.ds(head, 1), :], decays[pl.ds(head, 1), :], doc
    )
    for i, out in enumerate(outs):

        @pl.when(step == i)
        def _(out=out):
            out[...] = payload[...]


def total_kernel(group, scalars, *refs):
    states, out = refs[:group], refs[group]
    place = [jnp.bitwise_xor(scalars[0], r) for r in range(group)]
    metas = [read_meta(ref) for ref in states]
    zero = jnp.zeros((1, LANES), F32)
    doc = sum((jnp.where(place[r] == group - 1, metas[r][3], zero) for r in range(group)), zero)
    reached = []
    for r in range(group):
        after = sum(
            (jnp.where(place[i] > place[r], metas[i][2], zero) for i in range(group)), zero
        )
        reached.append(jnp.where(metas[r][3] == doc, metas[r][1] + after, FLOOR_NEG))
    top = functools.reduce(jnp.maximum, reached)
    coefs = [
        jnp.where(metas[r][3] == doc, jnp.exp(reached[r] - top), 0.0) for r in range(group)
    ]
    key_width = out.shape[0] - META
    out[:key_width, :] = weighted(states, coefs).astype(BF16)
    normal = sum(
        jnp.concatenate([coefs[r]] * (key_width // LANES), axis=1) * metas[r][0]
        for r in range(group)
    )
    decay = sum((metas[r][2] for r in range(group)), zero)
    out[key_width:, :] = meta_rows(normal, top, decay, doc)


def entering_kernel(group, reach, scalars, *refs):
    states, totals, outs = refs[:group], refs[group : group + reach], refs[group + reach :]
    place = [jnp.bitwise_xor(scalars[0], r) for r in range(group)]
    metas = [read_meta(ref) for ref in states]
    far = [read_meta(ref) for ref in totals]
    zero = jnp.zeros((1, LANES), F32)
    key_width = outs[0].shape[0] - META
    for r in range(group):
        mine = place[r]
        doc = jnp.where(mine == 0, far[0][3], zero)
        for i in range(group):
            doc = doc + jnp.where(place[i] == mine - 1, metas[i][3], zero)
        passed = sum(
            (jnp.where(place[i] < mine, metas[i][2], zero) for i in range(group)), zero
        )
        sources, reached, normals = [], [], []
        for i in range(group):
            if i == r:
                continue
            between = sum(
                (
                    jnp.where((place[n] < mine) & (place[n] > place[i]), metas[n][2], zero)
                    for n in range(group)
                ),
                zero,
            )
            there = jnp.where(place[i] < mine, metas[i][3], -1.0)
            alive = there == doc
            sources.append(states[i])
            normals.append(metas[i][0])
            reached.append((alive, jnp.where(alive, metas[i][1] + between, FLOOR_NEG)))
        for d in range(reach):
            alive = (far[d][3] == doc) & (far[d][3] > 0.5)
            sources.append(totals[d])
            normals.append(far[d][0])
            reached.append((alive, jnp.where(alive, far[d][1] + passed, FLOOR_NEG)))
            passed = passed + far[d][2]
        top = functools.reduce(jnp.maximum, [value for _, value in reached])
        coefs = [jnp.where(alive, jnp.exp(value - top), 0.0) for alive, value in reached]
        outs[r][:key_width, :] = weighted(sources, coefs).astype(BF16)
        normal = sum(
            jnp.concatenate([coef] * (key_width // LANES), axis=1) * line
            for coef, line in zip(coefs, normals, strict=True)
        )
        outs[r][key_width:, :] = meta_rows(normal, top, zero, doc)


def output_kernel(heads, group, scalars, *refs):
    q_own, k_own, v_own, q_oth, k_oth, v_oth, g_own, g_oth, ids_ref = refs[:9]
    entering = refs[9 : 9 + group]
    keep, send, source_rows, columns, bias, payload = refs[9 + group :]
    step = pl.program_id(0)
    core = scalars[1]
    half = heads // 2
    tokens, key_width = q_own.shape[1], q_own.shape[2]
    length = 2 * tokens
    scaling = key_width**-0.5

    @pl.when(step == 0)
    def _():
        gate_in, decay = gate_rows(core, g_own, g_oth, heads)
        source_rows[...] = gate_in - decay
        docs = ids_ref[...].astype(F32) + 1.0
        filler = jnp.zeros((LANES - heads - 1, length), F32)
        turned = jnp.concatenate([decay, docs, filler], axis=0).T
        columns[...] = turned
        same = turned[:, heads : heads + 1] == docs
        causal = iota((length, length), 0) >= iota((length, length), 1)
        bias[...] = jnp.where(same & causal, 0.0, FLOOR_NEG)

    for i, ref in enumerate(entering):

        @pl.when(step == i)
        def _(ref=ref):
            payload[...] = ref[...]

    head = half * core + jnp.bitwise_xor(scalars[0], step)
    is_first = core == 0
    source = source_rows[pl.ds(head, 1), :]
    lane = iota((length, LANES), 1)
    turned = columns[...]
    decay = jnp.sum(jnp.where(lane == head, turned, 0.0), axis=1, keepdims=True)
    docs = turned[:, heads : heads + 1]
    normal, top, _, doc = read_meta(payload)
    carried = jnp.where(docs == doc[:, :1], decay + top[:, :1], FLOOR_NEG)
    pieces = jnp.concatenate(split3(normal) + (jnp.zeros((META - 3, key_width), F32),), axis=0)
    pieces = pieces.astype(BF16)
    memory = payload[:key_width, :]

    def ordered(own, other):
        own, other = own[0], other[0]
        return jnp.where(is_first, own, other), jnp.where(is_first, other, own)

    queries, keys, values = ordered(q_own, q_oth), ordered(k_own, k_oth), ordered(v_own, v_oth)
    results = []
    for block in range(2):
        rows = slice(block * tokens, (block + 1) * tokens)
        query = queries[block]
        stabilizer = carried[rows]
        exponents = []
        for s in range(block + 1):
            cols = slice(s * tokens, (s + 1) * tokens)
            exponent = (decay[rows] + source[:, cols]) + bias[rows, cols]
            exponents.append(exponent)
            stabilizer = jnp.maximum(stabilizer, jnp.max(exponent, axis=1, keepdims=True))
        retained = jnp.exp(carried[rows] - stabilizer) * scaling
        seen = dot(query, pieces, NT)
        denominator = retained * ((seen[:, 2:3] + seen[:, 1:2]) + seen[:, 0:1])
        numerator = retained * dot(query, memory)
        for s in range(block + 1):
            weights = dot(query, keys[s], NT) * scaling * jnp.exp(exponents[s] - stabilizer)
            denominator = denominator + jnp.sum(weights, axis=1, keepdims=True)
            high = weights.astype(BF16)
            numerator = numerator + dot(high, values[s])
            if s < block:
                low = (weights - high.astype(F32)).astype(BF16)
                numerator = numerator + dot(low, values[s])
        results.append((numerator / jnp.maximum(jnp.abs(denominator), 1.0)).astype(BF16))
    keep[0] = jnp.where(is_first, results[0], results[1])
    send[0] = jnp.where(is_first, results[1], results[0])


def merge_kernel(scalars, own_ref, other_ref, out_ref):
    half = own_ref.shape[0]

    def body(low, high):
        for h in range(half):
            out_ref[:, h, :] = low[h]
            out_ref[:, half + h, :] = high[h]

    @pl.when(scalars[1] == 0)
    def _():
        body(own_ref, other_ref)

    @pl.when(scalars[1] != 0)
    def _():
        body(other_ref, own_ref)


def whole(shape):
    return pl.BlockSpec(shape, lambda *_: (0,) * len(shape))


def params():
    return pltpu.CompilerParams(vmem_limit_bytes=56 * 2**20)


SMEM = pl.BlockSpec(memory_space=pltpu.SMEM)


def shape_of(*dims, dtype=BF16):
    return jax.ShapeDtypeStruct(dims, dtype)


def local(devices, queries, key_vectors, value_vectors, input_gate, forget_gate, doc_ids):
    tokens, heads, key_width = queries.shape
    value_width = value_vectors.shape[2]
    half = heads // 2
    group = half
    chips = devices // 2
    levels = chips // group
    reach = max(1, levels // 2)
    ctx, hv = lax.axis_index("ctx"), lax.axis_index("hv")
    chip = ctx * (lax.axis_size("hv") // 2) + hv // 2
    scalars = jnp.stack([chip % group, hv % 2]).astype(jnp.int32)
    ids = lax.dynamic_slice(doc_ids, ((hv // 2) * 2 * tokens,), (2 * tokens,))[None, :]

    def swap_cores(x):
        return lax.ppermute(x, AXES, [(d, d ^ 1) for d in range(devices)])

    def in_group(x, r):
        pairs = [(d, d ^ (2 * r)) for d in range(devices)]
        return lax.ppermute(x, AXES, pairs)

    def to_later(x, levels_on):
        jump = 2 * group * levels_on
        return lax.ppermute(x, AXES, [(d, d + jump) for d in range(devices - jump)])

    rows = key_width + META
    narrow, wide = (half, tokens, key_width), (half, tokens, value_width)
    q_keep, k_keep, v_keep, q_send, k_send, v_send, gates = pl.pallas_call(
        functools.partial(relayout_kernel, half),
        in_specs=[
            whole(queries.shape),
            whole(key_vectors.shape),
            whole(value_vectors.shape),
            whole((heads, tokens)),
            whole((heads, tokens)),
            SMEM,
        ],
        out_specs=[whole(s) for s in (narrow, narrow, wide) * 2 + ((2 * heads, tokens),)],
        out_shape=[shape_of(*s) for s in (narrow, narrow, wide) * 2 + ((2 * heads, tokens),)],
        compiler_params=params(),
        name="relayout",
    )(queries, key_vectors, value_vectors, input_gate.T, forget_gate.T, scalars)
    gates_oth = swap_cores(gates)
    k_oth = swap_cores(k_send)
    v_oth = swap_cores(v_send)
    q_oth = swap_cores(q_send)

    def by_head(width):
        return pl.BlockSpec(
            (1, tokens, width), lambda i, s: (jnp.bitwise_xor(s[0], i), 0, 0)
        )

    small = [
        whole((2 * heads, tokens)),
        whole((2 * heads, tokens)),
        whole((1, 2 * tokens)),
    ]
    state = (rows, value_width)
    states = pl.pallas_call(
        functools.partial(state_kernel, heads),
        grid_spec=pltpu.PrefetchScalarGridSpec(
            num_scalar_prefetch=1,
            grid=(group,),
            in_specs=[by_head(key_width), by_head(value_width)] * 2 + small,
            out_specs=[whole(state)] * group,
            scratch_shapes=[
                pltpu.VMEM((heads, 2 * tokens), F32),
                pltpu.VMEM((heads, LANES), F32),
                pltpu.VMEM((heads, LANES), F32),
                pltpu.VMEM(state, BF16),
            ],
        ),
        out_shape=[shape_of(*state)] * group,
        compiler_params=params(),
        name="states",
    )(scalars, k_keep, v_keep, k_oth, v_oth, gates, gates_oth, ids)
    gathered = [states[0]] + [in_group(states[r], r) for r in range(1, group)]

    total = pl.pallas_call(
        functools.partial(total_kernel, group),
        in_specs=[SMEM] + [whole(state)] * group,
        out_specs=whole(state),
        out_shape=shape_of(*state),
        compiler_params=params(),
        name="group_total",
    )(scalars, *gathered)
    totals = [to_later(total, d) for d in range(1, reach + 1)]

    outgoing = pl.pallas_call(
        functools.partial(entering_kernel, group, reach),
        in_specs=[SMEM] + [whole(state)] * (group + reach),
        out_specs=[whole(state)] * group,
        out_shape=[shape_of(*state)] * group,
        compiler_params=params(),
        name="entering",
    )(scalars, *gathered, *totals)
    entering = [outgoing[0]] + [in_group(outgoing[r], r) for r in range(1, group)]

    length = 2 * tokens
    keep, send = pl.pallas_call(
        functools.partial(output_kernel, heads, group),
        grid_spec=pltpu.PrefetchScalarGridSpec(
            num_scalar_prefetch=1,
            grid=(group,),
            in_specs=[by_head(key_width), by_head(key_width), by_head(value_width)] * 2
            + small
            + [whole(state)] * group,
            out_specs=[by_head(value_width)] * 2,
            scratch_shapes=[
                pltpu.VMEM((heads, length), F32),
                pltpu.VMEM((length, LANES), F32),
                pltpu.VMEM((length, length), F32),
                pltpu.VMEM(state, BF16),
            ],
        ),
        out_shape=[shape_of(*wide)] * 2,
        compiler_params=params(),
        name="outputs",
    )(scalars, q_keep, k_keep, v_keep, q_oth, k_oth, v_oth, gates, gates_oth, ids, *entering)
    received = swap_cores(send)
    return pl.pallas_call(
        merge_kernel,
        in_specs=[SMEM, whole(wide), whole(wide)],
        out_specs=whole(value_vectors.shape),
        out_shape=shape_of(*value_vectors.shape),
        compiler_params=params(),
        name="merge",
    )(scalars, keep, received)


def solution(mesh):
    return jax.shard_map(
        functools.partial(local, mesh.size),
        mesh=mesh,
        in_specs=(
            P(AXES, None, None),
            P(AXES, None, None),
            P(AXES, None, None),
            P(AXES, None),
            P(AXES, None),
            P("ctx"),
        ),
        out_specs=P(AXES, None, None),
        check_vma=False,
    )
```

```python
import functools

import jax
import jax.numpy as jnp
from jax import lax
from jax.experimental import pallas as pl
from jax.experimental.pallas import tpu as pltpu
from jax.sharding import PartitionSpec as P

AXES = ("ctx", "hv")
FLOOR_NEG = -1e30
META = 16
LANES = 128
LAY = 256
F32, BF16 = jnp.float32, jnp.bfloat16

NN = (((1,), (0,)), ((), ()))
NT = (((1,), (1,)), ((), ()))


def dot(a, b, dims=NN):
    return lax.dot_general(a, b, dims, preferred_element_type=F32)


def split3(x):
    hi = x.astype(BF16).astype(F32)
    mid = (x - hi).astype(BF16).astype(F32)
    return hi, mid, (x - hi - mid).astype(BF16).astype(F32)


def iota(shape, dim):
    return lax.broadcasted_iota(jnp.int32, shape, dim)


def meta_rows(normalizer, top, decay, doc):
    line = jnp.concatenate([normalizer, top, decay], axis=1)
    hi, mid, low = split3(line)
    width = line.shape[1]
    doc_line = jnp.concatenate([doc] * (width // LANES), axis=1)
    row = iota((META, width), 0)
    rows = jnp.where(row == 0, hi, jnp.where(row == 1, mid, jnp.where(row == 2, low, 0.0)))
    return jnp.where(row == 3, doc_line, rows).astype(BF16)


def read_meta(ref):
    key_width = ref.shape[0] - META
    rows = ref[key_width:, :].astype(F32)
    line = (rows[2:3] + rows[1:2]) + rows[0:1]
    return (
        line[:, :key_width],
        line[:, key_width : key_width + LANES],
        line[:, key_width + LANES : key_width + 2 * LANES],
        rows[3:4, :LANES],
    )


def weighted(refs, coefs):
    key_width, value_width = refs[0].shape[0] - META, refs[0].shape[1]
    total = None
    for ref, coef in zip(refs, coefs, strict=True):
        wide = jnp.concatenate([coef] * (value_width // LANES), axis=1)
        term = wide * ref[:key_width, :].astype(F32)
        total = term if total is None else total + term
    return total


def gate_rows(core, own_ref, other_ref, heads):
    own, other = own_ref[...].astype(F32), other_ref[...].astype(F32)
    both = jnp.concatenate(
        [jnp.where(core == 0, own, other), jnp.where(core == 0, other, own)], axis=1
    )
    gate_in, forget = both[:heads], both[heads:]
    log_forget = jnp.minimum(forget, 0.0) - jnp.log1p(jnp.exp(-jnp.abs(forget)))
    length = both.shape[1]
    upto = (iota((length, length), 0) <= iota((length, length), 1)).astype(BF16)
    pieces = dot(jnp.concatenate(split3(log_forget), axis=0).astype(BF16), upto)
    decay = (pieces[2 * heads :] + pieces[heads : 2 * heads]) + pieces[:heads]
    return gate_in, decay


def by_head_order(heads):
    n = LAY // heads
    out, inside = iota((LAY, LAY), 0), iota((LAY, LAY), 1)
    return ((inside % heads == out // n) & (inside // heads == out % n)).astype(BF16)


def relayout_kernel(half, count, scalars, *refs):
    sources, outs = refs[:count], refs[count:]
    heads = 2 * half
    n = LAY // heads
    core = scalars[1]
    order = by_head_order(heads)
    for index, source in enumerate(sources):
        keep, send = outs[index], outs[count + index]
        tokens, _, width = source.shape
        for g in range(tokens // n):
            span = slice(g * n, (g + 1) * n)
            rows = dot(order, source[span].reshape(LAY, width)).astype(BF16)
            rows = rows.reshape(heads, n, width)
            keep[:, span, :] = jnp.where(core == 0, rows[:half], rows[half:])
            send[:, span, :] = jnp.where(core == 0, rows[half:], rows[:half])


def gates_kernel(heads, scalars, g_own, g_oth, ids_ref, *outs):
    factors, tops, decays, source_rows, columns = outs
    core = scalars[1]
    length = ids_ref.shape[1]
    gate_in, decay = gate_rows(core, g_own, g_oth, heads)
    ids = ids_ref[...]
    exponent = decay[:, length - 1 :] - decay + gate_in
    exponent = jnp.where(ids == ids[:, length - 1 :], exponent, FLOOR_NEG)
    top = jnp.max(exponent, axis=1, keepdims=True)
    factors[...] = jnp.exp(exponent - top)
    tops[...] = jnp.broadcast_to(top, tops.shape)
    decays[...] = jnp.broadcast_to(decay[:, length - 1 :], decays.shape)
    source_rows[...] = gate_in - decay
    docs = ids.astype(F32) + 1.0
    filler = jnp.zeros((LANES - heads - 1, length), F32)
    columns[...] = jnp.concatenate([decay, docs, filler], axis=0).T


def state_kernel(slot, heads, scalars, k_own, v_own, k_oth, v_oth, factors, tops, decays, ids_ref, out):
    core = scalars[1]
    tokens, key_width = k_own.shape[1:]
    length = 2 * tokens
    head = (heads // 2) * core + jnp.bitwise_xor(scalars[0], slot)
    row = factors[pl.ds(head, 1), :]
    first, last = row[:, :tokens], row[:, tokens:]
    total, normal = None, None
    for k_ref, v_ref, f in (
        (k_own, v_own, jnp.where(core == 0, first, last)),
        (k_oth, v_oth, jnp.where(core == 0, last, first)),
    ):
        keys, values = k_ref[0], v_ref[0]
        scaled = keys.astype(F32).T * f
        high = scaled.astype(BF16)
        low = (scaled - high.astype(F32)).astype(BF16)
        part = dot(low, values) + dot(high, values)
        pieces = jnp.concatenate(split3(f) + (jnp.zeros((META - 3, tokens), F32),), axis=0)
        sums = dot(pieces.astype(BF16), keys)
        line = (sums[2:3] + sums[1:2]) + sums[0:1]
        total = part if total is None else total + part
        normal = line if normal is None else normal + line
    doc = jnp.broadcast_to(ids_ref[:, length - 1 :].astype(F32) + 1.0, (1, LANES))
    out[:key_width, :] = total.astype(BF16)
    out[key_width:, :] = meta_rows(
        normal, tops[pl.ds(head, 1), :], decays[pl.ds(head, 1), :], doc
    )


def total_kernel(group, scalars, *refs):
    states, out = refs[:group], refs[group]
    place = [jnp.bitwise_xor(scalars[0], r) for r in range(group)]
    metas = [read_meta(ref) for ref in states]
    zero = jnp.zeros((1, LANES), F32)
    doc = sum((jnp.where(place[r] == group - 1, metas[r][3], zero) for r in range(group)), zero)
    reached = []
    for r in range(group):
        after = sum(
            (jnp.where(place[i] > place[r], metas[i][2], zero) for i in range(group)), zero
        )
        reached.append(jnp.where(metas[r][3] == doc, metas[r][1] + after, FLOOR_NEG))
    top = functools.reduce(jnp.maximum, reached)
    coefs = [
        jnp.where(metas[r][3] == doc, jnp.exp(reached[r] - top), 0.0) for r in range(group)
    ]
    key_width = out.shape[0] - META
    out[:key_width, :] = weighted(states, coefs).astype(BF16)
    normal = sum(
        jnp.concatenate([coefs[r]] * (key_width // LANES), axis=1) * metas[r][0]
        for r in range(group)
    )
    decay = sum((metas[r][2] for r in range(group)), zero)
    out[key_width:, :] = meta_rows(normal, top, decay, doc)


def entering_kernel(group, reach, scalars, *refs):
    states, totals, outs = refs[:group], refs[group : group + reach], refs[group + reach :]
    place = [jnp.bitwise_xor(scalars[0], r) for r in range(group)]
    metas = [read_meta(ref) for ref in states]
    far = [read_meta(ref) for ref in totals]
    zero = jnp.zeros((1, LANES), F32)
    key_width = outs[0].shape[0] - META
    for r in range(group):
        mine = place[r]
        doc = jnp.where(mine == 0, far[0][3], zero)
        for i in range(group):
            doc = doc + jnp.where(place[i] == mine - 1, metas[i][3], zero)
        passed = sum(
            (jnp.where(place[i] < mine, metas[i][2], zero) for i in range(group)), zero
        )
        sources, reached, normals = [], [], []
        for i in range(group):
            if i == r:
                continue
            between = sum(
                (
                    jnp.where((place[n] < mine) & (place[n] > place[i]), metas[n][2], zero)
                    for n in range(group)
                ),
                zero,
            )
            there = jnp.where(place[i] < mine, metas[i][3], -1.0)
            alive = there == doc
            sources.append(states[i])
            normals.append(metas[i][0])
            reached.append((alive, jnp.where(alive, metas[i][1] + between, FLOOR_NEG)))
        for d in range(reach):
            alive = (far[d][3] == doc) & (far[d][3] > 0.5)
            sources.append(totals[d])
            normals.append(far[d][0])
            reached.append((alive, jnp.where(alive, far[d][1] + passed, FLOOR_NEG)))
            passed = passed + far[d][2]
        top = functools.reduce(jnp.maximum, [value for _, value in reached])
        coefs = [jnp.where(alive, jnp.exp(value - top), 0.0) for alive, value in reached]
        outs[r][:key_width, :] = weighted(sources, coefs).astype(BF16)
        normal = sum(
            jnp.concatenate([coef] * (key_width // LANES), axis=1) * line
            for coef, line in zip(coefs, normals, strict=True)
        )
        outs[r][key_width:, :] = meta_rows(normal, top, zero, doc)


def output_kernel(slot, heads, scalars, *refs):
    q_own, k_own, v_own, q_oth, k_oth, v_oth, source_rows, columns, ids_ref, payload = refs[:10]
    keep, send = refs[10:]
    core = scalars[1]
    tokens, key_width = q_own.shape[1:]
    length = 2 * tokens
    scaling = key_width**-0.5
    head = (heads // 2) * core + jnp.bitwise_xor(scalars[0], slot)
    is_first = core == 0
    source = source_rows[pl.ds(head, 1), :]
    lane = iota((length, LANES), 1)
    turned = columns[...]
    decay = jnp.sum(jnp.where(lane == head, turned, 0.0), axis=1, keepdims=True)
    docs = turned[:, heads : heads + 1]
    source_docs = ids_ref[...].astype(F32) + 1.0
    causal = iota((tokens, tokens), 0) >= iota((tokens, tokens), 1)
    normal, top, _, doc = read_meta(payload)
    carried = jnp.where(docs == doc[:, :1], decay + top[:, :1], FLOOR_NEG)
    pieces = jnp.concatenate(split3(normal) + (jnp.zeros((META - 3, key_width), F32),), axis=0)
    pieces = pieces.astype(BF16)
    memory = payload[:key_width, :]

    def ordered(own, other):
        own, other = own[0], other[0]
        return jnp.where(is_first, own, other), jnp.where(is_first, other, own)

    queries, keys, values = ordered(q_own, q_oth), ordered(k_own, k_oth), ordered(v_own, v_oth)
    results = []
    for block in range(2):
        rows = slice(block * tokens, (block + 1) * tokens)
        query = queries[block]
        stabilizer = carried[rows]
        exponents = []
        for s in range(block + 1):
            cols = slice(s * tokens, (s + 1) * tokens)
            allowed = docs[rows] == source_docs[:, cols]
            if s == block:
                allowed = allowed & causal
            exponent = jnp.where(allowed, decay[rows] + source[:, cols], FLOOR_NEG)
            exponents.append(exponent)
            stabilizer = jnp.maximum(stabilizer, jnp.max(exponent, axis=1, keepdims=True))
        retained = jnp.exp(carried[rows] - stabilizer) * scaling
        seen = dot(query, pieces, NT)
        denominator = retained * ((seen[:, 2:3] + seen[:, 1:2]) + seen[:, 0:1])
        numerator = retained * dot(query, memory)
        for s in range(block + 1):
            weights = dot(query, keys[s], NT) * scaling * jnp.exp(exponents[s] - stabilizer)
            denominator = denominator + jnp.sum(weights, axis=1, keepdims=True)
            high = weights.astype(BF16)
            numerator = numerator + dot(high, values[s])
            if s < block:
                low = (weights - high.astype(F32)).astype(BF16)
                numerator = numerator + dot(low, values[s])
        results.append((numerator / jnp.maximum(jnp.abs(denominator), 1.0)).astype(BF16))
    keep[...] = jnp.where(is_first, results[0], results[1])
    send[...] = jnp.where(is_first, results[1], results[0])


def merge_kernel(heads, scalars, *refs):
    pieces, out = refs[:heads], refs[heads]
    half = heads // 2
    n = LAY // heads
    mine, core = scalars[0], scalars[1]
    into, given = iota((LAY, LAY), 0), iota((LAY, LAY), 1)
    index = given // n
    slot = jnp.bitwise_and(index, half - 1)
    side = jnp.where(index < half, core, 1 - core)
    head = side * half + jnp.bitwise_xor(slot, mine)
    order = ((into % heads == head) & (into // heads == given % n)).astype(BF16)
    tokens, width = pieces[0].shape
    for g in range(tokens // n):
        span = slice(g * n, (g + 1) * n)
        rows = jnp.concatenate([piece[span, :] for piece in pieces], axis=0)
        out[span] = dot(order, rows).reshape(n, heads, width).astype(BF16)


def whole(shape):
    return pl.BlockSpec(shape, lambda *_: (0,) * len(shape))


def params():
    return pltpu.CompilerParams(vmem_limit_bytes=56 * 2**20)


SMEM = pl.BlockSpec(memory_space=pltpu.SMEM)


def shape_of(*dims, dtype=BF16):
    return jax.ShapeDtypeStruct(dims, dtype)


def local(devices, queries, key_vectors, value_vectors, input_gate, forget_gate, doc_ids):
    tokens, heads, key_width = queries.shape
    value_width = value_vectors.shape[2]
    half = heads // 2
    group = half
    chips = devices // 2
    levels = chips // group
    reach = max(1, levels // 2)
    ctx, hv = lax.axis_index("ctx"), lax.axis_index("hv")
    chip = ctx * (lax.axis_size("hv") // 2) + hv // 2
    scalars = jnp.stack([chip % group, hv % 2]).astype(jnp.int32)
    ids = lax.dynamic_slice(doc_ids, ((hv // 2) * 2 * tokens,), (2 * tokens,))[None, :]

    def swap_cores(x):
        return lax.ppermute(x, AXES, [(d, d ^ 1) for d in range(devices)])

    def in_group(x, r):
        pairs = [(d, d ^ (2 * r)) for d in range(devices)]
        return lax.ppermute(x, AXES, pairs)

    def to_later(x, levels_on):
        jump = 2 * group * levels_on
        return lax.ppermute(x, AXES, [(d, d + jump) for d in range(devices - jump)])

    rows = key_width + META
    state = (rows, value_width)
    sizes = {key_width: (half, tokens, key_width), value_width: (half, tokens, value_width)}

    def relayout(*sources):
        outs = [sizes[x.shape[2]] for x in sources] * 2
        return pl.pallas_call(
            functools.partial(relayout_kernel, half, len(sources)),
            in_specs=[SMEM] + [whole(x.shape) for x in sources],
            out_specs=[whole(s) for s in outs],
            out_shape=[shape_of(*s) for s in outs],
            compiler_params=params(),
            name="relayout",
        )(scalars, *sources)

    gates = jnp.concatenate([input_gate.T, forget_gate.T], axis=0)
    gates_oth = swap_cores(gates)
    k_keep, v_keep, k_send, v_send = relayout(key_vectors, value_vectors)
    v_oth = swap_cores(v_send)
    k_oth = swap_cores(k_send)
    gate_shapes = [
        (heads, 2 * tokens),
        (heads, LANES),
        (heads, LANES),
        (heads, 2 * tokens),
        (2 * tokens, LANES),
    ]
    factors, tops, decays, source_rows, columns = pl.pallas_call(
        functools.partial(gates_kernel, heads),
        in_specs=[SMEM] + [whole(gates.shape)] * 2 + [whole(ids.shape)],
        out_specs=[whole(s) for s in gate_shapes],
        out_shape=[shape_of(*s, dtype=F32) for s in gate_shapes],
        compiler_params=params(),
        name="gates",
    )(scalars, gates, gates_oth, ids)

    def of_head(slot, x):
        return pl.BlockSpec(
            (1,) + x.shape[1:], lambda i, s: (jnp.bitwise_xor(s[0], slot), 0, 0)
        )

    def per_head(kernel, slot, by_head, others, out_shapes, name):
        return pl.pallas_call(
            functools.partial(kernel, slot, heads),
            grid_spec=pltpu.PrefetchScalarGridSpec(
                num_scalar_prefetch=1,
                grid=(1,),
                in_specs=[of_head(slot, x) for x in by_head] + [whole(x.shape) for x in others],
                out_specs=[whole(s) for s in out_shapes],
            ),
            out_shape=[shape_of(*s) for s in out_shapes],
            compiler_params=params(),
            name=name,
        )(scalars, *by_head, *others)

    farthest_first = list(range(group - 1, -1, -1))
    gathered = [None] * group
    for r in farthest_first:
        [made] = per_head(
            state_kernel,
            r,
            (k_keep, v_keep, k_oth, v_oth),
            (factors, tops, decays, ids),
            [state],
            "state",
        )
        gathered[r] = in_group(made, r) if r else made
    queries, gathered[0] = lax.optimization_barrier((queries, gathered[0]))
    q_keep, q_send = relayout(queries)
    q_oth = swap_cores(q_send)

    total = pl.pallas_call(
        functools.partial(total_kernel, group),
        in_specs=[SMEM] + [whole(state)] * group,
        out_specs=whole(state),
        out_shape=shape_of(*state),
        compiler_params=params(),
        name="group_total",
    )(scalars, *gathered)
    totals = [to_later(total, d) for d in range(reach, 0, -1)][::-1]

    outgoing = pl.pallas_call(
        functools.partial(entering_kernel, group, reach),
        in_specs=[SMEM] + [whole(state)] * (group + reach),
        out_specs=[whole(state)] * group,
        out_shape=[shape_of(*state)] * group,
        compiler_params=params(),
        name="entering",
    )(scalars, *gathered, *totals)
    entering = [in_group(outgoing[r], r) if r else outgoing[r] for r in farthest_first][::-1]

    kept, received = [], []
    for r in range(group):
        keep, send = per_head(
            output_kernel,
            r,
            (q_keep, k_keep, v_keep, q_oth, k_oth, v_oth),
            (source_rows, columns, ids, entering[r]),
            [(tokens, value_width)] * 2,
            "output",
        )
        kept.append(keep)
        received.append(swap_cores(send))
    return pl.pallas_call(
        functools.partial(merge_kernel, heads),
        in_specs=[SMEM] + [whole((tokens, value_width))] * heads,
        out_specs=whole(value_vectors.shape),
        out_shape=shape_of(*value_vectors.shape),
        compiler_params=params(),
        name="merge",
    )(scalars, *kept, *received)


def solution(mesh):
    return jax.shard_map(
        functools.partial(local, mesh.size),
        mesh=mesh,
        in_specs=(
            P(AXES, None, None),
            P(AXES, None, None),
            P(AXES, None, None),
            P(AXES, None),
            P(AXES, None),
            P("ctx"),
        ),
        out_specs=P(AXES, None, None),
        check_vma=False,
    )
```

```python
import functools

import jax
import jax.numpy as jnp
from jax import lax
from jax.experimental import pallas as pl
from jax.experimental.pallas import tpu as pltpu
from jax.sharding import PartitionSpec as P

AXES = ("ctx", "hv")
FLOOR_NEG = -1e30
META = 16
LANES = 128
LAY = 256
F32, BF16 = jnp.float32, jnp.bfloat16

NN = (((1,), (0,)), ((), ()))
NT = (((1,), (1,)), ((), ()))


def dot(a, b, dims=NN):
    return lax.dot_general(a, b, dims, preferred_element_type=F32)


def split3(x):
    hi = x.astype(BF16).astype(F32)
    mid = (x - hi).astype(BF16).astype(F32)
    return hi, mid, (x - hi - mid).astype(BF16).astype(F32)


def iota(shape, dim):
    return lax.broadcasted_iota(jnp.int32, shape, dim)


def meta_rows(normalizer, top, decay, doc):
    width = normalizer.shape[1]
    row = iota((META, width), 0)
    rows = jnp.where(row == 6, jnp.concatenate([doc] * (width // LANES), axis=1), 0.0)
    lines = split3(normalizer) + split3(jnp.concatenate([top, decay], axis=1))
    for index, line in enumerate(lines):
        rows = jnp.where(row == index, line, rows)
    return rows.astype(BF16)


def read_meta(refs):
    key_width = refs[0].shape[0] - META
    rows = [ref[key_width:, :].astype(F32) for ref in refs]
    normals = jnp.concatenate([(x[2:3] + x[1:2]) + x[0:1] for x in rows], axis=0)
    line = jnp.concatenate([(x[5:6] + x[4:5]) + x[3:4] for x in rows], axis=0)
    docs = jnp.concatenate([x[6:7, :LANES] for x in rows], axis=0)
    return normals, line[:, :LANES], line[:, LANES:], docs


def wide(x, width):
    return jnp.concatenate([x] * (width // LANES), axis=1)


def weighted(refs, coefs):
    key_width, width = refs[0].shape[0] - META, refs[0].shape[1]
    total = None
    for ref, coef in zip(refs, coefs, strict=True):
        term = wide(coef, width) * ref[:key_width, :].astype(F32)
        total = term if total is None else total + term
    return total


def gate_rows(core, own_ref, other_ref, heads):
    own, other = own_ref[...].astype(F32), other_ref[...].astype(F32)
    both = jnp.concatenate(
        [jnp.where(core == 0, own, other), jnp.where(core == 0, other, own)], axis=1
    )
    gate_in, forget = both[:heads], both[heads:]
    log_forget = jnp.minimum(forget, 0.0) - jnp.log1p(jnp.exp(-jnp.abs(forget)))
    length = both.shape[1]
    upto = (iota((length, length), 0) <= iota((length, length), 1)).astype(BF16)
    pieces = dot(jnp.concatenate(split3(log_forget), axis=0).astype(BF16), upto)
    decay = (pieces[2 * heads :] + pieces[heads : 2 * heads]) + pieces[:heads]
    return gate_in, decay


def by_head_order(heads):
    n = LAY // heads
    out, inside = iota((LAY, LAY), 0), iota((LAY, LAY), 1)
    return ((inside % heads == out // n) & (inside // heads == out % n)).astype(BF16)


def relayout_kernel(half, count, scalars, *refs):
    sources, outs = refs[:count], refs[count:]
    heads = 2 * half
    n = LAY // heads
    core = scalars[1]
    order = by_head_order(heads)
    for index, source in enumerate(sources):
        keep, send = outs[index], outs[count + index]
        tokens, _, width = source.shape
        for g in range(tokens // n):
            span = slice(g * n, (g + 1) * n)
            rows = dot(order, source[span].reshape(LAY, width)).astype(BF16)
            rows = rows.reshape(heads, n, width)
            keep[:, span, :] = jnp.where(core == 0, rows[:half], rows[half:])
            send[:, span, :] = jnp.where(core == 0, rows[half:], rows[:half])


def gates_kernel(heads, scalars, g_own, g_oth, ids_ref, *outs):
    factors, tops, decays, source_rows, columns = outs
    core = scalars[1]
    length = ids_ref.shape[1]
    gate_in, decay = gate_rows(core, g_own, g_oth, heads)
    ids = ids_ref[...]
    exponent = decay[:, length - 1 :] - decay + gate_in
    exponent = jnp.where(ids == ids[:, length - 1 :], exponent, FLOOR_NEG)
    top = jnp.max(exponent, axis=1, keepdims=True)
    factors[...] = jnp.exp(exponent - top)
    tops[...] = jnp.broadcast_to(top, tops.shape)
    decays[...] = jnp.broadcast_to(decay[:, length - 1 :], decays.shape)
    source_rows[...] = gate_in - decay
    docs = ids.astype(F32) + 1.0
    filler = jnp.zeros((LANES - heads - 1, length), F32)
    columns[...] = jnp.concatenate([decay, docs, filler], axis=0).T


def state_kernel(first_slot, heads, scalars, *refs):
    k_own, v_own, k_oth, v_oth, factors, tops, decays, ids_ref = refs[:8]
    outs, halves = refs[8:-1], refs[-1]
    step = pl.program_id(0)
    mine, core = scalars[0], scalars[1]
    tokens, key_width = k_own.shape[1:]
    part = v_own.shape[2] // 2
    length = 2 * tokens
    head = (heads // 2) * core + jnp.bitwise_xor(mine // 2, first_slot - step)
    row = factors[pl.ds(head, 1), :]
    first, last = row[:, :tokens], row[:, tokens:]
    total, normal = None, None
    for k_ref, v_ref, f in (
        (k_own, v_own, jnp.where(core == 0, first, last)),
        (k_oth, v_oth, jnp.where(core == 0, last, first)),
    ):
        keys, values = k_ref[0], v_ref[0]
        scaled = keys.astype(F32).T * f
        high = scaled.astype(BF16)
        low = (scaled - high.astype(F32)).astype(BF16)
        piece = dot(low, values) + dot(high, values)
        pieces = jnp.concatenate(split3(f) + (jnp.zeros((META - 3, tokens), F32),), axis=0)
        sums = dot(pieces.astype(BF16), keys)
        line = (sums[2:3] + sums[1:2]) + sums[0:1]
        total = piece if total is None else total + piece
        normal = line if normal is None else normal + line
    doc = jnp.broadcast_to(ids_ref[:, length - 1 :].astype(F32) + 1.0, (1, LANES))
    rows = meta_rows(normal, tops[pl.ds(head, 1), :], decays[pl.ds(head, 1), :], doc)
    for half in range(2):
        halves[half, :key_width, :] = total[:, half * part : (half + 1) * part].astype(BF16)
        halves[half, key_width:, :] = rows
    for i, out in enumerate(outs):

        @pl.when(step == i // 2)
        def _(out=out, i=i):
            out[...] = halves[jnp.bitwise_xor(mine % 2, i % 2)]


def decay_before(mine, place, decays):
    group = decays.shape[0]
    before = jnp.zeros_like(decays)
    for i in range(group):
        before = before + jnp.where(place > jnp.bitwise_xor(mine, i), decays[i : i + 1], 0.0)
    return before


def total_kernel(group, scalars, *refs):
    states, out = refs[:group], refs[group]
    mine = scalars[0]
    key_width, width = out.shape[0] - META, out.shape[1]
    normals, tops, decays, docs = read_meta(states)
    place = jnp.bitwise_xor(iota((group, LANES), 0), mine)
    whole_decay = jnp.sum(decays, axis=0, keepdims=True)
    after = whole_decay - decay_before(mine, place, decays) - decays
    doc = jnp.sum(jnp.where(place == group - 1, docs, 0.0), axis=0, keepdims=True)
    alive = docs == doc
    reached = jnp.where(alive, tops + after, FLOOR_NEG)
    top = jnp.max(reached, axis=0, keepdims=True)
    coefs = jnp.where(alive, jnp.exp(reached - top), 0.0)
    out[:key_width, :] = weighted(
        states, [coefs[i : i + 1] for i in range(group)]
    ).astype(BF16)
    normal = jnp.sum(wide(coefs, width) * normals, axis=0, keepdims=True)
    out[key_width:, :] = meta_rows(normal, top, whole_decay, doc)


def entering_kernel(group, reach, scalars, *refs):
    states, totals, outs = refs[:group], refs[group : group + reach], refs[group + reach :]
    mine = scalars[0]
    key_width, width = outs[0].shape[0] - META, outs[0].shape[1]
    normals, tops, decays, docs = read_meta(states)
    far_normals, far_tops, far_decays, far_docs = read_meta(totals)
    place = jnp.bitwise_xor(iota((group, LANES), 0), mine)
    before = decay_before(mine, place, decays)
    zero = jnp.zeros((1, LANES), F32)
    far_reached, passed = [], zero
    for d in range(reach):
        far_reached.append(far_tops[d : d + 1] + passed)
        passed = passed + far_decays[d : d + 1]
    far_reached = jnp.concatenate(far_reached, axis=0)
    for r in range(group):
        here = jnp.bitwise_xor(mine, r)
        doc = jnp.sum(jnp.where(place == here - 1, docs, 0.0), axis=0, keepdims=True)
        doc = jnp.where(here == 0, far_docs[0:1], doc)
        mark = before[r : r + 1]
        alive = (place < here) & (docs == doc)
        reached = jnp.where(alive, tops + (mark - before - decays), FLOOR_NEG)
        far_alive = (far_docs == doc) & (far_docs > 0.5)
        far = jnp.where(far_alive, far_reached + mark, FLOOR_NEG)
        top = jnp.maximum(
            jnp.max(reached, axis=0, keepdims=True), jnp.max(far, axis=0, keepdims=True)
        )
        coefs = jnp.where(alive, jnp.exp(reached - top), 0.0)
        far_coefs = jnp.where(far_alive, jnp.exp(far - top), 0.0)
        others = [i for i in range(group) if i != r]
        outs[r][:key_width, :] = weighted(
            [states[i] for i in others] + list(totals),
            [coefs[i : i + 1] for i in others]
            + [far_coefs[d : d + 1] for d in range(reach)],
        ).astype(BF16)
        normal = jnp.sum(wide(coefs, width) * normals, axis=0, keepdims=True)
        normal = normal + jnp.sum(wide(far_coefs, width) * far_normals, axis=0, keepdims=True)
        outs[r][key_width:, :] = meta_rows(normal, top, zero, doc)


def output_kernel(first_slot, heads, scalars, *refs):
    q_own, k_own, v_own, q_oth, k_oth, v_oth, source_rows, columns, ids_ref = refs[:9]
    entering, (keep, send, payload) = refs[9:-3], refs[-3:]
    step = pl.program_id(0)
    mine, core = scalars[0], scalars[1]
    tokens, key_width = q_own.shape[1:]
    length = 2 * tokens
    scaling = key_width**-0.5
    for i, ref in enumerate(entering):

        @pl.when(step == i // 2)
        def _(ref=ref, i=i):
            payload[jnp.bitwise_xor(mine % 2, i % 2)] = ref[...]

    head = (heads // 2) * core + jnp.bitwise_xor(mine // 2, first_slot + step)
    is_first = core == 0
    source = source_rows[pl.ds(head, 1), :]
    lane = iota((length, LANES), 1)
    turned = columns[...]
    decay = jnp.sum(jnp.where(lane == head, turned, 0.0), axis=1, keepdims=True)
    docs = turned[:, heads : heads + 1]
    source_docs = ids_ref[...].astype(F32) + 1.0
    causal = iota((tokens, tokens), 0) >= iota((tokens, tokens), 1)
    normal, top, _, doc = read_meta([payload.at[0]])
    carried = jnp.where(docs == doc[:, :1], decay + top[:, :1], FLOOR_NEG)
    pieces = jnp.concatenate(split3(normal) + (jnp.zeros((META - 3, key_width), F32),), axis=0)
    pieces = pieces.astype(BF16)
    memory = jnp.concatenate([payload[0, :key_width, :], payload[1, :key_width, :]], axis=1)

    def ordered(own, other):
        own, other = own[0], other[0]
        return jnp.where(is_first, own, other), jnp.where(is_first, other, own)

    queries, keys, values = ordered(q_own, q_oth), ordered(k_own, k_oth), ordered(v_own, v_oth)
    results = []
    for block in range(2):
        rows = slice(block * tokens, (block + 1) * tokens)
        query = queries[block]
        stabilizer = carried[rows]
        exponents = []
        for s in range(block + 1):
            cols = slice(s * tokens, (s + 1) * tokens)
            allowed = docs[rows] == source_docs[:, cols]
            if s == block:
                allowed = allowed & causal
            exponent = jnp.where(allowed, decay[rows] + source[:, cols], FLOOR_NEG)
            exponents.append(exponent)
            stabilizer = jnp.maximum(stabilizer, jnp.max(exponent, axis=1, keepdims=True))
        retained = jnp.exp(carried[rows] - stabilizer) * scaling
        seen = dot(query, pieces, NT)
        denominator = retained * ((seen[:, 2:3] + seen[:, 1:2]) + seen[:, 0:1])
        numerator = retained * dot(query, memory)
        for s in range(block + 1):
            weights = dot(query, keys[s], NT) * scaling * jnp.exp(exponents[s] - stabilizer)
            denominator = denominator + jnp.sum(weights, axis=1, keepdims=True)
            high = weights.astype(BF16)
            numerator = numerator + dot(high, values[s])
            if s < block:
                low = (weights - high.astype(F32)).astype(BF16)
                numerator = numerator + dot(low, values[s])
        results.append((numerator / jnp.maximum(jnp.abs(denominator), 1.0)).astype(BF16))
    keep[0] = jnp.where(is_first, results[0], results[1])
    send[0] = jnp.where(is_first, results[1], results[0])


def merge_kernel(heads, scalars, *refs):
    stacks, out = refs[:-1], refs[-1]
    half = heads // 2
    n = LAY // heads
    mine, core = scalars[0] // 2, scalars[1]
    into, given = iota((LAY, LAY), 0), iota((LAY, LAY), 1)
    index = given // n
    slot = jnp.bitwise_and(index, half - 1)
    side = jnp.where(index < half, core, 1 - core)
    head = side * half + jnp.bitwise_xor(slot, mine)
    order = ((into % heads == head) & (into // heads == given % n)).astype(BF16)
    _, tokens, width = stacks[0].shape
    for g in range(tokens // n):
        span = slice(g * n, (g + 1) * n)
        rows = jnp.concatenate(
            [stack[i, span, :] for stack in stacks for i in range(stack.shape[0])], axis=0
        )
        out[span] = dot(order, rows).reshape(n, heads, width).astype(BF16)


def whole(shape):
    return pl.BlockSpec(shape, lambda *_: (0,) * len(shape))


def params():
    return pltpu.CompilerParams(vmem_limit_bytes=56 * 2**20)


SMEM = pl.BlockSpec(memory_space=pltpu.SMEM)


def shape_of(*dims, dtype=BF16):
    return jax.ShapeDtypeStruct(dims, dtype)


def local(devices, queries, key_vectors, value_vectors, input_gate, forget_gate, doc_ids):
    tokens, heads, key_width = queries.shape
    value_width = value_vectors.shape[2]
    half = heads // 2
    group = heads
    part = value_width // 2
    chips = devices // 2
    levels = chips // group
    reach = max(1, levels // 2)
    ctx, hv = lax.axis_index("ctx"), lax.axis_index("hv")
    chip = ctx * (lax.axis_size("hv") // 2) + hv // 2
    scalars = jnp.stack([chip % group, hv % 2]).astype(jnp.int32)
    ids = lax.dynamic_slice(doc_ids, ((hv // 2) * 2 * tokens,), (2 * tokens,))[None, :]

    def swap_cores(x):
        return lax.ppermute(x, AXES, [(d, d ^ 1) for d in range(devices)])

    def in_group(x, r):
        pairs = [(d, d ^ (2 * r)) for d in range(devices)]
        return lax.ppermute(x, AXES, pairs)

    def to_later(x, levels_on):
        jump = 2 * group * levels_on
        return lax.ppermute(x, AXES, [(d, d + jump) for d in range(devices - jump)])

    rows = key_width + META
    state = (rows, part)
    sizes = {key_width: (half, tokens, key_width), value_width: (half, tokens, value_width)}

    def relayout(*sources):
        outs = [sizes[x.shape[2]] for x in sources] * 2
        return pl.pallas_call(
            functools.partial(relayout_kernel, half, len(sources)),
            in_specs=[SMEM] + [whole(x.shape) for x in sources],
            out_specs=[whole(s) for s in outs],
            out_shape=[shape_of(*s) for s in outs],
            compiler_params=params(),
            name="relayout",
        )(scalars, *sources)

    gates = jnp.concatenate([input_gate.T, forget_gate.T], axis=0)
    gates_oth = swap_cores(gates)
    k_keep, v_keep, k_send, v_send = relayout(key_vectors, value_vectors)
    v_oth = swap_cores(v_send)
    k_oth = swap_cores(k_send)
    gate_shapes = [
        (heads, 2 * tokens),
        (heads, LANES),
        (heads, LANES),
        (heads, 2 * tokens),
        (2 * tokens, LANES),
    ]
    factors, tops, decays, source_rows, columns = pl.pallas_call(
        functools.partial(gates_kernel, heads),
        in_specs=[SMEM] + [whole(gates.shape)] * 2 + [whole(ids.shape)],
        out_specs=[whole(s) for s in gate_shapes],
        out_shape=[shape_of(*s, dtype=F32) for s in gate_shapes],
        compiler_params=params(),
        name="gates",
    )(scalars, gates, gates_oth, ids)

    def per_head(kernel, first_slot, steps, down, by_head, others, outs, scratch, name):
        def block(x):
            def index(i, s):
                slot = first_slot - i if down else first_slot + i
                return (jnp.bitwise_xor(s[0] // 2, slot), 0, 0)

            return pl.BlockSpec((1,) + x.shape[1:], index)

        return pl.pallas_call(
            functools.partial(kernel, first_slot, heads),
            grid_spec=pltpu.PrefetchScalarGridSpec(
                num_scalar_prefetch=1,
                grid=(steps,),
                in_specs=[block(x) for x in by_head] + [whole(x.shape) for x in others],
                out_specs=[spec for spec, _ in outs],
                scratch_shapes=scratch,
            ),
            out_shape=[shape for _, shape in outs],
            compiler_params=params(),
            name=name,
        )(scalars, *by_head, *others)

    made = [None] * group
    at_once = half // 2
    for first_slot in range(half - 1, -1, -at_once):
        lowest = 2 * (first_slot - at_once + 1)
        pairs = [2 * (first_slot - i) + b for i in range(at_once) for b in range(2)]
        outs = per_head(
            state_kernel,
            first_slot,
            at_once,
            True,
            (k_keep, v_keep, k_oth, v_oth),
            (factors, tops, decays, ids),
            [(whole(state), shape_of(*state))] * len(pairs),
            [pltpu.VMEM((2,) + state, BF16)],
            "states",
        )
        for r, out in zip(pairs, outs, strict=True):
            made[r] = out
        if lowest == 0:
            queries, made[0] = lax.optimization_barrier((queries, made[0]))
    gathered = [in_group(made[r], r) if r else made[0] for r in range(group - 1, -1, -1)][::-1]
    q_keep, q_send = relayout(queries)
    q_oth = swap_cores(q_send)

    total = pl.pallas_call(
        functools.partial(total_kernel, group),
        in_specs=[SMEM] + [whole(state)] * group,
        out_specs=whole(state),
        out_shape=shape_of(*state),
        compiler_params=params(),
        name="group_total",
    )(scalars, *gathered)
    totals = [to_later(total, d) for d in range(reach, 0, -1)][::-1]

    outgoing = pl.pallas_call(
        functools.partial(entering_kernel, group, reach),
        in_specs=[SMEM] + [whole(state)] * (group + reach),
        out_specs=[whole(state)] * group,
        out_shape=[shape_of(*state)] * group,
        compiler_params=params(),
        name="entering",
    )(scalars, *gathered, *totals)
    entering = [in_group(outgoing[r], r) if r else outgoing[0] for r in range(group - 1, -1, -1)]
    entering = entering[::-1]

    kept, received = [], []
    for first_slot, count in ((0, 1), (1, half - 1)):
        spec = pl.BlockSpec((1, tokens, value_width), lambda i, s: (i, 0, 0))
        keep, send = per_head(
            output_kernel,
            first_slot,
            count,
            False,
            (q_keep, k_keep, v_keep, q_oth, k_oth, v_oth),
            (source_rows, columns, ids, *entering[2 * first_slot : 2 * (first_slot + count)]),
            [(spec, shape_of(count, tokens, value_width))] * 2,
            [pltpu.VMEM((2,) + state, BF16)],
            "outputs",
        )
        kept.append(keep)
        received.append(swap_cores(send))
    return pl.pallas_call(
        functools.partial(merge_kernel, heads),
        in_specs=[SMEM] + [whole(x.shape) for x in kept + received],
        out_specs=whole(value_vectors.shape),
        out_shape=shape_of(*value_vectors.shape),
        compiler_params=params(),
        name="merge",
    )(scalars, *kept, *received)


def solution(mesh):
    return jax.shard_map(
        functools.partial(local, mesh.size),
        mesh=mesh,
        in_specs=(
            P(AXES, None, None),
            P(AXES, None, None),
            P(AXES, None, None),
            P(AXES, None),
            P(AXES, None),
            P("ctx"),
        ),
        out_specs=P(AXES, None, None),
        check_vma=False,
    )
```

```python
import functools

import jax
import jax.numpy as jnp
from jax import lax
from jax.experimental import pallas as pl
from jax.experimental.pallas import tpu as pltpu
from jax.sharding import PartitionSpec as P

AXES = ("ctx", "hv")
FLOOR_NEG = -1e30
META = 16
LANES = 128
LAY = 256
F32, BF16 = jnp.float32, jnp.bfloat16

NN = (((1,), (0,)), ((), ()))
NT = (((1,), (1,)), ((), ()))


def dot(a, b, dims=NN):
    return lax.dot_general(a, b, dims, preferred_element_type=F32)


def split3(x):
    hi = x.astype(BF16).astype(F32)
    mid = (x - hi).astype(BF16).astype(F32)
    return hi, mid, (x - hi - mid).astype(BF16).astype(F32)


def iota(shape, dim):
    return lax.broadcasted_iota(jnp.int32, shape, dim)


def meta_rows(normalizer, top, decay, doc):
    width = normalizer.shape[1]
    row = iota((META, width), 0)
    rows = jnp.where(row == 6, jnp.concatenate([doc] * (width // LANES), axis=1), 0.0)
    lines = split3(normalizer) + split3(jnp.concatenate([top, decay], axis=1))
    for index, line in enumerate(lines):
        rows = jnp.where(row == index, line, rows)
    return rows.astype(BF16)


def read_meta(refs):
    key_width = refs[0].shape[0] - META
    rows = [ref[key_width:, :].astype(F32) for ref in refs]
    normals = jnp.concatenate([(x[2:3] + x[1:2]) + x[0:1] for x in rows], axis=0)
    line = jnp.concatenate([(x[5:6] + x[4:5]) + x[3:4] for x in rows], axis=0)
    docs = jnp.concatenate([x[6:7, :LANES] for x in rows], axis=0)
    return normals, line[:, :LANES], line[:, LANES:], docs


def wide(x, width):
    return jnp.concatenate([x] * (width // LANES), axis=1)


def weighted(refs, coefs):
    key_width, width = refs[0].shape[0] - META, refs[0].shape[1]
    total = None
    for ref, coef in zip(refs, coefs, strict=True):
        term = wide(coef, width) * ref[:key_width, :].astype(F32)
        total = term if total is None else total + term
    return total


def gate_rows(core, own_ref, other_ref, heads):
    own, other = own_ref[...].astype(F32), other_ref[...].astype(F32)
    both = jnp.concatenate(
        [jnp.where(core == 0, own, other), jnp.where(core == 0, other, own)], axis=1
    )
    gate_in, forget = both[:heads], both[heads:]
    log_forget = jnp.minimum(forget, 0.0) - jnp.log1p(jnp.exp(-jnp.abs(forget)))
    length = both.shape[1]
    upto = (iota((length, length), 0) <= iota((length, length), 1)).astype(BF16)
    pieces = dot(jnp.concatenate(split3(log_forget), axis=0).astype(BF16), upto)
    decay = (pieces[2 * heads :] + pieces[heads : 2 * heads]) + pieces[:heads]
    return gate_in, decay


def by_head_order(heads):
    n = LAY // heads
    out, inside = iota((LAY, LAY), 0), iota((LAY, LAY), 1)
    return ((inside % heads == out // n) & (inside // heads == out % n)).astype(BF16)


def relayout_kernel(half, count, scalars, *refs):
    sources, outs = refs[:count], refs[count:]
    heads = 2 * half
    n = LAY // heads
    core = scalars[1]
    order = by_head_order(heads)
    for index, source in enumerate(sources):
        keep, send = outs[index], outs[count + index]
        tokens, _, width = source.shape
        for g in range(tokens // n):
            span = slice(g * n, (g + 1) * n)
            rows = dot(order, source[span].reshape(LAY, width)).astype(BF16)
            rows = rows.reshape(heads, n, width)
            keep[:, span, :] = jnp.where(core == 0, rows[:half], rows[half:])
            send[:, span, :] = jnp.where(core == 0, rows[half:], rows[:half])


def gates_kernel(heads, scalars, g_own, g_oth, ids_ref, *outs):
    factors, tops, decays, source_rows, columns = outs
    core = scalars[1]
    length = ids_ref.shape[1]
    gate_in, decay = gate_rows(core, g_own, g_oth, heads)
    ids = ids_ref[...]
    exponent = decay[:, length - 1 :] - decay + gate_in
    exponent = jnp.where(ids == ids[:, length - 1 :], exponent, FLOOR_NEG)
    top = jnp.max(exponent, axis=1, keepdims=True)
    factors[...] = jnp.exp(exponent - top)
    tops[...] = jnp.broadcast_to(top, tops.shape)
    decays[...] = jnp.broadcast_to(decay[:, length - 1 :], decays.shape)
    source_rows[...] = gate_in - decay
    docs = ids.astype(F32) + 1.0
    filler = jnp.zeros((LANES - heads - 1, length), F32)
    columns[...] = jnp.concatenate([decay, docs, filler], axis=0).T


def state_kernel(heads, scalars, *refs):
    k_own, v_own, k_oth, v_oth, factors, tops, decays, ids_ref = refs[:8]
    outs, halves = refs[8:-1], refs[-1]
    step = pl.program_id(0)
    mine, core = scalars[0], scalars[1]
    tokens, key_width = k_own.shape[1:]
    part = v_own.shape[2] // 2
    length = 2 * tokens
    head = (heads // 2) * core + jnp.bitwise_xor(mine, step)
    row = factors[pl.ds(head, 1), :]
    first, last = row[:, :tokens], row[:, tokens:]
    total, normal = None, None
    for k_ref, v_ref, f in (
        (k_own, v_own, jnp.where(core == 0, first, last)),
        (k_oth, v_oth, jnp.where(core == 0, last, first)),
    ):
        keys, values = k_ref[0], v_ref[0]
        scaled = keys.astype(F32).T * f
        high = scaled.astype(BF16)
        low = (scaled - high.astype(F32)).astype(BF16)
        piece = dot(low, values) + dot(high, values)
        pieces = jnp.concatenate(split3(f) + (jnp.zeros((META - 3, tokens), F32),), axis=0)
        sums = dot(pieces.astype(BF16), keys)
        line = (sums[2:3] + sums[1:2]) + sums[0:1]
        total = piece if total is None else total + piece
        normal = line if normal is None else normal + line
    doc = jnp.broadcast_to(ids_ref[:, length - 1 :].astype(F32) + 1.0, (1, LANES))
    rows = meta_rows(normal, tops[pl.ds(head, 1), :], decays[pl.ds(head, 1), :], doc)
    for half in range(2):
        halves[half, :key_width, :] = total[:, half * part : (half + 1) * part].astype(BF16)
        halves[half, key_width:, :] = rows
    for i, out in enumerate(outs):

        @pl.when(step == i // 2)
        def _(out=out, i=i):
            out[...] = halves[i % 2]


def decay_before(mine, place, decays):
    group = decays.shape[0]
    before = jnp.zeros_like(decays)
    for i in range(group):
        before = before + jnp.where(place > jnp.bitwise_xor(mine, i), decays[i : i + 1], 0.0)
    return before


def total_kernel(group, scalars, *refs):
    states, out = refs[:group], refs[group]
    mine = scalars[0]
    key_width, width = out.shape[0] - META, out.shape[1]
    normals, tops, decays, docs = read_meta(states)
    place = jnp.bitwise_xor(iota((group, LANES), 0), mine)
    whole_decay = jnp.sum(decays, axis=0, keepdims=True)
    after = whole_decay - decay_before(mine, place, decays) - decays
    doc = jnp.sum(jnp.where(place == group - 1, docs, 0.0), axis=0, keepdims=True)
    alive = docs == doc
    reached = jnp.where(alive, tops + after, FLOOR_NEG)
    top = jnp.max(reached, axis=0, keepdims=True)
    coefs = jnp.where(alive, jnp.exp(reached - top), 0.0)
    out[:key_width, :] = weighted(
        states, [coefs[i : i + 1] for i in range(group)]
    ).astype(BF16)
    normal = jnp.sum(wide(coefs, width) * normals, axis=0, keepdims=True)
    out[key_width:, :] = meta_rows(normal, top, whole_decay, doc)


def entering_kernel(group, reach, scalars, *refs):
    states, totals, outs = refs[:group], refs[group : group + reach], refs[group + reach :]
    mine = scalars[0]
    key_width, width = outs[0].shape[0] - META, outs[0].shape[1]
    normals, tops, decays, docs = read_meta(states)
    far_normals, far_tops, far_decays, far_docs = read_meta(totals)
    place = jnp.bitwise_xor(iota((group, LANES), 0), mine)
    before = decay_before(mine, place, decays)
    zero = jnp.zeros((1, LANES), F32)
    far_reached, passed = [], zero
    for d in range(reach):
        far_reached.append(far_tops[d : d + 1] + passed)
        passed = passed + far_decays[d : d + 1]
    far_reached = jnp.concatenate(far_reached, axis=0)
    for r in range(group):
        here = jnp.bitwise_xor(mine, r)
        doc = jnp.sum(jnp.where(place == here - 1, docs, 0.0), axis=0, keepdims=True)
        doc = jnp.where(here == 0, far_docs[0:1], doc)
        mark = before[r : r + 1]
        alive = (place < here) & (docs == doc)
        reached = jnp.where(alive, tops + (mark - before - decays), FLOOR_NEG)
        far_alive = (far_docs == doc) & (far_docs > 0.5)
        far = jnp.where(far_alive, far_reached + mark, FLOOR_NEG)
        top = jnp.maximum(
            jnp.max(reached, axis=0, keepdims=True), jnp.max(far, axis=0, keepdims=True)
        )
        coefs = jnp.where(alive, jnp.exp(reached - top), 0.0)
        far_coefs = jnp.where(far_alive, jnp.exp(far - top), 0.0)
        others = [i for i in range(group) if i != r]
        outs[r][:key_width, :] = weighted(
            [states[i] for i in others] + list(totals),
            [coefs[i : i + 1] for i in others]
            + [far_coefs[d : d + 1] for d in range(reach)],
        ).astype(BF16)
        normal = jnp.sum(wide(coefs, width) * normals, axis=0, keepdims=True)
        normal = normal + jnp.sum(wide(far_coefs, width) * far_normals, axis=0, keepdims=True)
        outs[r][key_width:, :] = meta_rows(normal, top, zero, doc)


def local_kernel(first_slot, heads, scalars, *refs):
    q_own, k_own, v_own, q_oth, k_oth, v_oth, source_rows, columns, ids_ref = refs[:9]
    numerators, stats = refs[-2:]
    step = pl.program_id(0)
    mine, core = scalars[0], scalars[1]
    tokens, key_width = q_own.shape[1:]
    length = 2 * tokens
    scaling = key_width**-0.5
    head = (heads // 2) * core + jnp.bitwise_xor(mine, first_slot + step)
    is_first = core == 0
    source = source_rows[pl.ds(head, 1), :]
    lane = iota((length, LANES), 1)
    turned = columns[...]
    decay = jnp.sum(jnp.where(lane == head, turned, 0.0), axis=1, keepdims=True)
    docs = turned[:, heads : heads + 1]
    source_docs = ids_ref[...].astype(F32) + 1.0
    causal = iota((tokens, tokens), 0) >= iota((tokens, tokens), 1)

    def ordered(own, other):
        own, other = own[0], other[0]
        return jnp.where(is_first, own, other), jnp.where(is_first, other, own)

    queries, keys, values = ordered(q_own, q_oth), ordered(k_own, k_oth), ordered(v_own, v_oth)
    for block in range(2):
        rows = slice(block * tokens, (block + 1) * tokens)
        exponents = []
        for s in range(block + 1):
            cols = slice(s * tokens, (s + 1) * tokens)
            allowed = docs[rows] == source_docs[:, cols]
            if s == block:
                allowed = allowed & causal
            exponents.append(jnp.where(allowed, decay[rows] + source[:, cols], FLOOR_NEG))
        stabilizer = functools.reduce(
            jnp.maximum, [jnp.max(x, axis=1, keepdims=True) for x in exponents]
        )
        numerator, denominator = None, None
        for s in range(block + 1):
            weights = dot(queries[block], keys[s], NT) * scaling
            weights = weights * jnp.exp(exponents[s] - stabilizer)
            high = weights.astype(BF16)
            part = dot(high, values[s])
            if s < block:
                part = part + dot((weights - high.astype(F32)).astype(BF16), values[s])
            numerator = part if s == 0 else numerator + part
            part = jnp.sum(weights, axis=1, keepdims=True)
            denominator = part if s == 0 else denominator + part
        side = core if block == 0 else 1 - core
        numerators[0, side] = numerator
        lane = iota((tokens, LANES), 1)
        stats[0, side] = jnp.where(
            lane == 0,
            stabilizer,
            jnp.where(lane == 1, denominator, jnp.where(lane == 2, decay[rows], docs[rows])),
        )


def output_kernel(scalars, q_own, q_oth, numerators, stats, *refs):
    entering, (keep, send, payload) = refs[:-3], refs[-3:]
    step = pl.program_id(0)
    key_width = q_own.shape[2]
    scaling = key_width**-0.5
    for i, ref in enumerate(entering):

        @pl.when(step == i)
        def _(ref=ref):
            payload[...] = ref[...]

    normal, top, _, doc = read_meta([payload])
    pieces = jnp.concatenate(split3(normal) + (jnp.zeros((META - 3, key_width), F32),), axis=0)
    pieces = pieces.astype(BF16)
    memory = payload[:key_width, :]
    for side, (q_ref, out) in enumerate(((q_own, keep), (q_oth, send))):
        query = q_ref[0]
        stat = stats[0, side]
        local, docs = stat[:, 0:1], stat[:, 3:4]
        carried = jnp.where(docs == doc[:, :1], stat[:, 2:3] + top[:, :1], FLOOR_NEG)
        stabilizer = jnp.maximum(local, carried)
        shrink = jnp.exp(local - stabilizer)
        retained = jnp.exp(carried - stabilizer) * scaling
        seen = dot(query, pieces, NT)
        seen = (seen[:, 2:3] + seen[:, 1:2]) + seen[:, 0:1]
        denominator = shrink * stat[:, 1:2] + retained * seen
        inverse = 1.0 / jnp.maximum(jnp.abs(denominator), 1.0)
        result = (shrink * inverse) * numerators[0, side]
        result = result + (retained * inverse) * dot(query, memory)
        out[0] = result.astype(BF16)


def merge_kernel(heads, scalars, *refs):
    kept, received, out = refs[:2], refs[2:4], refs[4]
    half = heads // 2
    n = LAY // heads
    mine, core = scalars[0], scalars[1]
    into, given = iota((LAY, LAY), 0), iota((LAY, LAY), 1)
    index = given // n
    slot = jnp.bitwise_and(index, half - 1)
    side = jnp.where(index < half, core, 1 - core)
    head = side * half + jnp.bitwise_xor(slot, mine)
    order = ((into % heads == head) & (into // heads == given % n)).astype(BF16)
    _, tokens, width = kept[0].shape
    for g in range(tokens // n):
        span = slice(g * n, (g + 1) * n)
        for p in range(2):
            rows = jnp.concatenate([kept[p][:, span, :], received[p][:, span, :]], axis=0)
            turned = dot(order, rows.reshape(LAY, width))
            out[span, :, p * width : (p + 1) * width] = turned.reshape(n, heads, width).astype(
                BF16
            )


def whole(shape):
    return pl.BlockSpec(shape, lambda *_: (0,) * len(shape))


def params():
    return pltpu.CompilerParams(vmem_limit_bytes=56 * 2**20)


SMEM = pl.BlockSpec(memory_space=pltpu.SMEM)


def shape_of(*dims, dtype=BF16):
    return jax.ShapeDtypeStruct(dims, dtype)


def local(devices, queries, key_vectors, value_vectors, input_gate, forget_gate, doc_ids):
    tokens, heads, key_width = queries.shape
    value_width = value_vectors.shape[2]
    half = heads // 2
    group = half
    part = value_width // 2
    chips = devices // 2
    levels = chips // group
    reach = max(1, levels // 2)
    ctx, hv = lax.axis_index("ctx"), lax.axis_index("hv")
    chip = ctx * (lax.axis_size("hv") // 2) + hv // 2
    scalars = jnp.stack([chip % group, hv % 2]).astype(jnp.int32)
    ids = lax.dynamic_slice(doc_ids, ((hv // 2) * 2 * tokens,), (2 * tokens,))[None, :]

    def swap_cores(x):
        return lax.ppermute(x, AXES, [(d, d ^ 1) for d in range(devices)])

    def in_group(x, r):
        pairs = [(d, d ^ (2 * r)) for d in range(devices)]
        return lax.ppermute(x, AXES, pairs)

    def to_later(x, levels_on):
        jump = 2 * group * levels_on
        return lax.ppermute(x, AXES, [(d, d + jump) for d in range(devices - jump)])

    rows = key_width + META
    state = (rows, part)
    sizes = {key_width: (half, tokens, key_width), value_width: (half, tokens, value_width)}

    def relayout(*sources):
        outs = [sizes[x.shape[2]] for x in sources] * 2
        return pl.pallas_call(
            functools.partial(relayout_kernel, half, len(sources)),
            in_specs=[SMEM] + [whole(x.shape) for x in sources],
            out_specs=[whole(s) for s in outs],
            out_shape=[shape_of(*s) for s in outs],
            compiler_params=params(),
            name="relayout",
        )(scalars, *sources)

    gates = jnp.concatenate([input_gate.T, forget_gate.T], axis=0)
    gates, key_vectors = lax.optimization_barrier((gates, key_vectors))
    gates_oth = swap_cores(gates)
    k_keep, v_keep, k_send, v_send = relayout(key_vectors, value_vectors)
    gates_oth, k_send, v_send = lax.optimization_barrier((gates_oth, k_send, v_send))
    k_oth = swap_cores(k_send)
    v_oth = swap_cores(v_send)
    queries, _ = lax.optimization_barrier((queries, v_send))
    q_keep, q_send = relayout(queries)
    k_oth, q_send = lax.optimization_barrier((k_oth, q_send))
    q_oth = swap_cores(q_send)
    gate_shapes = [
        (heads, 2 * tokens),
        (heads, LANES),
        (heads, LANES),
        (heads, 2 * tokens),
        (2 * tokens, LANES),
    ]
    factors, tops, decays, source_rows, columns = pl.pallas_call(
        functools.partial(gates_kernel, heads),
        in_specs=[SMEM] + [whole(gates.shape)] * 2 + [whole(ids.shape)],
        out_specs=[whole(s) for s in gate_shapes],
        out_shape=[shape_of(*s, dtype=F32) for s in gate_shapes],
        compiler_params=params(),
        name="gates",
    )(scalars, gates, gates_oth, ids)

    def by_slot(x, first_slot=0):
        return pl.BlockSpec(
            (1,) + x.shape[1:], lambda i, s: (jnp.bitwise_xor(s[0], first_slot + i), 0, 0)
        )

    made = pl.pallas_call(
        functools.partial(state_kernel, heads),
        grid_spec=pltpu.PrefetchScalarGridSpec(
            num_scalar_prefetch=1,
            grid=(group,),
            in_specs=[by_slot(x) for x in (k_keep, v_keep, k_oth, v_oth)]
            + [whole(x.shape) for x in (factors, tops, decays, ids)],
            out_specs=[whole(state)] * (2 * group),
            scratch_shapes=[pltpu.VMEM((2,) + state, BF16)],
        ),
        out_shape=[shape_of(*state)] * (2 * group),
        compiler_params=params(),
        name="states",
    )(scalars, k_keep, v_keep, k_oth, v_oth, factors, tops, decays, ids)
    made = [made[p::2] for p in range(2)]
    gathered = [
        [made[p][0]] + [in_group(made[p][r], r) for r in range(1, group)] for p in range(2)
    ]
    local_shapes = [(half, 2, tokens, value_width), (half, 2, tokens, LANES)]

    def own_terms(first_slot, count, q_own, into):
        by_head = (q_own, k_keep, v_keep, q_oth, k_oth, v_oth)
        small = (source_rows, columns, ids)
        return pl.pallas_call(
            functools.partial(local_kernel, first_slot, heads),
            grid_spec=pltpu.PrefetchScalarGridSpec(
                num_scalar_prefetch=1,
                grid=(count,),
                in_specs=[by_slot(x, first_slot) for x in by_head]
                + [whole(x.shape) for x in small]
                + [pl.BlockSpec(memory_space=pl.ANY)] * len(into),
                out_specs=[
                    pl.BlockSpec((1,) + s[1:], lambda i, _: (first_slot + i, 0, 0, 0))
                    for s in local_shapes
                ],
            ),
            out_shape=[shape_of(*s, dtype=F32) for s in local_shapes],
            input_output_aliases={10 + i: i for i in range(len(into))},
            compiler_params=params(),
            name="own_terms",
        )(scalars, *by_head, *small, *into)

    def group_total(states):
        return pl.pallas_call(
            functools.partial(total_kernel, group),
            in_specs=[SMEM] + [whole(state)] * group,
            out_specs=whole(state),
            out_shape=shape_of(*state),
            compiler_params=params(),
            name="group_total",
        )(scalars, *states)

    def entering_states(states, total):
        totals = [to_later(total, d) for d in range(1, reach + 1)]
        return pl.pallas_call(
            functools.partial(entering_kernel, group, reach),
            in_specs=[SMEM] + [whole(state)] * (group + reach),
            out_specs=[whole(state)] * group,
            out_shape=[shape_of(*state)] * group,
            compiler_params=params(),
            name="entering",
        )(scalars, *states, *totals)

    def outputs(p, numerators, stats, entering):
        spec = pl.BlockSpec((1, tokens, part), lambda i, s: (i, 0, 0))
        return pl.pallas_call(
            output_kernel,
            grid_spec=pltpu.PrefetchScalarGridSpec(
                num_scalar_prefetch=1,
                grid=(group,),
                in_specs=[by_slot(q_keep), by_slot(q_oth)]
                + [
                    pl.BlockSpec((1, 2, tokens, part), lambda i, s: (i, 0, 0, p)),
                    pl.BlockSpec((1, 2, tokens, LANES), lambda i, s: (i, 0, 0, 0)),
                ]
                + [whole(state)] * group,
                out_specs=[spec] * 2,
                scratch_shapes=[pltpu.VMEM(state, BF16)],
            ),
            out_shape=[shape_of(half, tokens, part)] * 2,
            compiler_params=params(),
            name="outputs",
        )(scalars, q_keep, q_oth, numerators, stats, *entering)

    early = half // 2
    first_total = group_total(gathered[0])
    q_later, _ = lax.optimization_barrier((q_keep, first_total))
    terms = own_terms(0, early, q_later, ())
    gathered[1], terms = lax.optimization_barrier((gathered[1], terms))
    second_total = group_total(gathered[1])
    q_last, _ = lax.optimization_barrier((q_keep, second_total))
    terms = own_terms(early, half - early, q_last, terms)
    leaving = [entering_states(gathered[0], first_total)]
    gathered[1], leaving[0] = lax.optimization_barrier((gathered[1], leaving[0]))
    leaving.append(entering_states(gathered[1], second_total))
    (numerators, stats), _ = lax.optimization_barrier((terms, leaving[1][0]))
    kept, received = [], []
    for p in range(2):
        entering = [leaving[p][0]] + [in_group(leaving[p][r], r) for r in range(1, group)]
        keep, send = outputs(p, numerators, stats, entering)
        kept.append(keep)
        received.append(swap_cores(send))
    return pl.pallas_call(
        functools.partial(merge_kernel, heads),
        in_specs=[SMEM] + [whole(x.shape) for x in kept + received],
        out_specs=whole(value_vectors.shape),
        out_shape=shape_of(*value_vectors.shape),
        compiler_params=params(),
        name="merge",
    )(scalars, *kept, *received)


def solution(mesh):
    return jax.shard_map(
        functools.partial(local, mesh.size),
        mesh=mesh,
        in_specs=(
            P(AXES, None, None),
            P(AXES, None, None),
            P(AXES, None, None),
            P(AXES, None),
            P(AXES, None),
            P("ctx"),
        ),
        out_specs=P(AXES, None, None),
        check_vma=False,
    )
```

```python
import functools

import jax
import jax.numpy as jnp
from jax import lax
from jax.experimental import pallas as pl
from jax.experimental.pallas import tpu as pltpu
from jax.sharding import PartitionSpec as P

AXES = ("ctx", "hv")
FLOOR_NEG = -1e30
META = 16
LANES = 128
LAY = 256
F32, BF16 = jnp.float32, jnp.bfloat16

NN = (((1,), (0,)), ((), ()))
NT = (((1,), (1,)), ((), ()))


def dot(a, b, dims=NN):
    return lax.dot_general(a, b, dims, preferred_element_type=F32)


def split3(x):
    hi = x.astype(BF16).astype(F32)
    mid = (x - hi).astype(BF16).astype(F32)
    return hi, mid, (x - hi - mid).astype(BF16).astype(F32)


def iota(shape, dim):
    return lax.broadcasted_iota(jnp.int32, shape, dim)


def meta_rows(normalizer, top, decay, doc, width):
    used = normalizer.shape[1]
    row = iota((META, used), 0)
    rows = jnp.where(row == 6, wide(doc, used), 0.0)
    lines = split3(normalizer) + split3(jnp.concatenate([top, decay], axis=1))
    for index, line in enumerate(lines):
        rows = jnp.where(row == index, line, rows)
    spare = jnp.zeros((META, width - used), F32)
    return jnp.concatenate([rows, spare], axis=1).astype(BF16)


def read_meta(refs):
    key_width = refs[0].shape[0] - META
    rows = [ref[key_width:, : 2 * LANES].astype(F32) for ref in refs]
    normals = jnp.concatenate([(x[2:3] + x[1:2]) + x[0:1] for x in rows], axis=0)
    line = jnp.concatenate([(x[5:6] + x[4:5]) + x[3:4] for x in rows], axis=0)
    docs = jnp.concatenate([x[6:7, :LANES] for x in rows], axis=0)
    return normals, line[:, :LANES], line[:, LANES:], docs


def wide(x, width):
    return jnp.concatenate([x] * (width // LANES), axis=1)


def weighted(refs, coefs):
    key_width, width = refs[0].shape[0] - META, refs[0].shape[1]
    total = None
    for ref, coef in zip(refs, coefs, strict=True):
        term = wide(coef, width) * ref[:key_width, :].astype(F32)
        total = term if total is None else total + term
    return total


def gate_rows(core, own_ref, other_ref, heads):
    own, other = own_ref[...].astype(F32), other_ref[...].astype(F32)
    both = jnp.concatenate(
        [jnp.where(core == 0, own, other), jnp.where(core == 0, other, own)], axis=1
    )
    gate_in, forget = both[:heads], both[heads:]
    log_forget = jnp.minimum(forget, 0.0) - jnp.log1p(jnp.exp(-jnp.abs(forget)))
    length = both.shape[1]
    upto = (iota((length, length), 0) <= iota((length, length), 1)).astype(BF16)
    pieces = dot(jnp.concatenate(split3(log_forget), axis=0).astype(BF16), upto)
    decay = (pieces[2 * heads :] + pieces[heads : 2 * heads]) + pieces[:heads]
    return gate_in, decay


def by_head_order(heads):
    n = LAY // heads
    out, inside = iota((LAY, LAY), 0), iota((LAY, LAY), 1)
    return ((inside % heads == out // n) & (inside // heads == out % n)).astype(BF16)


def relayout_kernel(half, count, scalars, *refs):
    sources, outs = refs[:count], refs[count:]
    heads = 2 * half
    n = LAY // heads
    core = scalars[1]
    order = by_head_order(heads)
    for index, source in enumerate(sources):
        keep, send = outs[index], outs[count + index]
        tokens, _, width = source.shape
        for g in range(tokens // n):
            span = slice(g * n, (g + 1) * n)
            rows = dot(order, source[span].reshape(LAY, width)).astype(BF16)
            rows = rows.reshape(heads, n, width)
            keep[:, span, :] = jnp.where(core == 0, rows[:half], rows[half:])
            send[:, span, :] = jnp.where(core == 0, rows[half:], rows[:half])


def gates_kernel(heads, scalars, g_own, g_oth, ids_ref, *outs):
    factors, tops, decays, source_rows, decay_rows, columns = outs
    core = scalars[1]
    length = ids_ref.shape[1]
    gate_in, decay = gate_rows(core, g_own, g_oth, heads)
    ids = ids_ref[...]
    exponent = decay[:, length - 1 :] - decay + gate_in
    exponent = jnp.where(ids == ids[:, length - 1 :], exponent, FLOOR_NEG)
    top = jnp.max(exponent, axis=1, keepdims=True)
    factors[...] = jnp.exp(exponent - top)
    tops[...] = jnp.broadcast_to(top, tops.shape)
    decays[...] = jnp.broadcast_to(decay[:, length - 1 :], decays.shape)
    source_rows[...] = gate_in - decay
    decay_rows[...] = decay
    docs = ids.astype(F32) + 1.0
    filler = jnp.zeros((LANES - heads - 1, length), F32)
    columns[...] = jnp.concatenate([decay, docs, filler], axis=0).T


def state_kernel(heads, scalars, *refs):
    k_own, v_own, k_oth, v_oth, factors, tops, decays, ids_ref = refs[:8]
    outs, payload = refs[8:-1], refs[-1]
    step = pl.program_id(0)
    mine, core = scalars[0], scalars[1]
    tokens, key_width = k_own.shape[1:]
    length = 2 * tokens
    head = (heads // 2) * core + jnp.bitwise_xor(mine, step)
    row = factors[pl.ds(head, 1), :]
    first, last = row[:, :tokens], row[:, tokens:]
    total, normal = None, None
    for k_ref, v_ref, f in (
        (k_own, v_own, jnp.where(core == 0, first, last)),
        (k_oth, v_oth, jnp.where(core == 0, last, first)),
    ):
        keys, values = k_ref[0], v_ref[0]
        scaled = keys.astype(F32).T * f
        high = scaled.astype(BF16)
        low = (scaled - high.astype(F32)).astype(BF16)
        piece = dot(low, values) + dot(high, values)
        pieces = jnp.concatenate(split3(f) + (jnp.zeros((META - 3, tokens), F32),), axis=0)
        sums = dot(pieces.astype(BF16), keys)
        line = (sums[2:3] + sums[1:2]) + sums[0:1]
        total = piece if total is None else total + piece
        normal = line if normal is None else normal + line
    doc = jnp.broadcast_to(ids_ref[:, length - 1 :].astype(F32) + 1.0, (1, LANES))
    payload[:key_width, :] = total.astype(BF16)
    payload[key_width:, :] = meta_rows(
        normal, tops[pl.ds(head, 1), :], decays[pl.ds(head, 1), :], doc, payload.shape[1]
    )
    for i, out in enumerate(outs):

        @pl.when(step == i)
        def _(out=out):
            out[...] = payload[...]


def decay_before(mine, place, decays):
    group = decays.shape[0]
    before = jnp.zeros_like(decays)
    for i in range(group):
        before = before + jnp.where(place > jnp.bitwise_xor(mine, i), decays[i : i + 1], 0.0)
    return before


def total_kernel(group, scalars, *refs):
    states, out = refs[:group], refs[group]
    mine = scalars[0]
    key_width, width = out.shape[0] - META, out.shape[1]
    normals, tops, decays, docs = read_meta(states)
    place = jnp.bitwise_xor(iota((group, LANES), 0), mine)
    whole_decay = jnp.sum(decays, axis=0, keepdims=True)
    after = whole_decay - decay_before(mine, place, decays) - decays
    doc = jnp.sum(jnp.where(place == group - 1, docs, 0.0), axis=0, keepdims=True)
    alive = docs == doc
    reached = jnp.where(alive, tops + after, FLOOR_NEG)
    top = jnp.max(reached, axis=0, keepdims=True)
    coefs = jnp.where(alive, jnp.exp(reached - top), 0.0)
    out[:key_width, :] = weighted(
        states, [coefs[i : i + 1] for i in range(group)]
    ).astype(BF16)
    normal = jnp.sum(wide(coefs, key_width) * normals, axis=0, keepdims=True)
    out[key_width:, :] = meta_rows(normal, top, whole_decay, doc, width)


def entering_kernel(group, reach, scalars, *refs):
    states, totals, outs = refs[:group], refs[group : group + reach], refs[group + reach :]
    mine = scalars[0]
    key_width, width = outs[0].shape[0] - META, outs[0].shape[1]
    normals, tops, decays, docs = read_meta(states)
    far_normals, far_tops, far_decays, far_docs = read_meta(totals)
    place = jnp.bitwise_xor(iota((group, LANES), 0), mine)
    before = decay_before(mine, place, decays)
    zero = jnp.zeros((1, LANES), F32)
    far_reached, passed = [], zero
    for d in range(reach):
        far_reached.append(far_tops[d : d + 1] + passed)
        passed = passed + far_decays[d : d + 1]
    far_reached = jnp.concatenate(far_reached, axis=0)
    for r in range(group):
        here = jnp.bitwise_xor(mine, r)
        doc = jnp.sum(jnp.where(place == here - 1, docs, 0.0), axis=0, keepdims=True)
        doc = jnp.where(here == 0, far_docs[0:1], doc)
        mark = before[r : r + 1]
        alive = (place < here) & (docs == doc)
        reached = jnp.where(alive, tops + (mark - before - decays), FLOOR_NEG)
        far_alive = (far_docs == doc) & (far_docs > 0.5)
        far = jnp.where(far_alive, far_reached + mark, FLOOR_NEG)
        top = jnp.maximum(
            jnp.max(reached, axis=0, keepdims=True), jnp.max(far, axis=0, keepdims=True)
        )
        coefs = jnp.where(alive, jnp.exp(reached - top), 0.0)
        far_coefs = jnp.where(far_alive, jnp.exp(far - top), 0.0)
        others = [i for i in range(group) if i != r]
        outs[r][:key_width, :] = weighted(
            [states[i] for i in others] + list(totals),
            [coefs[i : i + 1] for i in others]
            + [far_coefs[d : d + 1] for d in range(reach)],
        ).astype(BF16)
        normal = jnp.sum(wide(coefs, key_width) * normals, axis=0, keepdims=True)
        normal = normal + jnp.sum(wide(far_coefs, key_width) * far_normals, axis=0, keepdims=True)
        outs[r][key_width:, :] = meta_rows(normal, top, zero, doc, width)


def local_kernel(heads, scalars, *refs):
    q_own, k_own, v_own, q_oth, k_oth, v_oth, source_rows, decay_rows, columns, ids_ref = refs[:10]
    numerators, stats = refs[10:]
    step = pl.program_id(0)
    mine, core = scalars[0], scalars[1]
    tokens, key_width = q_own.shape[1:]
    length = 2 * tokens
    scaling = key_width**-0.5
    head = (heads // 2) * core + jnp.bitwise_xor(mine, step)
    is_first = core == 0
    source = source_rows[pl.ds(head, 1), :]
    lane = iota((length, LANES), 1)
    turned = columns[...]
    decay = jnp.sum(jnp.where(lane == head, turned, 0.0), axis=1, keepdims=True)
    docs = turned[:, heads : heads + 1]
    source_docs = ids_ref[...].astype(F32) + 1.0
    causal = iota((tokens, tokens), 0) >= iota((tokens, tokens), 1)

    def ordered(own, other):
        own, other = own[0], other[0]
        return jnp.where(is_first, own, other), jnp.where(is_first, other, own)

    queries, keys, values = ordered(q_own, q_oth), ordered(k_own, k_oth), ordered(v_own, v_oth)
    for block in range(2):
        rows = slice(block * tokens, (block + 1) * tokens)
        exponents = []
        for s in range(block + 1):
            cols = slice(s * tokens, (s + 1) * tokens)
            allowed = docs[rows] == source_docs[:, cols]
            if s == block:
                allowed = allowed & causal
            exponents.append(jnp.where(allowed, decay[rows] + source[:, cols], FLOOR_NEG))
        stabilizer = functools.reduce(
            jnp.maximum, [jnp.max(x, axis=1, keepdims=True) for x in exponents]
        )
        numerator, denominator = None, None
        for s in range(block + 1):
            weights = dot(queries[block], keys[s], NT) * scaling
            weights = weights * jnp.exp(exponents[s] - stabilizer)
            high = weights.astype(BF16)
            part = dot(high, values[s])
            if s < block:
                part = part + dot((weights - high.astype(F32)).astype(BF16), values[s])
            numerator = part if s == 0 else numerator + part
            part = jnp.sum(weights, axis=1, keepdims=True)
            denominator = part if s == 0 else denominator + part
        side = core if block == 0 else 1 - core
        numerators[0, side] = numerator
        lane = iota((tokens, LANES), 1)
        pair = jnp.where(lane == 0, stabilizer, denominator).T
        stats[0, side] = jnp.concatenate(
            [pair[:2], decay_rows[pl.ds(head, 1), rows], source_docs[:, rows], pair[4:8]], axis=0
        )


def output_kernel(scalars, q_own, q_oth, numerators, stats, *refs):
    entering, (keep, send, payload) = refs[:-3], refs[-3:]
    step = pl.program_id(0)
    key_width = q_own.shape[2]
    scaling = key_width**-0.5
    for i, ref in enumerate(entering):

        @pl.when(step == i)
        def _(ref=ref):
            payload[...] = ref[...]

    normal, top, _, doc = read_meta([payload])
    pieces = jnp.concatenate(split3(normal) + (jnp.zeros((META - 3, key_width), F32),), axis=0)
    pieces = pieces.astype(BF16)
    memory = payload[:key_width, :]
    width = memory.shape[1]
    for side, (q_ref, out) in enumerate(((q_own, keep), (q_oth, send))):
        query = q_ref[0]
        tokens = query.shape[0]
        stat = stats[0, side]
        local = stat[0:1]
        alive = stat[3:4] == wide(doc, tokens)
        carried = jnp.where(alive, stat[2:3] + wide(top, tokens), FLOOR_NEG)
        stabilizer = jnp.maximum(local, carried)
        shrink = jnp.exp(local - stabilizer)
        retained = jnp.exp(carried - stabilizer) * scaling
        seen = dot(pieces, query, NT)
        seen = (seen[2:3] + seen[1:2]) + seen[0:1]
        denominator = shrink * stat[1:2] + retained * seen
        inverse = 1.0 / jnp.maximum(jnp.abs(denominator), 1.0)
        near = jnp.broadcast_to(shrink * inverse, (LANES, tokens)).T
        far = jnp.broadcast_to(retained * inverse, (LANES, tokens)).T
        result = wide(near, width) * numerators[0, side]
        out[0] = (result + wide(far, width) * dot(query, memory)).astype(BF16)


def merge_kernel(heads, scalars, *refs):
    stacks, out = refs[:-1], refs[-1]
    half = heads // 2
    n = LAY // heads
    mine, core = scalars[0], scalars[1]
    into, given = iota((LAY, LAY), 0), iota((LAY, LAY), 1)
    index = given // n
    slot = jnp.bitwise_and(index, half - 1)
    side = jnp.where(index < half, core, 1 - core)
    head = side * half + jnp.bitwise_xor(slot, mine)
    order = ((into % heads == head) & (into // heads == given % n)).astype(BF16)
    _, tokens, width = stacks[0].shape
    for g in range(tokens // n):
        span = slice(g * n, (g + 1) * n)
        rows = jnp.concatenate([stack[:, span, :] for stack in stacks], axis=0)
        turned = dot(order, rows.reshape(LAY, width))
        out[span] = turned.reshape(n, heads, width).astype(BF16)


def whole(shape):
    return pl.BlockSpec(shape, lambda *_: (0,) * len(shape))


def params():
    return pltpu.CompilerParams(vmem_limit_bytes=56 * 2**20)


SMEM = pl.BlockSpec(memory_space=pltpu.SMEM)


def shape_of(*dims, dtype=BF16):
    return jax.ShapeDtypeStruct(dims, dtype)


def local(devices, queries, key_vectors, value_vectors, input_gate, forget_gate, doc_ids):
    tokens, heads, key_width = queries.shape
    value_width = value_vectors.shape[2]
    half = heads // 2
    group = half
    chips = devices // 2
    levels = chips // group
    reach = max(1, levels // 2)
    ctx, hv = lax.axis_index("ctx"), lax.axis_index("hv")
    chip = ctx * (lax.axis_size("hv") // 2) + hv // 2
    scalars = jnp.stack([chip % group, hv % 2]).astype(jnp.int32)
    ids = lax.dynamic_slice(doc_ids, ((hv // 2) * 2 * tokens,), (2 * tokens,))[None, :]

    def swap_cores(x):
        return lax.ppermute(x, AXES, [(d, d ^ 1) for d in range(devices)])

    def in_group(x, r):
        pairs = [(d, d ^ (2 * r)) for d in range(devices)]
        return lax.ppermute(x, AXES, pairs)

    def to_later(x, levels_on):
        jump = 2 * group * levels_on
        return lax.ppermute(x, AXES, [(d, d + jump) for d in range(devices - jump)])

    rows = key_width + META
    state = (rows, value_width)
    sizes = {key_width: (half, tokens, key_width), value_width: (half, tokens, value_width)}

    def relayout(*sources):
        outs = [sizes[x.shape[2]] for x in sources] * 2
        return pl.pallas_call(
            functools.partial(relayout_kernel, half, len(sources)),
            in_specs=[SMEM] + [whole(x.shape) for x in sources],
            out_specs=[whole(s) for s in outs],
            out_shape=[shape_of(*s) for s in outs],
            compiler_params=params(),
            name="relayout",
        )(scalars, *sources)

    gates = jnp.concatenate([input_gate.T, forget_gate.T], axis=0)
    gates, key_vectors = lax.optimization_barrier((gates, key_vectors))
    gates_oth = swap_cores(gates)
    k_keep, v_keep, k_send, v_send = relayout(key_vectors, value_vectors)
    gates_oth, k_send, v_send = lax.optimization_barrier((gates_oth, k_send, v_send))
    k_oth = swap_cores(k_send)
    v_oth = swap_cores(v_send)
    gate_shapes = [
        (heads, 2 * tokens),
        (heads, LANES),
        (heads, LANES),
        (heads, 2 * tokens),
        (heads, 2 * tokens),
        (2 * tokens, LANES),
    ]
    factors, tops, decays, source_rows, decay_rows, columns = pl.pallas_call(
        functools.partial(gates_kernel, heads),
        in_specs=[SMEM] + [whole(gates.shape)] * 2 + [whole(ids.shape)],
        out_specs=[whole(s) for s in gate_shapes],
        out_shape=[shape_of(*s, dtype=F32) for s in gate_shapes],
        compiler_params=params(),
        name="gates",
    )(scalars, gates, gates_oth, ids)

    def by_slot(x, first_slot=0):
        return pl.BlockSpec(
            (1,) + x.shape[1:], lambda i, s: (jnp.bitwise_xor(s[0], first_slot + i), 0, 0)
        )

    made = pl.pallas_call(
        functools.partial(state_kernel, heads),
        grid_spec=pltpu.PrefetchScalarGridSpec(
            num_scalar_prefetch=1,
            grid=(group,),
            in_specs=[by_slot(x) for x in (k_keep, v_keep, k_oth, v_oth)]
            + [whole(x.shape) for x in (factors, tops, decays, ids)],
            out_specs=[whole(state)] * group,
            scratch_shapes=[pltpu.VMEM(state, BF16)],
        ),
        out_shape=[shape_of(*state)] * group,
        compiler_params=params(),
        name="states",
    )(scalars, k_keep, v_keep, k_oth, v_oth, factors, tops, decays, ids)
    gathered = [made[0]] + [in_group(made[r], r) for r in range(1, group)]
    total = pl.pallas_call(
        functools.partial(total_kernel, group),
        in_specs=[SMEM] + [whole(state)] * group,
        out_specs=whole(state),
        out_shape=shape_of(*state),
        compiler_params=params(),
        name="group_total",
    )(scalars, *gathered)
    totals = [to_later(total, d) for d in range(1, reach + 1)]

    queries, gathered[0] = lax.optimization_barrier((queries, gathered[0]))
    q_keep, q_send = relayout(queries)
    q_oth = swap_cores(q_send)
    by_head = (q_keep, k_keep, v_keep, q_oth, k_oth, v_oth)
    small = (source_rows, decay_rows, columns, ids)
    local_shapes = [(half, 2, tokens, value_width), (half, 2, 8, tokens)]
    numerators, stats = pl.pallas_call(
        functools.partial(local_kernel, heads),
        grid_spec=pltpu.PrefetchScalarGridSpec(
            num_scalar_prefetch=1,
            grid=(group,),
            in_specs=[by_slot(x) for x in by_head] + [whole(x.shape) for x in small],
            out_specs=[
                pl.BlockSpec((1,) + s[1:], lambda i, _: (i, 0, 0, 0)) for s in local_shapes
            ],
        ),
        out_shape=[shape_of(*s, dtype=F32) for s in local_shapes],
        compiler_params=params(),
        name="own_terms",
    )(scalars, *by_head, *small)
    gathered[0], numerators = lax.optimization_barrier((gathered[0], numerators))

    leaving = pl.pallas_call(
        functools.partial(entering_kernel, group, reach),
        in_specs=[SMEM] + [whole(state)] * (group + reach),
        out_specs=[whole(state)] * group,
        out_shape=[shape_of(*state)] * group,
        compiler_params=params(),
        name="entering",
    )(scalars, *gathered, *totals)
    entering = [leaving[0]] + [in_group(leaving[r], r) for r in range(1, group)]

    kept, received = [], []
    for first, count in ((0, 1), (1, group - 1)):
        spec = pl.BlockSpec((1, tokens, value_width), lambda i, s: (i, 0, 0))
        keep, send = pl.pallas_call(
            output_kernel,
            grid_spec=pltpu.PrefetchScalarGridSpec(
                num_scalar_prefetch=1,
                grid=(count,),
                in_specs=[by_slot(q_keep, first), by_slot(q_oth, first)]
                + [
                    pl.BlockSpec((1,) + s[1:], lambda i, _, first=first: (first + i, 0, 0, 0))
                    for s in local_shapes
                ]
                + [whole(state)] * count,
                out_specs=[spec] * 2,
                scratch_shapes=[pltpu.VMEM(state, BF16)],
            ),
            out_shape=[shape_of(count, tokens, value_width)] * 2,
            compiler_params=params(),
            name="outputs",
        )(scalars, q_keep, q_oth, numerators, stats, *entering[first : first + count])
        kept.append(keep)
        swapped = swap_cores(send)
        numerators, swapped = lax.optimization_barrier((numerators, swapped))
        received.append(swapped)
    return pl.pallas_call(
        functools.partial(merge_kernel, heads),
        in_specs=[SMEM] + [whole(x.shape) for x in kept + received],
        out_specs=whole(value_vectors.shape),
        out_shape=shape_of(*value_vectors.shape),
        compiler_params=params(),
        name="merge",
    )(scalars, *kept, *received)


def solution(mesh):
    return jax.shard_map(
        functools.partial(local, mesh.size),
        mesh=mesh,
        in_specs=(
            P(AXES, None, None),
            P(AXES, None, None),
            P(AXES, None, None),
            P(AXES, None),
            P(AXES, None),
            P("ctx"),
        ),
        out_specs=P(AXES, None, None),
        check_vma=False,
    )
```

```python
import functools

import jax
import jax.numpy as jnp
from jax import lax
from jax.experimental import pallas as pl
from jax.experimental.pallas import tpu as pltpu
from jax.sharding import PartitionSpec as P

AXES = ("ctx", "hv")
FLOOR_NEG = -1e30
META = 16
LANES = 128
LAY = 256
F32, BF16 = jnp.float32, jnp.bfloat16

NN = (((1,), (0,)), ((), ()))
NT = (((1,), (1,)), ((), ()))


def dot(a, b, dims=NN):
    return lax.dot_general(a, b, dims, preferred_element_type=F32)


def split3(x):
    hi = x.astype(BF16).astype(F32)
    mid = (x - hi).astype(BF16).astype(F32)
    return hi, mid, (x - hi - mid).astype(BF16).astype(F32)


def iota(shape, dim):
    return lax.broadcasted_iota(jnp.int32, shape, dim)


def meta_rows(normalizer, top, decay, doc, width):
    used = normalizer.shape[1]
    row = iota((META, used), 0)
    rows = jnp.where(row == 6, wide(doc, used), 0.0)
    lines = split3(normalizer) + split3(jnp.concatenate([top, decay], axis=1))
    for index, line in enumerate(lines):
        rows = jnp.where(row == index, line, rows)
    spare = jnp.zeros((META, width - used), F32)
    return jnp.concatenate([rows, spare], axis=1).astype(BF16)


def read_meta(refs):
    key_width = refs[0].shape[0] - META
    rows = [ref[key_width:, : 2 * LANES].astype(F32) for ref in refs]
    normals = jnp.concatenate([(x[2:3] + x[1:2]) + x[0:1] for x in rows], axis=0)
    line = jnp.concatenate([(x[5:6] + x[4:5]) + x[3:4] for x in rows], axis=0)
    docs = jnp.concatenate([x[6:7, :LANES] for x in rows], axis=0)
    return normals, line[:, :LANES], line[:, LANES:], docs


def wide(x, width):
    return jnp.concatenate([x] * (width // LANES), axis=1)


def weighted(refs, coefs):
    key_width, width = refs[0].shape[0] - META, refs[0].shape[1]
    total = None
    for ref, coef in zip(refs, coefs, strict=True):
        term = wide(coef, width) * ref[:key_width, :].astype(F32)
        total = term if total is None else total + term
    return total


def gate_rows(core, own_ref, other_ref, heads):
    own, other = own_ref[...].astype(F32), other_ref[...].astype(F32)
    both = jnp.concatenate(
        [jnp.where(core == 0, own, other), jnp.where(core == 0, other, own)], axis=1
    )
    gate_in, forget = both[:heads], both[heads:]
    log_forget = jnp.minimum(forget, 0.0) - jnp.log1p(jnp.exp(-jnp.abs(forget)))
    length = both.shape[1]
    upto = (iota((length, length), 0) <= iota((length, length), 1)).astype(BF16)
    pieces = dot(jnp.concatenate(split3(log_forget), axis=0).astype(BF16), upto)
    decay = (pieces[2 * heads :] + pieces[heads : 2 * heads]) + pieces[:heads]
    return gate_in, decay


def by_head_order(heads):
    n = LAY // heads
    out, inside = iota((LAY, LAY), 0), iota((LAY, LAY), 1)
    return ((inside % heads == out // n) & (inside // heads == out % n)).astype(BF16)


def relayout_kernel(half, count, scalars, *refs):
    sources, outs = refs[:count], refs[count:]
    heads = 2 * half
    n = LAY // heads
    core = scalars[1]
    order = by_head_order(heads)
    for index, source in enumerate(sources):
        keep, send = outs[index], outs[count + index]
        tokens, _, width = source.shape
        for g in range(tokens // n):
            span = slice(g * n, (g + 1) * n)
            rows = dot(order, source[span].reshape(LAY, width)).astype(BF16)
            rows = rows.reshape(heads, n, width)
            keep[:, span, :] = jnp.where(core == 0, rows[:half], rows[half:])
            send[:, span, :] = jnp.where(core == 0, rows[half:], rows[:half])


def gates_kernel(heads, scalars, g_own, g_oth, ids_ref, *outs):
    factors, tops, decays, source_rows, decay_rows, columns = outs
    core = scalars[1]
    length = ids_ref.shape[1]
    gate_in, decay = gate_rows(core, g_own, g_oth, heads)
    ids = ids_ref[...]
    exponent = decay[:, length - 1 :] - decay + gate_in
    exponent = jnp.where(ids == ids[:, length - 1 :], exponent, FLOOR_NEG)
    top = jnp.max(exponent, axis=1, keepdims=True)
    factors[...] = jnp.exp(exponent - top)
    tops[...] = jnp.broadcast_to(top, tops.shape)
    decays[...] = jnp.broadcast_to(decay[:, length - 1 :], decays.shape)
    source_rows[...] = gate_in - decay
    decay_rows[...] = decay
    docs = ids.astype(F32) + 1.0
    filler = jnp.zeros((LANES - heads - 1, length), F32)
    columns[...] = jnp.concatenate([decay, docs, filler], axis=0).T


def state_kernel(slot_of, heads, scalars, *refs):
    k_own, v_own, k_oth, v_oth, factors, tops, decays, ids_ref = refs[:8]
    outs, payload = refs[8:-1], refs[-1]
    step = pl.program_id(0)
    mine, core = scalars[0], scalars[1]
    tokens, key_width = k_own.shape[1:]
    length = 2 * tokens
    head = (heads // 2) * core + jnp.bitwise_xor(mine, slot_of(step))
    row = factors[pl.ds(head, 1), :]
    first, last = row[:, :tokens], row[:, tokens:]
    high, low, values, normal = [], [], [], None
    for k_ref, v_ref, f in (
        (k_own, v_own, jnp.where(core == 0, first, last)),
        (k_oth, v_oth, jnp.where(core == 0, last, first)),
    ):
        keys = k_ref[0]
        scaled = keys.astype(F32).T * f
        high.append(scaled.astype(BF16))
        low.append((scaled - high[-1].astype(F32)).astype(BF16))
        values.append(v_ref[0])
        pieces = jnp.concatenate(split3(f) + (jnp.zeros((META - 3, tokens), F32),), axis=0)
        sums = dot(pieces.astype(BF16), keys)
        line = (sums[2:3] + sums[1:2]) + sums[0:1]
        normal = line if normal is None else normal + line
    total = dot(jnp.concatenate(low + high, axis=1), jnp.concatenate(values * 2, axis=0))
    doc = jnp.broadcast_to(ids_ref[:, length - 1 :].astype(F32) + 1.0, (1, LANES))
    payload[:key_width, :] = total.astype(BF16)
    payload[key_width:, :] = meta_rows(
        normal, tops[pl.ds(head, 1), :], decays[pl.ds(head, 1), :], doc, payload.shape[1]
    )
    for i, out in enumerate(outs):

        @pl.when(step == i)
        def _(out=out):
            out[...] = payload[...]


def decay_before(mine, place, decays):
    group = decays.shape[0]
    before = jnp.zeros_like(decays)
    for i in range(group):
        before = before + jnp.where(place > jnp.bitwise_xor(mine, i), decays[i : i + 1], 0.0)
    return before


def total_kernel(group, scalars, *refs):
    states, out = refs[:group], refs[group]
    mine = scalars[0]
    key_width, width = out.shape[0] - META, out.shape[1]
    normals, tops, decays, docs = read_meta(states)
    place = jnp.bitwise_xor(iota((group, LANES), 0), mine)
    whole_decay = jnp.sum(decays, axis=0, keepdims=True)
    after = whole_decay - decay_before(mine, place, decays) - decays
    doc = jnp.sum(jnp.where(place == group - 1, docs, 0.0), axis=0, keepdims=True)
    alive = docs == doc
    reached = jnp.where(alive, tops + after, FLOOR_NEG)
    top = jnp.max(reached, axis=0, keepdims=True)
    coefs = jnp.where(alive, jnp.exp(reached - top), 0.0)
    out[:key_width, :] = weighted(
        states, [coefs[i : i + 1] for i in range(group)]
    ).astype(BF16)
    normal = jnp.sum(wide(coefs, key_width) * normals, axis=0, keepdims=True)
    out[key_width:, :] = meta_rows(normal, top, whole_decay, doc, width)


def entering_kernel(group, reach, scalars, *refs):
    states, totals, outs = refs[:group], refs[group : group + reach], refs[group + reach :]
    mine = scalars[0]
    key_width, width = outs[0].shape[0] - META, outs[0].shape[1]
    normals, tops, decays, docs = read_meta(states)
    far_normals, far_tops, far_decays, far_docs = read_meta(totals)
    place = jnp.bitwise_xor(iota((group, LANES), 0), mine)
    before = decay_before(mine, place, decays)
    zero = jnp.zeros((1, LANES), F32)
    far_reached, passed = [], zero
    for d in range(reach):
        far_reached.append(far_tops[d : d + 1] + passed)
        passed = passed + far_decays[d : d + 1]
    far_reached = jnp.concatenate(far_reached, axis=0)
    for r in range(group):
        here = jnp.bitwise_xor(mine, r)
        doc = jnp.sum(jnp.where(place == here - 1, docs, 0.0), axis=0, keepdims=True)
        doc = jnp.where(here == 0, far_docs[0:1], doc)
        mark = before[r : r + 1]
        alive = (place < here) & (docs == doc)
        reached = jnp.where(alive, tops + (mark - before - decays), FLOOR_NEG)
        far_alive = (far_docs == doc) & (far_docs > 0.5)
        far = jnp.where(far_alive, far_reached + mark, FLOOR_NEG)
        top = jnp.maximum(
            jnp.max(reached, axis=0, keepdims=True), jnp.max(far, axis=0, keepdims=True)
        )
        coefs = jnp.where(alive, jnp.exp(reached - top), 0.0)
        far_coefs = jnp.where(far_alive, jnp.exp(far - top), 0.0)
        others = [i for i in range(group) if i != r]
        outs[r][:key_width, :] = weighted(
            [states[i] for i in others] + list(totals),
            [coefs[i : i + 1] for i in others]
            + [far_coefs[d : d + 1] for d in range(reach)],
        ).astype(BF16)
        normal = jnp.sum(wide(coefs, key_width) * normals, axis=0, keepdims=True)
        normal = normal + jnp.sum(wide(far_coefs, key_width) * far_normals, axis=0, keepdims=True)
        outs[r][key_width:, :] = meta_rows(normal, top, zero, doc, width)


def local_kernel(heads, scalars, *refs):
    q_own, k_own, v_own, q_oth, k_oth, v_oth, source_rows, decay_rows, columns, ids_ref = refs[:10]
    numerators, stats = refs[10:]
    step = pl.program_id(0)
    mine, core = scalars[0], scalars[1]
    tokens, key_width = q_own.shape[1:]
    length = 2 * tokens
    scaling = key_width**-0.5
    head = (heads // 2) * core + jnp.bitwise_xor(mine, step)
    is_first = core == 0
    source = source_rows[pl.ds(head, 1), :]
    lane = iota((length, LANES), 1)
    turned = columns[...]
    decay = jnp.sum(jnp.where(lane == head, turned, 0.0), axis=1, keepdims=True)
    docs = turned[:, heads : heads + 1]
    source_docs = ids_ref[...].astype(F32) + 1.0
    causal = iota((tokens, tokens), 0) >= iota((tokens, tokens), 1)

    def ordered(own, other):
        own, other = own[0], other[0]
        return jnp.where(is_first, own, other), jnp.where(is_first, other, own)

    queries, keys, values = ordered(q_own, q_oth), ordered(k_own, k_oth), ordered(v_own, v_oth)
    for block in range(2):
        rows = slice(block * tokens, (block + 1) * tokens)
        exponents = []
        for s in range(block + 1):
            cols = slice(s * tokens, (s + 1) * tokens)
            allowed = docs[rows] == source_docs[:, cols]
            if s == block:
                allowed = allowed & causal
            exponents.append(jnp.where(allowed, decay[rows] + source[:, cols], FLOOR_NEG))
        stabilizer = functools.reduce(
            jnp.maximum, [jnp.max(x, axis=1, keepdims=True) for x in exponents]
        )
        factors, sources, denominator = [], [], None
        for s in range(block + 1):
            weights = dot(queries[block], keys[s], NT) * scaling
            weights = weights * jnp.exp(exponents[s] - stabilizer)
            high = weights.astype(BF16)
            factors.append(high)
            sources.append(values[s])
            if s < block:
                factors.append((weights - high.astype(F32)).astype(BF16))
                sources.append(values[s])
            part = jnp.sum(weights, axis=1, keepdims=True)
            denominator = part if s == 0 else denominator + part
        numerator = dot(jnp.concatenate(factors, axis=1), jnp.concatenate(sources, axis=0))
        side = core if block == 0 else 1 - core
        numerators[0, side] = numerator
        lane = iota((tokens, LANES), 1)
        pair = jnp.where(lane == 0, stabilizer, denominator).T
        stats[0, side] = jnp.concatenate(
            [pair[:2], decay_rows[pl.ds(head, 1), rows], source_docs[:, rows], pair[4:8]], axis=0
        )


def output_kernel(sides, scalars, *refs):
    count = len(sides)
    query_refs, numerators, stats = refs[:count], refs[count], refs[count + 1]
    outs, payload = refs[-1 - count : -1], refs[-1]
    entering = refs[count + 2 : -1 - count]
    step = pl.program_id(0)
    key_width = query_refs[0].shape[2]
    scaling = key_width**-0.5
    for i, ref in enumerate(entering):

        @pl.when(step == i)
        def _(ref=ref):
            payload[...] = ref[...]

    normal, top, _, doc = read_meta([payload])
    pieces = jnp.concatenate(split3(normal) + (jnp.zeros((META - 3, key_width), F32),), axis=0)
    pieces = pieces.astype(BF16)
    memory = payload[:key_width, :]
    width = memory.shape[1]
    for side, (q_ref, out) in enumerate(zip(query_refs, outs, strict=True)):
        query = q_ref[0]
        tokens = query.shape[0]
        stat = stats[0, side]
        local = stat[0:1]
        alive = stat[3:4] == wide(doc, tokens)
        carried = jnp.where(alive, stat[2:3] + wide(top, tokens), FLOOR_NEG)
        stabilizer = jnp.maximum(local, carried)
        shrink = jnp.exp(local - stabilizer)
        retained = jnp.exp(carried - stabilizer) * scaling
        seen = dot(pieces, query, NT)
        seen = (seen[2:3] + seen[1:2]) + seen[0:1]
        denominator = shrink * stat[1:2] + retained * seen
        inverse = 1.0 / jnp.maximum(jnp.abs(denominator), 1.0)
        near = jnp.broadcast_to(shrink * inverse, (LANES, tokens)).T
        far = jnp.broadcast_to(retained * inverse, (LANES, tokens)).T
        result = wide(near, width) * numerators[0, side]
        out[0] = (result + wide(far, width) * dot(query, memory)).astype(BF16)


def merge_kernel(heads, scalars, *refs):
    stacks, out = refs[:-1], refs[-1]
    half = heads // 2
    n = LAY // heads
    mine, core = scalars[0], scalars[1]
    into, given = iota((LAY, LAY), 0), iota((LAY, LAY), 1)
    index = given // n
    slot = jnp.bitwise_and(index, half - 1)
    side = jnp.where(index < half, core, 1 - core)
    head = side * half + jnp.bitwise_xor(slot, mine)
    order = ((into % heads == head) & (into // heads == given % n)).astype(BF16)
    _, tokens, width = stacks[0].shape
    for g in range(tokens // n):
        span = slice(g * n, (g + 1) * n)
        rows = jnp.concatenate([stack[:, span, :] for stack in stacks], axis=0)
        turned = dot(order, rows.reshape(LAY, width))
        out[span] = turned.reshape(n, heads, width).astype(BF16)


def whole(shape):
    return pl.BlockSpec(shape, lambda *_: (0,) * len(shape))


def params():
    return pltpu.CompilerParams(vmem_limit_bytes=56 * 2**20)


SMEM = pl.BlockSpec(memory_space=pltpu.SMEM)


def shape_of(*dims, dtype=BF16):
    return jax.ShapeDtypeStruct(dims, dtype)


def local(devices, queries, key_vectors, value_vectors, input_gate, forget_gate, doc_ids):
    tokens, heads, key_width = queries.shape
    value_width = value_vectors.shape[2]
    half = heads // 2
    group = half
    chips = devices // 2
    levels = chips // group
    reach = max(1, levels // 2)
    ctx, hv = lax.axis_index("ctx"), lax.axis_index("hv")
    chip = ctx * (lax.axis_size("hv") // 2) + hv // 2
    scalars = jnp.stack([chip % group, hv % 2]).astype(jnp.int32)
    ids = lax.dynamic_slice(doc_ids, ((hv // 2) * 2 * tokens,), (2 * tokens,))[None, :]

    def swap_cores(x):
        return lax.ppermute(x, AXES, [(d, d ^ 1) for d in range(devices)])

    def in_group(x, r):
        pairs = [(d, d ^ (2 * r)) for d in range(devices)]
        return lax.ppermute(x, AXES, pairs)

    def to_later(x, levels_on):
        jump = 2 * group * levels_on
        return lax.ppermute(x, AXES, [(d, d + jump) for d in range(devices - jump)])

    rows = key_width + META
    state = (rows, value_width)
    sizes = {key_width: (half, tokens, key_width), value_width: (half, tokens, value_width)}

    def relayout(*sources):
        outs = [sizes[x.shape[2]] for x in sources] * 2
        return pl.pallas_call(
            functools.partial(relayout_kernel, half, len(sources)),
            in_specs=[SMEM] + [whole(x.shape) for x in sources],
            out_specs=[whole(s) for s in outs],
            out_shape=[shape_of(*s) for s in outs],
            compiler_params=params(),
            name="relayout",
        )(scalars, *sources)

    gates = jnp.concatenate([input_gate.T, forget_gate.T], axis=0)
    gates, key_vectors = lax.optimization_barrier((gates, key_vectors))
    gates_oth = swap_cores(gates)
    k_keep, v_keep, k_send, v_send = relayout(key_vectors, value_vectors)
    gates_oth, k_send, v_send = lax.optimization_barrier((gates_oth, k_send, v_send))
    k_oth = swap_cores(k_send)
    v_oth = swap_cores(v_send)
    gate_shapes = [
        (heads, 2 * tokens),
        (heads, LANES),
        (heads, LANES),
        (heads, 2 * tokens),
        (heads, 2 * tokens),
        (2 * tokens, LANES),
    ]
    factors, tops, decays, source_rows, decay_rows, columns = pl.pallas_call(
        functools.partial(gates_kernel, heads),
        in_specs=[SMEM] + [whole(gates.shape)] * 2 + [whole(ids.shape)],
        out_specs=[whole(s) for s in gate_shapes],
        out_shape=[shape_of(*s, dtype=F32) for s in gate_shapes],
        compiler_params=params(),
        name="gates",
    )(scalars, gates, gates_oth, ids)

    def by_slot(x, slot_of=lambda i: i):
        return pl.BlockSpec(
            (1,) + x.shape[1:], lambda i, s: (jnp.bitwise_xor(s[0], slot_of(i)), 0, 0)
        )

    made = [None] * group
    for first in (1, 0):
        slot_of = lambda i, first=first: group - 2 + first - 2 * i
        slots = [slot_of(i) for i in range(half // 2)]
        outs = pl.pallas_call(
            functools.partial(state_kernel, slot_of, heads),
            grid_spec=pltpu.PrefetchScalarGridSpec(
                num_scalar_prefetch=1,
                grid=(len(slots),),
                in_specs=[by_slot(x, slot_of) for x in (k_keep, v_keep, k_oth, v_oth)]
                + [whole(x.shape) for x in (factors, tops, decays, ids)],
                out_specs=[whole(state)] * len(slots),
                scratch_shapes=[pltpu.VMEM(state, BF16)],
            ),
            out_shape=[shape_of(*state)] * len(slots),
            compiler_params=params(),
            name="states",
        )(scalars, k_keep, v_keep, k_oth, v_oth, factors, tops, decays, ids)
        for slot, out in zip(slots, outs, strict=True):
            made[slot] = out
    gathered = [made[0]] + [in_group(made[r], r) for r in range(1, group)]
    total = pl.pallas_call(
        functools.partial(total_kernel, group),
        in_specs=[SMEM] + [whole(state)] * group,
        out_specs=whole(state),
        out_shape=shape_of(*state),
        compiler_params=params(),
        name="group_total",
    )(scalars, *gathered)
    totals = [to_later(total, d) for d in range(1, reach + 1)]

    queries, gathered[0] = lax.optimization_barrier((queries, gathered[0]))
    q_keep, q_send = relayout(queries)
    q_oth = swap_cores(q_send)
    by_head = (q_keep, k_keep, v_keep, q_oth, k_oth, v_oth)
    small = (source_rows, decay_rows, columns, ids)
    local_shapes = [(half, 2, tokens, value_width), (half, 2, 8, tokens)]
    numerators, stats = pl.pallas_call(
        functools.partial(local_kernel, heads),
        grid_spec=pltpu.PrefetchScalarGridSpec(
            num_scalar_prefetch=1,
            grid=(group,),
            in_specs=[by_slot(x) for x in by_head] + [whole(x.shape) for x in small],
            out_specs=[
                pl.BlockSpec((1,) + s[1:], lambda i, _: (i, 0, 0, 0)) for s in local_shapes
            ],
        ),
        out_shape=[shape_of(*s, dtype=F32) for s in local_shapes],
        compiler_params=params(),
        name="own_terms",
    )(scalars, *by_head, *small)
    gathered[0], numerators = lax.optimization_barrier((gathered[0], numerators))

    leaving = pl.pallas_call(
        functools.partial(entering_kernel, group, reach),
        in_specs=[SMEM] + [whole(state)] * (group + reach),
        out_specs=[whole(state)] * group,
        out_shape=[shape_of(*state)] * group,
        compiler_params=params(),
        name="entering",
    )(scalars, *gathered, *totals)
    entering = [leaving[0]] + [in_group(leaving[r], r) for r in range(1, group)]

    def outputs(first, count, first_side, sides):
        spec = pl.BlockSpec((1, tokens, value_width), lambda i, s: (i, 0, 0))
        relaid = (q_keep, q_oth)[first_side : first_side + sides]
        return pl.pallas_call(
            functools.partial(output_kernel, range(sides)),
            grid_spec=pltpu.PrefetchScalarGridSpec(
                num_scalar_prefetch=1,
                grid=(count,),
                in_specs=[by_slot(x, lambda i: first + i) for x in relaid]
                + [
                    pl.BlockSpec(
                        (1, sides) + s[2:], lambda i, _: (first + i, first_side // sides, 0, 0)
                    )
                    for s in local_shapes
                ]
                + [whole(state)] * count,
                out_specs=[spec] * sides,
                scratch_shapes=[pltpu.VMEM(state, BF16)],
            ),
            out_shape=[shape_of(count, tokens, value_width)] * sides,
            compiler_params=params(),
            name="outputs",
        )(scalars, *relaid, numerators, stats, *entering[first : first + count])

    keep, send = outputs(0, 1, 0, 2)
    swapped = swap_cores(send)
    numerators, swapped = lax.optimization_barrier((numerators, swapped))
    [send] = outputs(1, group - 1, 1, 1)
    numerators, _ = lax.optimization_barrier((numerators, send))
    [keep_far] = outputs(1, group - 1, 0, 1)
    kept, received = [keep, keep_far], [swapped, swap_cores(send)]
    return pl.pallas_call(
        functools.partial(merge_kernel, heads),
        in_specs=[SMEM] + [whole(x.shape) for x in kept + received],
        out_specs=whole(value_vectors.shape),
        out_shape=shape_of(*value_vectors.shape),
        compiler_params=params(),
        name="merge",
    )(scalars, *kept, *received)


def solution(mesh):
    return jax.shard_map(
        functools.partial(local, mesh.size),
        mesh=mesh,
        in_specs=(
            P(AXES, None, None),
            P(AXES, None, None),
            P(AXES, None, None),
            P(AXES, None),
            P(AXES, None),
            P("ctx"),
        ),
        out_specs=P(AXES, None, None),
        check_vma=False,
    )
```

```python
import functools

import jax
import jax.numpy as jnp
from jax import lax
from jax.experimental import pallas as pl
from jax.experimental.pallas import tpu as pltpu
from jax.sharding import PartitionSpec as P

AXES = ("ctx", "hv")
FLOOR_NEG = -1e30
META = 16
LANES = 128
LAY = 256
F32, BF16 = jnp.float32, jnp.bfloat16

NN = (((1,), (0,)), ((), ()))
NT = (((1,), (1,)), ((), ()))


def dot(a, b, dims=NN):
    return lax.dot_general(a, b, dims, preferred_element_type=F32)


def split3(x):
    hi = x.astype(BF16).astype(F32)
    mid = (x - hi).astype(BF16).astype(F32)
    return hi, mid, (x - hi - mid).astype(BF16).astype(F32)


def iota(shape, dim):
    return lax.broadcasted_iota(jnp.int32, shape, dim)


def meta_rows(normalizer, top, decay, doc, width):
    used = normalizer.shape[1]
    row = iota((META, used), 0)
    rows = jnp.where(row == 6, wide(doc, used), 0.0)
    lines = split3(normalizer) + split3(jnp.concatenate([top, decay], axis=1))
    for index, line in enumerate(lines):
        rows = jnp.where(row == index, line, rows)
    spare = jnp.zeros((META, width - used), F32)
    return jnp.concatenate([rows, spare], axis=1).astype(BF16)


def read_meta(refs):
    key_width = refs[0].shape[0] - META
    rows = [ref[key_width:, : 2 * LANES].astype(F32) for ref in refs]
    normals = jnp.concatenate([(x[2:3] + x[1:2]) + x[0:1] for x in rows], axis=0)
    line = jnp.concatenate([(x[5:6] + x[4:5]) + x[3:4] for x in rows], axis=0)
    docs = jnp.concatenate([x[6:7, :LANES] for x in rows], axis=0)
    return normals, line[:, :LANES], line[:, LANES:], docs


def wide(x, width):
    return jnp.concatenate([x] * (width // LANES), axis=1)


CHUNK = 32


def weighted(refs, outs, coefs):
    key_width, width = refs[0].shape[0] - META, refs[0].shape[1]
    coefs = [[None if c is None else wide(c, width) for c in line] for line in coefs]
    for start in range(0, key_width, CHUNK):
        rows = slice(start, start + CHUNK)
        parts = [ref[rows, :].astype(F32) for ref in refs]
        for out, line in zip(outs, coefs, strict=True):
            terms = [c * part for c, part in zip(line, parts, strict=True) if c is not None]
            out[rows, :] = functools.reduce(jnp.add, terms).astype(BF16)


def gate_rows(core, own_ref, other_ref, heads):
    own, other = own_ref[...].astype(F32), other_ref[...].astype(F32)
    both = jnp.concatenate(
        [jnp.where(core == 0, own, other), jnp.where(core == 0, other, own)], axis=1
    )
    gate_in, forget = both[:heads], both[heads:]
    log_forget = jnp.minimum(forget, 0.0) - jnp.log1p(jnp.exp(-jnp.abs(forget)))
    length = both.shape[1]
    upto = (iota((length, length), 0) <= iota((length, length), 1)).astype(BF16)
    pieces = dot(jnp.concatenate(split3(log_forget), axis=0).astype(BF16), upto)
    decay = (pieces[2 * heads :] + pieces[heads : 2 * heads]) + pieces[:heads]
    return gate_in, decay


def by_head_order(heads):
    n = LAY // heads
    out, inside = iota((LAY, LAY), 0), iota((LAY, LAY), 1)
    return ((inside % heads == out // n) & (inside // heads == out % n)).astype(BF16)


def relayout_kernel(half, count, scalars, *refs):
    sources, outs = refs[:count], refs[count:]
    heads = 2 * half
    n = LAY // heads
    core = scalars[1]
    order = by_head_order(heads)
    for index, source in enumerate(sources):
        keep, send = outs[index], outs[count + index]
        tokens, _, width = source.shape
        for g in range(tokens // n):
            span = slice(g * n, (g + 1) * n)
            rows = dot(order, source[span].reshape(LAY, width)).astype(BF16)
            rows = rows.reshape(heads, n, width)
            keep[:, span, :] = jnp.where(core == 0, rows[:half], rows[half:])
            send[:, span, :] = jnp.where(core == 0, rows[half:], rows[:half])


def gates_kernel(heads, scalars, g_own, g_oth, ids_ref, *outs):
    factors, tops, decays, source_rows, decay_rows, columns = outs
    core = scalars[1]
    length = ids_ref.shape[1]
    gate_in, decay = gate_rows(core, g_own, g_oth, heads)
    ids = ids_ref[...]
    exponent = decay[:, length - 1 :] - decay + gate_in
    exponent = jnp.where(ids == ids[:, length - 1 :], exponent, FLOOR_NEG)
    top = jnp.max(exponent, axis=1, keepdims=True)
    factors[...] = jnp.exp(exponent - top)
    tops[...] = jnp.broadcast_to(top, tops.shape)
    decays[...] = jnp.broadcast_to(decay[:, length - 1 :], decays.shape)
    source_rows[...] = gate_in - decay
    decay_rows[...] = decay
    docs = ids.astype(F32) + 1.0
    filler = jnp.zeros((LANES - heads - 1, length), F32)
    columns[...] = jnp.concatenate([decay, docs, filler], axis=0).T


def state_kernel(heads, scalars, *refs):
    k_own, v_own, k_oth, v_oth, factors, tops, decays, ids_ref = refs[:8]
    outs = refs[8:]
    mine, core = scalars[0], scalars[1]
    tokens, key_width = k_own.shape[1:]
    length = 2 * tokens
    doc = jnp.broadcast_to(ids_ref[:, length - 1 :].astype(F32) + 1.0, (1, LANES))
    for slot in range(len(outs) - 1, -1, -1):
        out = outs[slot]
        local_head = jnp.bitwise_xor(mine, slot)
        head = (heads // 2) * core + local_head
        row = factors[pl.ds(head, 1), :]
        first, last = row[:, :tokens], row[:, tokens:]
        high, low, values, normal = [], [], [], None
        for k_ref, v_ref, f in (
            (k_own, v_own, jnp.where(core == 0, first, last)),
            (k_oth, v_oth, jnp.where(core == 0, last, first)),
        ):
            keys = k_ref[local_head]
            scaled = keys.astype(F32).T * f
            high.append(scaled.astype(BF16))
            low.append((scaled - high[-1].astype(F32)).astype(BF16))
            values.append(v_ref[local_head])
            pieces = jnp.concatenate(split3(f) + (jnp.zeros((META - 3, tokens), F32),), axis=0)
            sums = dot(pieces.astype(BF16), keys)
            line = (sums[2:3] + sums[1:2]) + sums[0:1]
            normal = line if normal is None else normal + line
        total = dot(jnp.concatenate(low + high, axis=1), jnp.concatenate(values * 2, axis=0))
        out[:key_width, :] = total.astype(BF16)
        out[key_width:, :] = meta_rows(
            normal, tops[pl.ds(head, 1), :], decays[pl.ds(head, 1), :], doc, out.shape[1]
        )


def decay_before(mine, place, decays):
    group = decays.shape[0]
    before = jnp.zeros_like(decays)
    for i in range(group):
        before = before + jnp.where(place > jnp.bitwise_xor(mine, i), decays[i : i + 1], 0.0)
    return before


def total_kernel(group, scalars, *refs):
    states, out = refs[:group], refs[group]
    mine = scalars[0]
    key_width, width = out.shape[0] - META, out.shape[1]
    normals, tops, decays, docs = read_meta(states)
    place = jnp.bitwise_xor(iota((group, LANES), 0), mine)
    whole_decay = jnp.sum(decays, axis=0, keepdims=True)
    after = whole_decay - decay_before(mine, place, decays) - decays
    doc = jnp.sum(jnp.where(place == group - 1, docs, 0.0), axis=0, keepdims=True)
    alive = docs == doc
    reached = jnp.where(alive, tops + after, FLOOR_NEG)
    top = jnp.max(reached, axis=0, keepdims=True)
    coefs = jnp.where(alive, jnp.exp(reached - top), 0.0)
    weighted(states, [out], [[coefs[i : i + 1] for i in range(group)]])
    normal = jnp.sum(wide(coefs, key_width) * normals, axis=0, keepdims=True)
    out[key_width:, :] = meta_rows(normal, top, whole_decay, doc, width)


def entering_kernel(group, reach, scalars, *refs):
    states, totals, outs = refs[:group], refs[group : group + reach], refs[group + reach :]
    mine = scalars[0]
    key_width, width = outs[0].shape[0] - META, outs[0].shape[1]
    normals, tops, decays, docs = read_meta(states)
    far_normals, far_tops, far_decays, far_docs = read_meta(totals)
    place = jnp.bitwise_xor(iota((group, LANES), 0), mine)
    before = decay_before(mine, place, decays)
    zero = jnp.zeros((1, LANES), F32)
    far_reached, passed, lines = [], zero, []
    for d in range(reach):
        far_reached.append(far_tops[d : d + 1] + passed)
        passed = passed + far_decays[d : d + 1]
    far_reached = jnp.concatenate(far_reached, axis=0)
    for r in range(group):
        here = jnp.bitwise_xor(mine, r)
        doc = jnp.sum(jnp.where(place == here - 1, docs, 0.0), axis=0, keepdims=True)
        doc = jnp.where(here == 0, far_docs[0:1], doc)
        mark = before[r : r + 1]
        alive = (place < here) & (docs == doc)
        reached = jnp.where(alive, tops + (mark - before - decays), FLOOR_NEG)
        far_alive = (far_docs == doc) & (far_docs > 0.5)
        far = jnp.where(far_alive, far_reached + mark, FLOOR_NEG)
        top = jnp.maximum(
            jnp.max(reached, axis=0, keepdims=True), jnp.max(far, axis=0, keepdims=True)
        )
        coefs = jnp.where(alive, jnp.exp(reached - top), 0.0)
        far_coefs = jnp.where(far_alive, jnp.exp(far - top), 0.0)
        lines.append(
            [None if i == r else coefs[i : i + 1] for i in range(group)]
            + [far_coefs[d : d + 1] for d in range(reach)]
        )
        normal = jnp.sum(wide(coefs, key_width) * normals, axis=0, keepdims=True)
        normal = normal + jnp.sum(wide(far_coefs, key_width) * far_normals, axis=0, keepdims=True)
        outs[r][key_width:, :] = meta_rows(normal, top, zero, doc, width)
    weighted(list(states) + list(totals), outs, lines)


def local_kernel(heads, scalars, *refs):
    q_own, k_own, v_own, q_oth, k_oth, v_oth, source_rows, decay_rows, columns, ids_ref = refs[:10]
    numerators, stats = refs[10:]
    step = pl.program_id(0)
    mine, core = scalars[0], scalars[1]
    tokens, key_width = q_own.shape[1:]
    length = 2 * tokens
    scaling = key_width**-0.5
    head = (heads // 2) * core + jnp.bitwise_xor(mine, step)
    is_first = core == 0
    source = source_rows[pl.ds(head, 1), :]
    lane = iota((length, LANES), 1)
    turned = columns[...]
    decay = jnp.sum(jnp.where(lane == head, turned, 0.0), axis=1, keepdims=True)
    docs = turned[:, heads : heads + 1]
    source_docs = ids_ref[...].astype(F32) + 1.0
    causal = iota((tokens, tokens), 0) >= iota((tokens, tokens), 1)

    def ordered(own, other):
        own, other = own[0], other[0]
        return jnp.where(is_first, own, other), jnp.where(is_first, other, own)

    queries, keys, values = ordered(q_own, q_oth), ordered(k_own, k_oth), ordered(v_own, v_oth)
    for block in range(2):
        rows = slice(block * tokens, (block + 1) * tokens)
        exponents = []
        for s in range(block + 1):
            cols = slice(s * tokens, (s + 1) * tokens)
            allowed = docs[rows] == source_docs[:, cols]
            if s == block:
                allowed = allowed & causal
            exponents.append(jnp.where(allowed, decay[rows] + source[:, cols], FLOOR_NEG))
        stabilizer = functools.reduce(
            jnp.maximum, [jnp.max(x, axis=1, keepdims=True) for x in exponents]
        )
        factors, sources, denominator = [], [], None
        for s in range(block + 1):
            weights = dot(queries[block], keys[s], NT) * scaling
            weights = weights * jnp.exp(exponents[s] - stabilizer)
            high = weights.astype(BF16)
            factors.append(high)
            sources.append(values[s])
            if s < block:
                factors.append((weights - high.astype(F32)).astype(BF16))
                sources.append(values[s])
            part = jnp.sum(weights, axis=1, keepdims=True)
            denominator = part if s == 0 else denominator + part
        numerator = dot(jnp.concatenate(factors, axis=1), jnp.concatenate(sources, axis=0))
        side = core if block == 0 else 1 - core
        numerators[0, side] = numerator
        lane = iota((tokens, LANES), 1)
        pair = jnp.where(lane == 0, stabilizer, denominator).T
        stats[0, side] = jnp.concatenate(
            [pair[:2], decay_rows[pl.ds(head, 1), rows], source_docs[:, rows], pair[4:8]], axis=0
        )


def output_kernel(first, count, scalars, q_own, q_oth, numerators, stats, *refs):
    entering, (keep, send) = refs[:count], refs[count:]
    key_width = q_own.shape[2]
    scaling = key_width**-0.5
    for i, payload in enumerate(entering):
        at = first + i
        local_head = jnp.bitwise_xor(scalars[0], first + i)
        normal, top, _, doc = read_meta([payload])
        pieces = split3(normal) + (jnp.zeros((META - 3, key_width), F32),)
        pieces = jnp.concatenate(pieces, axis=0).astype(BF16)
        memory = payload[:key_width, :]
        width = memory.shape[1]
        for side, (q_ref, out) in enumerate(((q_own, keep), (q_oth, send))):
            query = q_ref[local_head]
            tokens = query.shape[0]
            stat = stats[at, side]
            local = stat[0:1]
            alive = stat[3:4] == wide(doc, tokens)
            carried = jnp.where(alive, stat[2:3] + wide(top, tokens), FLOOR_NEG)
            stabilizer = jnp.maximum(local, carried)
            shrink = jnp.exp(local - stabilizer)
            retained = jnp.exp(carried - stabilizer) * scaling
            seen = dot(pieces, query, NT)
            seen = (seen[2:3] + seen[1:2]) + seen[0:1]
            denominator = shrink * stat[1:2] + retained * seen
            inverse = 1.0 / jnp.maximum(jnp.abs(denominator), 1.0)
            near = jnp.broadcast_to(shrink * inverse, (LANES, tokens)).T
            far = jnp.broadcast_to(retained * inverse, (LANES, tokens)).T
            result = wide(near, width) * numerators[at, side]
            out[i] = (result + wide(far, width) * dot(query, memory)).astype(BF16)


def merge_kernel(heads, scalars, *refs):
    stacks, out = refs[:-1], refs[-1]
    half = heads // 2
    n = LAY // heads
    mine, core = scalars[0], scalars[1]
    into, given = iota((LAY, LAY), 0), iota((LAY, LAY), 1)
    index = given // n
    slot = jnp.bitwise_and(index, half - 1)
    side = jnp.where(index < half, core, 1 - core)
    head = side * half + jnp.bitwise_xor(slot, mine)
    order = ((into % heads == head) & (into // heads == given % n)).astype(BF16)
    _, tokens, width = stacks[0].shape
    for g in range(tokens // n):
        span = slice(g * n, (g + 1) * n)
        rows = jnp.concatenate([stack[:, span, :] for stack in stacks], axis=0)
        turned = dot(order, rows.reshape(LAY, width))
        out[span] = turned.reshape(n, heads, width).astype(BF16)


def whole(shape):
    return pl.BlockSpec(shape, lambda *_: (0,) * len(shape))


def params():
    return pltpu.CompilerParams(vmem_limit_bytes=56 * 2**20)


SMEM = pl.BlockSpec(memory_space=pltpu.SMEM)


def shape_of(*dims, dtype=BF16):
    return jax.ShapeDtypeStruct(dims, dtype)


def local(devices, queries, key_vectors, value_vectors, input_gate, forget_gate, doc_ids):
    tokens, heads, key_width = queries.shape
    value_width = value_vectors.shape[2]
    half = heads // 2
    group = half
    chips = devices // 2
    levels = chips // group
    reach = max(1, levels // 2)
    ctx, hv = lax.axis_index("ctx"), lax.axis_index("hv")
    chip = ctx * (lax.axis_size("hv") // 2) + hv // 2
    scalars = jnp.stack([chip % group, hv % 2]).astype(jnp.int32)
    ids = lax.dynamic_slice(doc_ids, ((hv // 2) * 2 * tokens,), (2 * tokens,))[None, :]

    def swap_cores(x):
        return lax.ppermute(x, AXES, [(d, d ^ 1) for d in range(devices)])

    def in_group(x, r):
        pairs = [(d, d ^ (2 * r)) for d in range(devices)]
        return lax.ppermute(x, AXES, pairs)

    def to_next(x):
        jump = 2 * group
        return lax.ppermute(x, AXES, [(d, d + jump) for d in range(devices - jump)])

    rows = key_width + META
    state = (rows, value_width)
    sizes = {key_width: (half, tokens, key_width), value_width: (half, tokens, value_width)}

    def relayout(*sources):
        outs = [sizes[x.shape[2]] for x in sources] * 2
        return pl.pallas_call(
            functools.partial(relayout_kernel, half, len(sources)),
            in_specs=[SMEM] + [whole(x.shape) for x in sources],
            out_specs=[whole(s) for s in outs],
            out_shape=[shape_of(*s) for s in outs],
            compiler_params=params(),
            name="relayout",
        )(scalars, *sources)

    gates = jnp.concatenate([input_gate.T, forget_gate.T], axis=0)
    gates, key_vectors = lax.optimization_barrier((gates, key_vectors))
    gates_oth = swap_cores(gates)
    k_keep, v_keep, k_send, v_send = relayout(key_vectors, value_vectors)
    gates_oth, k_send, v_send = lax.optimization_barrier((gates_oth, k_send, v_send))
    k_oth = swap_cores(k_send)
    v_oth = swap_cores(v_send)
    gate_shapes = [
        (heads, 2 * tokens),
        (heads, LANES),
        (heads, LANES),
        (heads, 2 * tokens),
        (heads, 2 * tokens),
        (2 * tokens, LANES),
    ]
    factors, tops, decays, source_rows, decay_rows, columns = pl.pallas_call(
        functools.partial(gates_kernel, heads),
        in_specs=[SMEM] + [whole(gates.shape)] * 2 + [whole(ids.shape)],
        out_specs=[whole(s) for s in gate_shapes],
        out_shape=[shape_of(*s, dtype=F32) for s in gate_shapes],
        compiler_params=params(),
        name="gates",
    )(scalars, gates, gates_oth, ids)

    def by_slot(x):
        return pl.BlockSpec((1,) + x.shape[1:], lambda i, s: (jnp.bitwise_xor(s[0], i), 0, 0))

    by_core = (k_keep, v_keep, k_oth, v_oth, factors, tops, decays, ids)
    made = pl.pallas_call(
        functools.partial(state_kernel, heads),
        in_specs=[SMEM] + [whole(x.shape) for x in by_core],
        out_specs=[whole(state)] * group,
        out_shape=[shape_of(*state)] * group,
        compiler_params=params(),
        name="states",
    )(scalars, *by_core)
    gathered = [made[0]] + [in_group(made[r], r) for r in range(1, group)]
    total = pl.pallas_call(
        functools.partial(total_kernel, group),
        in_specs=[SMEM] + [whole(state)] * group,
        out_specs=whole(state),
        out_shape=shape_of(*state),
        compiler_params=params(),
        name="group_total",
    )(scalars, *gathered)
    totals = [to_next(total)]
    while len(totals) < reach:
        totals.append(to_next(totals[-1]))

    queries, gathered[0] = lax.optimization_barrier((queries, gathered[0]))
    q_keep, q_send = relayout(queries)
    q_oth = swap_cores(q_send)
    by_head = (q_keep, k_keep, v_keep, q_oth, k_oth, v_oth)
    small = (source_rows, decay_rows, columns, ids)
    local_shapes = [(half, 2, tokens, value_width), (half, 2, 8, tokens)]
    numerators, stats = pl.pallas_call(
        functools.partial(local_kernel, heads),
        grid_spec=pltpu.PrefetchScalarGridSpec(
            num_scalar_prefetch=1,
            grid=(group,),
            in_specs=[by_slot(x) for x in by_head] + [whole(x.shape) for x in small],
            out_specs=[
                pl.BlockSpec((1,) + s[1:], lambda i, _: (i, 0, 0, 0)) for s in local_shapes
            ],
        ),
        out_shape=[shape_of(*s, dtype=F32) for s in local_shapes],
        compiler_params=params(),
        name="own_terms",
    )(scalars, *by_head, *small)
    gathered[0], numerators = lax.optimization_barrier((gathered[0], numerators))

    leaving = pl.pallas_call(
        functools.partial(entering_kernel, group, reach),
        in_specs=[SMEM] + [whole(state)] * (group + reach),
        out_specs=[whole(state)] * group,
        out_shape=[shape_of(*state)] * group,
        compiler_params=params(),
        name="entering",
    )(scalars, *gathered, *totals)
    entering = [leaving[0]] + [in_group(leaving[r], r) for r in range(1, group)]

    def outputs(first, count):
        return pl.pallas_call(
            functools.partial(output_kernel, first, count),
            in_specs=[SMEM, whole(q_keep.shape), whole(q_oth.shape)]
            + [whole(x) for x in local_shapes]
            + [whole(state)] * count,
            out_specs=[whole((count, tokens, value_width))] * 2,
            out_shape=[shape_of(count, tokens, value_width)] * 2,
            compiler_params=params(),
            name="outputs",
        )(scalars, q_keep, q_oth, numerators, stats, *entering[first : first + count])

    keep, send = outputs(0, 1)
    swapped = swap_cores(send)
    numerators, swapped = lax.optimization_barrier((numerators, swapped))
    keep_far, send = outputs(1, group - 1)
    kept, received = [keep, keep_far], [swapped, swap_cores(send)]
    return pl.pallas_call(
        functools.partial(merge_kernel, heads),
        in_specs=[SMEM] + [whole(x.shape) for x in kept + received],
        out_specs=whole(value_vectors.shape),
        out_shape=shape_of(*value_vectors.shape),
        compiler_params=params(),
        name="merge",
    )(scalars, *kept, *received)


def solution(mesh):
    return jax.shard_map(
        functools.partial(local, mesh.size),
        mesh=mesh,
        in_specs=(
            P(AXES, None, None),
            P(AXES, None, None),
            P(AXES, None, None),
            P(AXES, None),
            P(AXES, None),
            P("ctx"),
        ),
        out_specs=P(AXES, None, None),
        check_vma=False,
    )
```

```python
import functools

import jax
import jax.numpy as jnp
from jax import lax
from jax.experimental import pallas as pl
from jax.experimental.pallas import tpu as pltpu
from jax.sharding import PartitionSpec as P

AXES = ("ctx", "hv")
FLOOR_NEG = -1e30
META = 16
LANES = 128
LAY = 256
F32, BF16 = jnp.float32, jnp.bfloat16

NN = (((1,), (0,)), ((), ()))
NT = (((1,), (1,)), ((), ()))


def dot(a, b, dims=NN):
    return lax.dot_general(a, b, dims, preferred_element_type=F32)


def split3(x):
    hi = x.astype(BF16).astype(F32)
    mid = (x - hi).astype(BF16).astype(F32)
    return hi, mid, (x - hi - mid).astype(BF16).astype(F32)


def iota(shape, dim):
    return lax.broadcasted_iota(jnp.int32, shape, dim)


def meta_rows(normalizer, top, decay, doc, width):
    used = normalizer.shape[1]
    row = iota((META, used), 0)
    rows = jnp.where(row == 6, wide(doc, used), 0.0)
    lines = split3(normalizer) + split3(jnp.concatenate([top, decay], axis=1))
    for index, line in enumerate(lines):
        rows = jnp.where(row == index, line, rows)
    spare = jnp.zeros((META, width - used), F32)
    return jnp.concatenate([rows, spare], axis=1).astype(BF16)


def read_meta(refs):
    key_width = refs[0].shape[0] - META
    rows = [ref[key_width:, : 2 * LANES].astype(F32) for ref in refs]
    normals = jnp.concatenate([(x[2:3] + x[1:2]) + x[0:1] for x in rows], axis=0)
    line = jnp.concatenate([(x[5:6] + x[4:5]) + x[3:4] for x in rows], axis=0)
    docs = jnp.concatenate([x[6:7, :LANES] for x in rows], axis=0)
    return normals, line[:, :LANES], line[:, LANES:], docs


def wide(x, width):
    return jnp.concatenate([x] * (width // LANES), axis=1)


CHUNK = 32


def weighted(refs, outs, coefs):
    key_width, width = refs[0].shape[0] - META, refs[0].shape[1]
    coefs = [[None if c is None else wide(c, width) for c in line] for line in coefs]
    for start in range(0, key_width, CHUNK):
        rows = slice(start, start + CHUNK)
        parts = [ref[rows, :].astype(F32) for ref in refs]
        for out, line in zip(outs, coefs, strict=True):
            terms = [c * part for c, part in zip(line, parts, strict=True) if c is not None]
            out[rows, :] = functools.reduce(jnp.add, terms).astype(BF16)


def gate_rows(core, own_ref, other_ref, heads):
    own, other = own_ref[...].astype(F32), other_ref[...].astype(F32)
    both = jnp.concatenate(
        [jnp.where(core == 0, own, other), jnp.where(core == 0, other, own)], axis=1
    )
    gate_in, forget = both[:heads], both[heads:]
    log_forget = jnp.minimum(forget, 0.0) - jnp.log1p(jnp.exp(-jnp.abs(forget)))
    length = both.shape[1]
    upto = (iota((length, length), 0) <= iota((length, length), 1)).astype(BF16)
    pieces = dot(jnp.concatenate(split3(log_forget), axis=0).astype(BF16), upto)
    decay = (pieces[2 * heads :] + pieces[heads : 2 * heads]) + pieces[:heads]
    return gate_in, decay


def by_head_order(heads):
    n = LAY // heads
    out, inside = iota((LAY, LAY), 0), iota((LAY, LAY), 1)
    return ((inside % heads == out // n) & (inside // heads == out % n)).astype(BF16)


def relayout_kernel(half, count, *refs):
    sources, outs = refs[:count], refs[count:]
    heads = 2 * half
    n = LAY // heads
    core = lax.axis_index("hv") % 2
    order = by_head_order(heads)
    for index, source in enumerate(sources):
        keep, send = outs[index], outs[count + index]
        tokens, _, width = source.shape
        for g in range(tokens // n):
            span = slice(g * n, (g + 1) * n)
            rows = dot(order, source[span].reshape(LAY, width)).astype(BF16)
            rows = rows.reshape(heads, n, width)
            keep[:, span, :] = jnp.where(core == 0, rows[:half], rows[half:])
            send[:, span, :] = jnp.where(core == 0, rows[half:], rows[:half])


def gates_kernel(heads, scalars, g_own, g_oth, ids_ref, *outs):
    factors, tops, decays, source_rows, decay_rows, columns = outs
    core = scalars[1]
    length = ids_ref.shape[1]
    gate_in, decay = gate_rows(core, g_own, g_oth, heads)
    ids = ids_ref[...]
    exponent = decay[:, length - 1 :] - decay + gate_in
    exponent = jnp.where(ids == ids[:, length - 1 :], exponent, FLOOR_NEG)
    top = jnp.max(exponent, axis=1, keepdims=True)
    factors[...] = jnp.exp(exponent - top)
    tops[...] = jnp.broadcast_to(top, tops.shape)
    decays[...] = jnp.broadcast_to(decay[:, length - 1 :], decays.shape)
    source_rows[...] = gate_in - decay
    decay_rows[...] = decay
    docs = ids.astype(F32) + 1.0
    filler = jnp.zeros((LANES - heads - 1, length), F32)
    columns[...] = jnp.concatenate([decay, docs, filler], axis=0).T


def state_kernel(heads, scalars, *refs):
    k_own, v_own, k_oth, v_oth, factors, tops, decays, ids_ref = refs[:8]
    outs = refs[8:]
    mine, core = scalars[0], scalars[1]
    tokens, key_width = k_own.shape[1:]
    length = 2 * tokens
    doc = jnp.broadcast_to(ids_ref[:, length - 1 :].astype(F32) + 1.0, (1, LANES))
    for slot in range(len(outs) - 1, -1, -1):
        out = outs[slot]
        local_head = jnp.bitwise_xor(mine, slot)
        head = (heads // 2) * core + local_head
        row = factors[pl.ds(head, 1), :]
        first, last = row[:, :tokens], row[:, tokens:]
        high, low, values, normal = [], [], [], None
        for k_ref, v_ref, f in (
            (k_own, v_own, jnp.where(core == 0, first, last)),
            (k_oth, v_oth, jnp.where(core == 0, last, first)),
        ):
            keys = k_ref[local_head]
            scaled = keys.astype(F32).T * f
            high.append(scaled.astype(BF16))
            low.append((scaled - high[-1].astype(F32)).astype(BF16))
            values.append(v_ref[local_head])
            pieces = jnp.concatenate(split3(f) + (jnp.zeros((META - 3, tokens), F32),), axis=0)
            sums = dot(pieces.astype(BF16), keys)
            line = (sums[2:3] + sums[1:2]) + sums[0:1]
            normal = line if normal is None else normal + line
        total = dot(jnp.concatenate(low + high, axis=1), jnp.concatenate(values * 2, axis=0))
        out[:key_width, :] = total.astype(BF16)
        out[key_width:, :] = meta_rows(
            normal, tops[pl.ds(head, 1), :], decays[pl.ds(head, 1), :], doc, out.shape[1]
        )


def decay_before(mine, place, decays):
    group = decays.shape[0]
    before = jnp.zeros_like(decays)
    for i in range(group):
        before = before + jnp.where(place > jnp.bitwise_xor(mine, i), decays[i : i + 1], 0.0)
    return before


def total_kernel(group, scalars, *refs):
    states, out = refs[:group], refs[group]
    mine = scalars[0]
    key_width, width = out.shape[0] - META, out.shape[1]
    normals, tops, decays, docs = read_meta(states)
    place = jnp.bitwise_xor(iota((group, LANES), 0), mine)
    whole_decay = jnp.sum(decays, axis=0, keepdims=True)
    after = whole_decay - decay_before(mine, place, decays) - decays
    doc = jnp.sum(jnp.where(place == group - 1, docs, 0.0), axis=0, keepdims=True)
    alive = docs == doc
    reached = jnp.where(alive, tops + after, FLOOR_NEG)
    top = jnp.max(reached, axis=0, keepdims=True)
    coefs = jnp.where(alive, jnp.exp(reached - top), 0.0)
    weighted(states, [out], [[coefs[i : i + 1] for i in range(group)]])
    normal = jnp.sum(wide(coefs, key_width) * normals, axis=0, keepdims=True)
    out[key_width:, :] = meta_rows(normal, top, whole_decay, doc, width)


def entering_kernel(group, reach, scalars, *refs):
    states, totals, outs = refs[:group], refs[group : group + reach], refs[group + reach :]
    mine = scalars[0]
    key_width, width = outs[0].shape[0] - META, outs[0].shape[1]
    normals, tops, decays, docs = read_meta(states)
    far_normals, far_tops, far_decays, far_docs = read_meta(totals)
    place = jnp.bitwise_xor(iota((group, LANES), 0), mine)
    before = decay_before(mine, place, decays)
    zero = jnp.zeros((1, LANES), F32)
    far_reached, passed, lines = [], zero, []
    for d in range(reach):
        far_reached.append(far_tops[d : d + 1] + passed)
        passed = passed + far_decays[d : d + 1]
    far_reached = jnp.concatenate(far_reached, axis=0)
    for r in range(group):
        here = jnp.bitwise_xor(mine, r)
        doc = jnp.sum(jnp.where(place == here - 1, docs, 0.0), axis=0, keepdims=True)
        doc = jnp.where(here == 0, far_docs[0:1], doc)
        mark = before[r : r + 1]
        alive = (place < here) & (docs == doc)
        reached = jnp.where(alive, tops + (mark - before - decays), FLOOR_NEG)
        far_alive = (far_docs == doc) & (far_docs > 0.5)
        far = jnp.where(far_alive, far_reached + mark, FLOOR_NEG)
        top = jnp.maximum(
            jnp.max(reached, axis=0, keepdims=True), jnp.max(far, axis=0, keepdims=True)
        )
        coefs = jnp.where(alive, jnp.exp(reached - top), 0.0)
        far_coefs = jnp.where(far_alive, jnp.exp(far - top), 0.0)
        lines.append(
            [None if i == r else coefs[i : i + 1] for i in range(group)]
            + [far_coefs[d : d + 1] for d in range(reach)]
        )
        normal = jnp.sum(wide(coefs, key_width) * normals, axis=0, keepdims=True)
        normal = normal + jnp.sum(wide(far_coefs, key_width) * far_normals, axis=0, keepdims=True)
        outs[r][key_width:, :] = meta_rows(normal, top, zero, doc, width)
    weighted(list(states) + list(totals), outs, lines)


def local_kernel(first_slot, heads, scalars, *refs):
    q_own, k_own, v_own, q_oth, k_oth, v_oth, source_rows, decay_rows, columns, ids_ref = refs[:10]
    numerators, stats = refs[-2:]
    step = pl.program_id(0)
    mine, core = scalars[0], scalars[1]
    tokens, key_width = q_own.shape[1:]
    length = 2 * tokens
    scaling = key_width**-0.5
    head = (heads // 2) * core + jnp.bitwise_xor(mine, first_slot + step)
    is_first = core == 0
    source = source_rows[pl.ds(head, 1), :]
    lane = iota((length, LANES), 1)
    turned = columns[...]
    decay = jnp.sum(jnp.where(lane == head, turned, 0.0), axis=1, keepdims=True)
    docs = turned[:, heads : heads + 1]
    source_docs = ids_ref[...].astype(F32) + 1.0
    causal = iota((tokens, tokens), 0) >= iota((tokens, tokens), 1)

    def ordered(own, other):
        own, other = own[0], other[0]
        return jnp.where(is_first, own, other), jnp.where(is_first, other, own)

    queries, keys, values = ordered(q_own, q_oth), ordered(k_own, k_oth), ordered(v_own, v_oth)
    for block in range(2):
        rows = slice(block * tokens, (block + 1) * tokens)
        exponents = []
        for s in range(block + 1):
            cols = slice(s * tokens, (s + 1) * tokens)
            allowed = docs[rows] == source_docs[:, cols]
            if s == block:
                allowed = allowed & causal
            exponents.append(jnp.where(allowed, decay[rows] + source[:, cols], FLOOR_NEG))
        stabilizer = functools.reduce(
            jnp.maximum, [jnp.max(x, axis=1, keepdims=True) for x in exponents]
        )
        factors, sources, denominator = [], [], None
        for s in range(block + 1):
            weights = dot(queries[block], keys[s], NT) * scaling
            weights = weights * jnp.exp(exponents[s] - stabilizer)
            high = weights.astype(BF16)
            factors.append(high)
            sources.append(values[s])
            if s < block:
                factors.append((weights - high.astype(F32)).astype(BF16))
                sources.append(values[s])
            part = jnp.sum(weights, axis=1, keepdims=True)
            denominator = part if s == 0 else denominator + part
        numerator = dot(jnp.concatenate(factors, axis=1), jnp.concatenate(sources, axis=0))
        side = core if block == 0 else 1 - core
        numerators[0, side] = numerator
        lane = iota((tokens, LANES), 1)
        pair = jnp.where(lane == 0, stabilizer, denominator).T
        stats[0, side] = jnp.concatenate(
            [pair[:2], decay_rows[pl.ds(head, 1), rows], source_docs[:, rows], pair[4:8]], axis=0
        )


def output_kernel(first, count, scalars, q_own, q_oth, numerators, stats, *refs):
    entering, (keep, send, near_terms, queries, landed) = refs[:count], refs[count:]
    key_width = q_own.shape[2]
    scaling = key_width**-0.5
    copies = []
    for i in range(count):
        local_head = jnp.bitwise_xor(scalars[0], first + i)
        moves = [
            (q_own.at[local_head], queries.at[i, 0]),
            (q_oth.at[local_head], queries.at[i, 1]),
            (numerators.at[first + i], near_terms.at[i]),
        ]
        copies.append(
            [pltpu.make_async_copy(x, y, landed.at[i, n]) for n, (x, y) in enumerate(moves)]
        )
        for copy in copies[-1]:
            copy.start()
    for i, payload in enumerate(entering):
        at = first + i
        for copy in copies[i]:
            copy.wait()
        normal, top, _, doc = read_meta([payload])
        pieces = split3(normal) + (jnp.zeros((META - 3, key_width), F32),)
        pieces = jnp.concatenate(pieces, axis=0).astype(BF16)
        memory = payload[:key_width, :]
        width = memory.shape[1]
        for side, out in enumerate((keep, send)):
            query = queries[i, side]
            tokens = query.shape[0]
            stat = stats[at, side]
            local = stat[0:1]
            alive = stat[3:4] == wide(doc, tokens)
            carried = jnp.where(alive, stat[2:3] + wide(top, tokens), FLOOR_NEG)
            stabilizer = jnp.maximum(local, carried)
            shrink = jnp.exp(local - stabilizer)
            retained = jnp.exp(carried - stabilizer) * scaling
            seen = dot(pieces, query, NT)
            seen = (seen[2:3] + seen[1:2]) + seen[0:1]
            denominator = shrink * stat[1:2] + retained * seen
            inverse = 1.0 / jnp.maximum(jnp.abs(denominator), 1.0)
            near = jnp.broadcast_to(shrink * inverse, (LANES, tokens)).T
            far = jnp.broadcast_to(retained * inverse, (LANES, tokens)).T
            result = wide(near, width) * near_terms[i, side]
            out[i] = (result + wide(far, width) * dot(query, memory)).astype(BF16)


def merge_kernel(heads, scalars, *refs):
    stacks, out = refs[:-1], refs[-1]
    half = heads // 2
    n = LAY // heads
    mine, core = scalars[0], scalars[1]
    into, given = iota((LAY, LAY), 0), iota((LAY, LAY), 1)
    index = given // n
    slot = jnp.bitwise_and(index, half - 1)
    side = jnp.where(index < half, core, 1 - core)
    head = side * half + jnp.bitwise_xor(slot, mine)
    order = ((into % heads == head) & (into // heads == given % n)).astype(BF16)
    _, tokens, width = stacks[0].shape
    for g in range(tokens // n):
        span = slice(g * n, (g + 1) * n)
        rows = jnp.concatenate([stack[:, span, :] for stack in stacks], axis=0)
        turned = dot(order, rows.reshape(LAY, width))
        out[span] = turned.reshape(n, heads, width).astype(BF16)


def whole(shape):
    return pl.BlockSpec(shape, lambda *_: (0,) * len(shape))


def params():
    return pltpu.CompilerParams(vmem_limit_bytes=56 * 2**20)


SMEM = pl.BlockSpec(memory_space=pltpu.SMEM)
HERE = pl.BlockSpec(memory_space=pl.ANY)


def shape_of(*dims, dtype=BF16):
    return jax.ShapeDtypeStruct(dims, dtype)


def local(devices, queries, key_vectors, value_vectors, input_gate, forget_gate, doc_ids):
    tokens, heads, key_width = queries.shape
    value_width = value_vectors.shape[2]
    half = heads // 2
    group = half
    chips = devices // 2
    levels = chips // group
    reach = max(1, levels // 2)
    ctx, hv = lax.axis_index("ctx"), lax.axis_index("hv")
    chip = ctx * (lax.axis_size("hv") // 2) + hv // 2
    scalars = jnp.stack([chip % group, hv % 2]).astype(jnp.int32)
    ids = lax.dynamic_slice(doc_ids, ((hv // 2) * 2 * tokens,), (2 * tokens,))[None, :]

    def swap_cores(x):
        return lax.ppermute(x, AXES, [(d, d ^ 1) for d in range(devices)])

    def in_group(x, r):
        pairs = [(d, d ^ (2 * r)) for d in range(devices)]
        return lax.ppermute(x, AXES, pairs)

    def to_next(x):
        jump = 2 * group
        return lax.ppermute(x, AXES, [(d, d + jump) for d in range(devices - jump)])

    rows = key_width + META
    state = (rows, value_width)
    sizes = {key_width: (half, tokens, key_width), value_width: (half, tokens, value_width)}

    def relayout(*sources):
        outs = [sizes[x.shape[2]] for x in sources] * 2
        return pl.pallas_call(
            functools.partial(relayout_kernel, half, len(sources)),
            in_specs=[whole(x.shape) for x in sources],
            out_specs=[whole(s) for s in outs],
            out_shape=[shape_of(*s) for s in outs],
            compiler_params=params(),
                name="relayout",
        )(*sources)

    gates = jnp.concatenate([input_gate.T, forget_gate.T], axis=0)
    gates, key_vectors = lax.optimization_barrier((gates, key_vectors))
    gates_oth = swap_cores(gates)
    k_keep, v_keep, k_send, v_send = relayout(key_vectors, value_vectors)
    gates_oth, k_send, v_send = lax.optimization_barrier((gates_oth, k_send, v_send))
    k_oth = swap_cores(k_send)
    v_oth = swap_cores(v_send)
    gate_shapes = [
        (heads, 2 * tokens),
        (heads, LANES),
        (heads, LANES),
        (heads, 2 * tokens),
        (heads, 2 * tokens),
        (2 * tokens, LANES),
    ]
    factors, tops, decays, source_rows, decay_rows, columns = pl.pallas_call(
        functools.partial(gates_kernel, heads),
        in_specs=[SMEM] + [whole(gates.shape)] * 2 + [whole(ids.shape)],
        out_specs=[whole(s) for s in gate_shapes],
        out_shape=[shape_of(*s, dtype=F32) for s in gate_shapes],
        compiler_params=params(),
        name="gates",
    )(scalars, gates, gates_oth, ids)

    def by_slot(x, first_slot):
        return pl.BlockSpec(
            (1,) + x.shape[1:], lambda i, s: (jnp.bitwise_xor(s[0], first_slot + i), 0, 0)
        )

    by_core = (k_keep, v_keep, k_oth, v_oth, factors, tops, decays, ids)
    made = pl.pallas_call(
        functools.partial(state_kernel, heads),
        in_specs=[SMEM] + [whole(x.shape) for x in by_core],
        out_specs=[whole(state)] * group,
        out_shape=[shape_of(*state)] * group,
        compiler_params=params(),
        name="states",
    )(scalars, *by_core)
    gathered = [made[0]] + [in_group(made[r], r) for r in range(1, group)]
    total = pl.pallas_call(
        functools.partial(total_kernel, group),
        in_specs=[SMEM] + [whole(state)] * group,
        out_specs=whole(state),
        out_shape=shape_of(*state),
        compiler_params=params(),
        name="group_total",
    )(scalars, *gathered)
    queries, gathered[0] = lax.optimization_barrier((queries, gathered[0]))
    q_keep, q_send = relayout(queries)
    q_oth = swap_cores(q_send)
    small = (source_rows, decay_rows, columns, ids)
    local_shapes = [(half, 2, tokens, value_width), (half, 2, 8, tokens)]

    def own_terms(first_slot, count, q_own, into):
        by_head = (q_own, k_keep, v_keep, q_oth, k_oth, v_oth)
        return pl.pallas_call(
            functools.partial(local_kernel, first_slot, heads),
            grid_spec=pltpu.PrefetchScalarGridSpec(
                num_scalar_prefetch=1,
                grid=(count,),
                in_specs=[by_slot(x, first_slot) for x in by_head]
                + [whole(x.shape) for x in small]
                + [HERE] * len(into),
                out_specs=[
                    pl.BlockSpec((1,) + s[1:], lambda i, _: (first_slot + i, 0, 0, 0))
                    for s in local_shapes
                ],
            ),
            out_shape=[shape_of(*s, dtype=F32) for s in local_shapes],
            input_output_aliases={11 + i: i for i in range(len(into))},
            compiler_params=params(),
            name="own_terms",
        )(scalars, *by_head, *small, *into)

    early = half // 2
    q_first, _ = lax.optimization_barrier((q_keep, total))
    terms = own_terms(0, early, q_first, ())
    totals = [to_next(total)]
    totals[0], terms = lax.optimization_barrier((totals[0], terms))
    while len(totals) < reach:
        totals.append(to_next(totals[-1]))
    terms = own_terms(early, half - early, q_keep, terms)
    gathered[0], (numerators, stats) = lax.optimization_barrier((gathered[0], terms))

    leaving = pl.pallas_call(
        functools.partial(entering_kernel, group, reach),
        in_specs=[SMEM] + [whole(state)] * (group + reach),
        out_specs=[whole(state)] * group,
        out_shape=[shape_of(*state)] * group,
        compiler_params=params(),
        name="entering",
    )(scalars, *gathered, *totals)
    entering = [leaving[0]] + [in_group(leaving[r], r) for r in range(1, group)]

    def outputs(first, count):
        return pl.pallas_call(
            functools.partial(output_kernel, first, count),
            in_specs=[SMEM, HERE, HERE, HERE, whole(local_shapes[1])] + [whole(state)] * count,
            out_specs=[whole((count, tokens, value_width))] * 2,
            scratch_shapes=[
                pltpu.VMEM((count, 2, tokens, value_width), F32),
                pltpu.VMEM((count, 2, tokens, key_width), BF16),
                pltpu.SemaphoreType.DMA((count, 3)),
            ],
            out_shape=[shape_of(count, tokens, value_width)] * 2,
            compiler_params=params(),
            name="outputs",
        )(scalars, q_keep, q_oth, numerators, stats, *entering[first : first + count])

    keep, send = outputs(0, 1)
    swapped = swap_cores(send)
    numerators, swapped = lax.optimization_barrier((numerators, swapped))
    keep_far, send = outputs(1, group - 1)
    kept, received = [keep, keep_far], [swapped, swap_cores(send)]
    return pl.pallas_call(
        functools.partial(merge_kernel, heads),
        in_specs=[SMEM] + [whole(x.shape) for x in kept + received],
        out_specs=whole(value_vectors.shape),
        out_shape=shape_of(*value_vectors.shape),
        compiler_params=params(),
        name="merge",
    )(scalars, *kept, *received)


def solution(mesh):
    return jax.shard_map(
        functools.partial(local, mesh.size),
        mesh=mesh,
        in_specs=(
            P(AXES, None, None),
            P(AXES, None, None),
            P(AXES, None, None),
            P(AXES, None),
            P(AXES, None),
            P("ctx"),
        ),
        out_specs=P(AXES, None, None),
        check_vma=False,
    )
```

```python
import functools

import jax
import jax.numpy as jnp
from jax import lax
from jax.experimental import pallas as pl
from jax.experimental.pallas import tpu as pltpu
from jax.sharding import PartitionSpec as P

AXES = ("ctx", "hv")
FLOOR_NEG = -1e30
META = 16
LANES = 128
LAY = 256
F32, BF16 = jnp.float32, jnp.bfloat16

NN = (((1,), (0,)), ((), ()))
NT = (((1,), (1,)), ((), ()))


def dot(a, b, dims=NN):
    return lax.dot_general(a, b, dims, preferred_element_type=F32)


def split3(x):
    hi = x.astype(BF16).astype(F32)
    mid = (x - hi).astype(BF16).astype(F32)
    return hi, mid, (x - hi - mid).astype(BF16).astype(F32)


def iota(shape, dim):
    return lax.broadcasted_iota(jnp.int32, shape, dim)


def meta_rows(normalizer, top, decay, doc, width):
    used = normalizer.shape[1]
    row = iota((META, used), 0)
    rows = jnp.where(row == 6, wide(doc, used), 0.0)
    lines = split3(normalizer) + split3(jnp.concatenate([top, decay], axis=1))
    for index, line in enumerate(lines):
        rows = jnp.where(row == index, line, rows)
    spare = jnp.zeros((META, width - used), F32)
    return jnp.concatenate([rows, spare], axis=1).astype(BF16)


def read_meta(refs):
    key_width = refs[0].shape[0] - META
    rows = [ref[key_width:, : 2 * LANES].astype(F32) for ref in refs]
    normals = jnp.concatenate([(x[2:3] + x[1:2]) + x[0:1] for x in rows], axis=0)
    line = jnp.concatenate([(x[5:6] + x[4:5]) + x[3:4] for x in rows], axis=0)
    docs = jnp.concatenate([x[6:7, :LANES] for x in rows], axis=0)
    return normals, line[:, :LANES], line[:, LANES:], docs


def wide(x, width):
    return jnp.concatenate([x] * (width // LANES), axis=1)


CHUNK = 32


def weighted(refs, outs, coefs):
    key_width, width = refs[0].shape[0] - META, refs[0].shape[1]
    coefs = [[None if c is None else wide(c, width) for c in line] for line in coefs]
    for start in range(0, key_width, CHUNK):
        rows = slice(start, start + CHUNK)
        parts = [ref[rows, :].astype(F32) for ref in refs]
        for out, line in zip(outs, coefs, strict=True):
            terms = [c * part for c, part in zip(line, parts, strict=True) if c is not None]
            out[rows, :] = functools.reduce(jnp.add, terms).astype(BF16)


def gate_rows(core, own_ref, other_ref, heads):
    own, other = own_ref[...].astype(F32), other_ref[...].astype(F32)
    both = jnp.concatenate(
        [jnp.where(core == 0, own, other), jnp.where(core == 0, other, own)], axis=1
    )
    gate_in, forget = both[:heads], both[heads:]
    log_forget = jnp.minimum(forget, 0.0) - jnp.log1p(jnp.exp(-jnp.abs(forget)))
    length = both.shape[1]
    upto = (iota((length, length), 0) <= iota((length, length), 1)).astype(BF16)
    pieces = dot(jnp.concatenate(split3(log_forget), axis=0).astype(BF16), upto)
    decay = (pieces[2 * heads :] + pieces[heads : 2 * heads]) + pieces[:heads]
    return gate_in, decay


def by_head_order(heads):
    n = LAY // heads
    out, inside = iota((LAY, LAY), 0), iota((LAY, LAY), 1)
    return ((inside % heads == out // n) & (inside // heads == out % n)).astype(BF16)


def relayout_kernel(half, count, *refs):
    sources, outs = refs[:count], refs[count:]
    heads = 2 * half
    n = LAY // heads
    core = lax.axis_index("hv") % 2
    order = by_head_order(heads)
    for index, source in enumerate(sources):
        keep, send = outs[index], outs[count + index]
        tokens, _, width = source.shape
        for g in range(tokens // n):
            span = slice(g * n, (g + 1) * n)
            rows = dot(order, source[span].reshape(LAY, width)).astype(BF16)
            rows = rows.reshape(heads, n, width)
            keep[:, span, :] = jnp.where(core == 0, rows[:half], rows[half:])
            send[:, span, :] = jnp.where(core == 0, rows[half:], rows[:half])


def gates_kernel(heads, scalars, g_own, g_oth, ids_ref, *outs):
    factors, tops, decays, source_rows, decay_rows, columns, docs_row = outs
    core = scalars[1]
    length = factors.shape[1]
    gate_in, decay = gate_rows(core, g_own, g_oth, heads)
    chip = lax.axis_index("hv") // 2
    ids = ids_ref[:, pl.ds(pl.multiple_of(chip * length, length), length)]
    exponent = decay[:, length - 1 :] - decay + gate_in
    exponent = jnp.where(ids == ids[:, length - 1 :], exponent, FLOOR_NEG)
    top = jnp.max(exponent, axis=1, keepdims=True)
    factors[...] = jnp.exp(exponent - top)
    tops[...] = jnp.broadcast_to(top, tops.shape)
    decays[...] = jnp.broadcast_to(decay[:, length - 1 :], decays.shape)
    source_rows[...] = gate_in - decay
    decay_rows[...] = decay
    docs = ids.astype(F32) + 1.0
    docs_row[...] = docs
    filler = jnp.zeros((LANES - heads - 1, length), F32)
    columns[...] = jnp.concatenate([decay, docs, filler], axis=0).T


def state_kernel(heads, scalars, *refs):
    k_own, v_own, k_oth, v_oth, factors, tops, decays, docs_ref = refs[:8]
    outs = refs[8:]
    mine, core = scalars[0], scalars[1]
    tokens, key_width = k_own.shape[1:]
    length = 2 * tokens
    doc = jnp.broadcast_to(docs_ref[:, length - 1 :], (1, LANES))
    for slot in range(len(outs) - 1, -1, -1):
        out = outs[slot]
        local_head = jnp.bitwise_xor(mine, slot)
        head = (heads // 2) * core + local_head
        row = factors[pl.ds(head, 1), :]
        first, last = row[:, :tokens], row[:, tokens:]
        high, low, values, normal = [], [], [], None
        for k_ref, v_ref, f in (
            (k_own, v_own, jnp.where(core == 0, first, last)),
            (k_oth, v_oth, jnp.where(core == 0, last, first)),
        ):
            keys = k_ref[local_head]
            scaled = keys.astype(F32).T * f
            high.append(scaled.astype(BF16))
            low.append((scaled - high[-1].astype(F32)).astype(BF16))
            values.append(v_ref[local_head])
            pieces = jnp.concatenate(split3(f) + (jnp.zeros((META - 3, tokens), F32),), axis=0)
            sums = dot(pieces.astype(BF16), keys)
            line = (sums[2:3] + sums[1:2]) + sums[0:1]
            normal = line if normal is None else normal + line
        total = dot(jnp.concatenate(low + high, axis=1), jnp.concatenate(values * 2, axis=0))
        out[:key_width, :] = total.astype(BF16)
        out[key_width:, :] = meta_rows(
            normal, tops[pl.ds(head, 1), :], decays[pl.ds(head, 1), :], doc, out.shape[1]
        )


def decay_before(mine, place, decays):
    group = decays.shape[0]
    before = jnp.zeros_like(decays)
    for i in range(group):
        before = before + jnp.where(place > jnp.bitwise_xor(mine, i), decays[i : i + 1], 0.0)
    return before


def total_kernel(group, scalars, *refs):
    states, out = refs[:group], refs[group]
    mine = scalars[0]
    key_width, width = out.shape[0] - META, out.shape[1]
    normals, tops, decays, docs = read_meta(states)
    place = jnp.bitwise_xor(iota((group, LANES), 0), mine)
    whole_decay = jnp.sum(decays, axis=0, keepdims=True)
    after = whole_decay - decay_before(mine, place, decays) - decays
    doc = jnp.sum(jnp.where(place == group - 1, docs, 0.0), axis=0, keepdims=True)
    alive = docs == doc
    reached = jnp.where(alive, tops + after, FLOOR_NEG)
    top = jnp.max(reached, axis=0, keepdims=True)
    coefs = jnp.where(alive, jnp.exp(reached - top), 0.0)
    weighted(states, [out], [[coefs[i : i + 1] for i in range(group)]])
    normal = jnp.sum(wide(coefs, key_width) * normals, axis=0, keepdims=True)
    out[key_width:, :] = meta_rows(normal, top, whole_decay, doc, width)


def entering_kernel(group, reach, scalars, *refs):
    states, totals, outs = refs[:group], refs[group : group + reach], refs[group + reach :]
    mine = scalars[0]
    key_width, width = outs[0].shape[0] - META, outs[0].shape[1]
    normals, tops, decays, docs = read_meta(states)
    far_normals, far_tops, far_decays, far_docs = read_meta(totals)
    place = jnp.bitwise_xor(iota((group, LANES), 0), mine)
    before = decay_before(mine, place, decays)
    zero = jnp.zeros((1, LANES), F32)
    far_reached, passed, lines = [], zero, []
    for d in range(reach):
        far_reached.append(far_tops[d : d + 1] + passed)
        passed = passed + far_decays[d : d + 1]
    far_reached = jnp.concatenate(far_reached, axis=0)
    for r in range(group):
        here = jnp.bitwise_xor(mine, r)
        doc = jnp.sum(jnp.where(place == here - 1, docs, 0.0), axis=0, keepdims=True)
        doc = jnp.where(here == 0, far_docs[0:1], doc)
        mark = before[r : r + 1]
        alive = (place < here) & (docs == doc)
        reached = jnp.where(alive, tops + (mark - before - decays), FLOOR_NEG)
        far_alive = (far_docs == doc) & (far_docs > 0.5)
        far = jnp.where(far_alive, far_reached + mark, FLOOR_NEG)
        top = jnp.maximum(
            jnp.max(reached, axis=0, keepdims=True), jnp.max(far, axis=0, keepdims=True)
        )
        coefs = jnp.where(alive, jnp.exp(reached - top), 0.0)
        far_coefs = jnp.where(far_alive, jnp.exp(far - top), 0.0)
        lines.append(
            [None if i == r else coefs[i : i + 1] for i in range(group)]
            + [far_coefs[d : d + 1] for d in range(reach)]
        )
        normal = jnp.sum(wide(coefs, key_width) * normals, axis=0, keepdims=True)
        normal = normal + jnp.sum(wide(far_coefs, key_width) * far_normals, axis=0, keepdims=True)
        outs[r][key_width:, :] = meta_rows(normal, top, zero, doc, width)
    weighted(list(states) + list(totals), outs, lines)


def local_kernel(first_slot, heads, scalars, *refs):
    q_own, k_own, v_own, q_oth, k_oth, v_oth, source_rows, decay_rows, columns, docs_ref = refs[:10]
    numerators, stats = refs[-2:]
    mine, core = scalars[0], scalars[1]
    tokens, key_width = q_own.shape[1:]
    length = 2 * tokens
    scaling = key_width**-0.5
    is_first = core == 0
    lane = iota((length, LANES), 1)
    turned = columns[...]
    docs = turned[:, heads : heads + 1]
    source_docs = docs_ref[...]
    causal = iota((tokens, tokens), 0) >= iota((tokens, tokens), 1)
    for step in range(numerators.shape[0]):
        local_head = jnp.bitwise_xor(mine, first_slot + step)
        head = (heads // 2) * core + local_head
        source = source_rows[pl.ds(head, 1), :]
        decay = jnp.sum(jnp.where(lane == head, turned, 0.0), axis=1, keepdims=True)

        def ordered(own, other):
            own, other = own[local_head], other[local_head]
            return jnp.where(is_first, own, other), jnp.where(is_first, other, own)

        queries, keys, values = ordered(q_own, q_oth), ordered(k_own, k_oth), ordered(v_own, v_oth)
        for block in range(2):
            rows = slice(block * tokens, (block + 1) * tokens)
            exponents = []
            for s in range(block + 1):
                cols = slice(s * tokens, (s + 1) * tokens)
                allowed = docs[rows] == source_docs[:, cols]
                if s == block:
                    allowed = allowed & causal
                exponents.append(jnp.where(allowed, decay[rows] + source[:, cols], FLOOR_NEG))
            stabilizer = functools.reduce(
                jnp.maximum, [jnp.max(x, axis=1, keepdims=True) for x in exponents]
            )
            factors, sources, denominator = [], [], None
            for s in range(block + 1):
                weights = dot(queries[block], keys[s], NT) * scaling
                weights = weights * jnp.exp(exponents[s] - stabilizer)
                high = weights.astype(BF16)
                factors.append(high)
                sources.append(values[s])
                if s < block:
                    factors.append((weights - high.astype(F32)).astype(BF16))
                    sources.append(values[s])
                part = jnp.sum(weights, axis=1, keepdims=True)
                denominator = part if s == 0 else denominator + part
            numerator = dot(jnp.concatenate(factors, axis=1), jnp.concatenate(sources, axis=0))
            side = core if block == 0 else 1 - core
            numerators[step, side] = numerator
            first_lane = iota((tokens, LANES), 1) == 0
            pair = jnp.where(first_lane, stabilizer, denominator).T
            stats[step, side] = jnp.concatenate(
                [pair[:2], decay_rows[pl.ds(head, 1), rows], source_docs[:, rows], pair[4:8]], axis=0
            )


def output_kernel(first, count, scalars, q_own, q_oth, *refs):
    terms, entering, (keep, send) = refs[:4], refs[4 : 4 + count], refs[4 + count :]
    key_width = q_own.shape[2]
    scaling = key_width**-0.5
    early = terms[0].shape[0]
    for i, payload in enumerate(entering):
        slot = first + i
        numerators, stats = terms[:2] if slot < early else terms[2:]
        at = slot % early
        local_head = jnp.bitwise_xor(scalars[0], slot)
        normal, top, _, doc = read_meta([payload])
        pieces = split3(normal) + (jnp.zeros((META - 3, key_width), F32),)
        pieces = jnp.concatenate(pieces, axis=0).astype(BF16)
        memory = payload[:key_width, :]
        width = memory.shape[1]
        for side, (q_ref, out) in enumerate(((q_own, keep), (q_oth, send))):
            query = q_ref[local_head]
            tokens = query.shape[0]
            stat = stats[at, side]
            local = stat[0:1]
            alive = stat[3:4] == wide(doc, tokens)
            carried = jnp.where(alive, stat[2:3] + wide(top, tokens), FLOOR_NEG)
            stabilizer = jnp.maximum(local, carried)
            shrink = jnp.exp(local - stabilizer)
            retained = jnp.exp(carried - stabilizer) * scaling
            seen = dot(pieces, query, NT)
            seen = (seen[2:3] + seen[1:2]) + seen[0:1]
            denominator = shrink * stat[1:2] + retained * seen
            inverse = 1.0 / jnp.maximum(jnp.abs(denominator), 1.0)
            near = jnp.broadcast_to(shrink * inverse, (LANES, tokens)).T
            far = jnp.broadcast_to(retained * inverse, (LANES, tokens)).T
            result = wide(near, width) * numerators[at, side]
            out[i] = (result + wide(far, width) * dot(query, memory)).astype(BF16)


def merge_kernel(heads, scalars, *refs):
    stacks, out = refs[:-1], refs[-1]
    half = heads // 2
    n = LAY // heads
    mine, core = scalars[0], scalars[1]
    into, given = iota((LAY, LAY), 0), iota((LAY, LAY), 1)
    index = given // n
    slot = jnp.bitwise_and(index, half - 1)
    side = jnp.where(index < half, core, 1 - core)
    head = side * half + jnp.bitwise_xor(slot, mine)
    order = ((into % heads == head) & (into // heads == given % n)).astype(BF16)
    _, tokens, width = stacks[0].shape
    for g in range(tokens // n):
        span = slice(g * n, (g + 1) * n)
        rows = jnp.concatenate([stack[:, span, :] for stack in stacks], axis=0)
        turned = dot(order, rows.reshape(LAY, width))
        out[span] = turned.reshape(n, heads, width).astype(BF16)


def whole(shape):
    return pl.BlockSpec(shape, lambda *_: (0,) * len(shape))


def params():
    return pltpu.CompilerParams(vmem_limit_bytes=16 * 2**20)


SMEM = pl.BlockSpec(memory_space=pltpu.SMEM)
VMEM = pl.BlockSpec(memory_space=pltpu.VMEM)


def shape_of(*dims, dtype=BF16):
    return jax.ShapeDtypeStruct(dims, dtype)


def local(devices, queries, key_vectors, value_vectors, input_gate, forget_gate, doc_ids):
    tokens, heads, key_width = queries.shape
    value_width = value_vectors.shape[2]
    half = heads // 2
    group = half
    chips = devices // 2
    levels = chips // group
    reach = max(1, levels // 2)
    ctx, hv = lax.axis_index("ctx"), lax.axis_index("hv")
    chip = ctx * (lax.axis_size("hv") // 2) + hv // 2
    scalars = jnp.stack([chip % group, hv % 2]).astype(jnp.int32)
    ids = doc_ids[None, :]

    def swap_cores(x):
        return lax.ppermute(x, AXES, [(d, d ^ 1) for d in range(devices)])

    def in_group(x, r):
        pairs = [(d, d ^ (2 * r)) for d in range(devices)]
        return lax.ppermute(x, AXES, pairs)

    def to_next(x):
        jump = 2 * group
        return lax.ppermute(x, AXES, [(d, d + jump) for d in range(devices - jump)])

    rows = key_width + META
    state = (rows, value_width)
    sizes = {key_width: (half, tokens, key_width), value_width: (half, tokens, value_width)}

    def relayout(*sources):
        outs = [sizes[x.shape[2]] for x in sources] * 2
        return pl.pallas_call(
            functools.partial(relayout_kernel, half, len(sources)),
            in_specs=[whole(x.shape) for x in sources],
            out_specs=[VMEM] * len(outs),
            out_shape=[shape_of(*s) for s in outs],
            compiler_params=params(),
                name="relayout",
        )(*sources)

    gates = jnp.concatenate([input_gate.T, forget_gate.T], axis=0)
    gates, key_vectors = lax.optimization_barrier((gates, key_vectors))
    gates_oth = swap_cores(gates)
    k_keep, v_keep, k_send, v_send = relayout(key_vectors, value_vectors)
    gates_oth, k_send, v_send = lax.optimization_barrier((gates_oth, k_send, v_send))
    k_oth = swap_cores(k_send)
    v_oth = swap_cores(v_send)
    gate_shapes = [
        (heads, 2 * tokens),
        (heads, LANES),
        (heads, LANES),
        (heads, 2 * tokens),
        (heads, 2 * tokens),
        (2 * tokens, LANES),
        (1, 2 * tokens),
    ]
    factors, tops, decays, source_rows, decay_rows, columns, docs = pl.pallas_call(
        functools.partial(gates_kernel, heads),
        in_specs=[SMEM, VMEM, VMEM, VMEM],
        out_specs=[VMEM] * len(gate_shapes),
        out_shape=[shape_of(*s, dtype=F32) for s in gate_shapes],
        compiler_params=params(),
        name="gates",
    )(scalars, gates, gates_oth, ids)

    by_core = (k_keep, v_keep, k_oth, v_oth, factors, tops, decays, docs)
    made = pl.pallas_call(
        functools.partial(state_kernel, heads),
        in_specs=[SMEM] + [VMEM] * len(by_core),
        out_specs=[VMEM] * group,
        out_shape=[shape_of(*state)] * group,
        compiler_params=params(),
        name="states",
    )(scalars, *by_core)
    gathered = [made[0]] + [in_group(made[r], r) for r in range(1, group)]
    total = pl.pallas_call(
        functools.partial(total_kernel, group),
        in_specs=[SMEM] + [VMEM] * group,
        out_specs=VMEM,
        out_shape=shape_of(*state),
        compiler_params=params(),
        name="group_total",
    )(scalars, *gathered)
    queries, gathered[0] = lax.optimization_barrier((queries, gathered[0]))
    q_keep, q_send = relayout(queries)
    q_oth = swap_cores(q_send)
    small = (source_rows, decay_rows, columns, docs)
    early = half // 2

    def own_terms(first_slot, q_own):
        operands = (q_own, k_keep, v_keep, q_oth, k_oth, v_oth, *small)
        return pl.pallas_call(
            functools.partial(local_kernel, first_slot, heads),
            in_specs=[SMEM] + [VMEM] * len(operands),
            out_specs=[VMEM] * 2,
            out_shape=[
                shape_of(early, 2, tokens, value_width, dtype=F32),
                shape_of(early, 2, 8, tokens, dtype=F32),
            ],
            compiler_params=params(),
            name="own_terms",
        )(scalars, *operands)

    q_first, _ = lax.optimization_barrier((q_keep, total))
    first_terms = own_terms(0, q_first)
    totals = [to_next(total)]
    totals[0], first_terms = lax.optimization_barrier((totals[0], first_terms))
    while len(totals) < reach:
        totals.append(to_next(totals[-1]))
    q_last, _ = lax.optimization_barrier((q_keep, totals[0]))
    last_terms = own_terms(early, q_last)
    gathered[0], last_terms = lax.optimization_barrier((gathered[0], last_terms))
    terms = [*first_terms, *last_terms]

    leaving = pl.pallas_call(
        functools.partial(entering_kernel, group, reach),
        in_specs=[SMEM] + [VMEM] * (group + reach),
        out_specs=[VMEM] * group,
        out_shape=[shape_of(*state)] * group,
        compiler_params=params(),
        name="entering",
    )(scalars, *gathered, *totals)
    entering = [leaving[0]] + [in_group(leaving[r], r) for r in range(1, group)]

    def outputs(first, count):
        return pl.pallas_call(
            functools.partial(output_kernel, first, count),
            in_specs=[SMEM] + [VMEM] * (6 + count),
            out_specs=[VMEM] * 2,
            out_shape=[shape_of(count, tokens, value_width)] * 2,
            compiler_params=params(),
            name="outputs",
        )(scalars, q_keep, q_oth, *terms, *entering[first : first + count])

    keep, send = outputs(0, 1)
    swapped = swap_cores(send)
    terms, swapped = lax.optimization_barrier((terms, swapped))
    keep_far, send = outputs(1, group - 1)
    kept, received = [keep, keep_far], [swapped, swap_cores(send)]
    return pl.pallas_call(
        functools.partial(merge_kernel, heads),
        in_specs=[SMEM] + [VMEM] * 4,
        out_specs=whole(value_vectors.shape),
        out_shape=shape_of(*value_vectors.shape),
        compiler_params=params(),
        name="merge",
    )(scalars, *kept, *received)


def solution(mesh):
    return jax.shard_map(
        functools.partial(local, mesh.size),
        mesh=mesh,
        in_specs=(
            P(AXES, None, None),
            P(AXES, None, None),
            P(AXES, None, None),
            P(AXES, None),
            P(AXES, None),
            P("ctx"),
        ),
        out_specs=P(AXES, None, None),
        check_vma=False,
    )
```

```python
import functools

import jax
import jax.numpy as jnp
from jax import lax
from jax.experimental import pallas as pl
from jax.experimental.pallas import tpu as pltpu
from jax.sharding import PartitionSpec as P

AXES = ("ctx", "hv")
FLOOR_NEG = -1e30
META = 16
LANES = 128
LAY = 256
F32, BF16 = jnp.float32, jnp.bfloat16

NN = (((1,), (0,)), ((), ()))
NT = (((1,), (1,)), ((), ()))


def dot(a, b, dims=NN):
    return lax.dot_general(a, b, dims, preferred_element_type=F32)


def split3(x):
    hi = x.astype(BF16).astype(F32)
    mid = (x - hi).astype(BF16).astype(F32)
    return hi, mid, (x - hi - mid).astype(BF16).astype(F32)


def iota(shape, dim):
    return lax.broadcasted_iota(jnp.int32, shape, dim)


def meta_rows(normalizer, top, decay, doc, width):
    used = normalizer.shape[1]
    row = iota((META, used), 0)
    rows = jnp.where(row == 6, wide(doc, used), 0.0)
    lines = split3(normalizer) + split3(jnp.concatenate([top, decay], axis=1))
    for index, line in enumerate(lines):
        rows = jnp.where(row == index, line, rows)
    spare = jnp.zeros((META, width - used), F32)
    return jnp.concatenate([rows, spare], axis=1).astype(BF16)


def read_meta(refs):
    key_width = refs[0].shape[0] - META
    rows = [ref[key_width:, : 2 * LANES].astype(F32) for ref in refs]
    normals = jnp.concatenate([(x[2:3] + x[1:2]) + x[0:1] for x in rows], axis=0)
    line = jnp.concatenate([(x[5:6] + x[4:5]) + x[3:4] for x in rows], axis=0)
    docs = jnp.concatenate([x[6:7, :LANES] for x in rows], axis=0)
    return normals, line[:, :LANES], line[:, LANES:], docs


def wide(x, width):
    return jnp.concatenate([x] * (width // LANES), axis=1)


CHUNK = 32


def weighted(refs, outs, coefs):
    key_width, width = refs[0].shape[0] - META, refs[0].shape[1]
    coefs = [[None if c is None else wide(c, width) for c in line] for line in coefs]
    for start in range(0, key_width, CHUNK):
        rows = slice(start, start + CHUNK)
        parts = [ref[rows, :].astype(F32) for ref in refs]
        for out, line in zip(outs, coefs, strict=True):
            terms = [c * part for c, part in zip(line, parts, strict=True) if c is not None]
            out[rows, :] = functools.reduce(jnp.add, terms).astype(BF16)


def gate_rows(core, own_ref, other_ref, heads):
    own, other = own_ref[...].astype(F32), other_ref[...].astype(F32)
    both = jnp.concatenate(
        [jnp.where(core == 0, own, other), jnp.where(core == 0, other, own)], axis=1
    )
    gate_in, forget = both[:heads], both[heads:]
    log_forget = jnp.minimum(forget, 0.0) - jnp.log1p(jnp.exp(-jnp.abs(forget)))
    length = both.shape[1]
    upto = (iota((length, length), 0) <= iota((length, length), 1)).astype(BF16)
    pieces = dot(jnp.concatenate(split3(log_forget), axis=0).astype(BF16), upto)
    decay = (pieces[2 * heads :] + pieces[heads : 2 * heads]) + pieces[:heads]
    return gate_in, decay


def by_head_order(heads):
    n = LAY // heads
    out, inside = iota((LAY, LAY), 0), iota((LAY, LAY), 1)
    return ((inside % heads == out // n) & (inside // heads == out % n)).astype(BF16)


def relayout_kernel(half, count, *refs):
    sources, outs = refs[:count], refs[count:]
    heads = 2 * half
    n = LAY // heads
    core = lax.axis_index("hv") % 2
    order = by_head_order(heads)
    for index, source in enumerate(sources):
        keep, send = outs[index], outs[count + index]
        tokens, _, width = source.shape
        for g in range(tokens // n):
            span = slice(g * n, (g + 1) * n)
            rows = dot(order, source[span].reshape(LAY, width)).astype(BF16)
            rows = rows.reshape(heads, n, width)
            keep[:, span, :] = jnp.where(core == 0, rows[:half], rows[half:])
            send[:, span, :] = jnp.where(core == 0, rows[half:], rows[:half])


def gates_kernel(heads, scalars, g_own, g_oth, ids_ref, *outs):
    factors, tops, decays, source_rows, decay_rows, columns, docs_row = outs
    core = scalars[1]
    length = factors.shape[1]
    gate_in, decay = gate_rows(core, g_own, g_oth, heads)
    chip = lax.axis_index("hv") // 2
    ids = ids_ref[:, pl.ds(pl.multiple_of(chip * length, length), length)]
    exponent = decay[:, length - 1 :] - decay + gate_in
    exponent = jnp.where(ids == ids[:, length - 1 :], exponent, FLOOR_NEG)
    top = jnp.max(exponent, axis=1, keepdims=True)
    factors[...] = jnp.exp(exponent - top)
    tops[...] = jnp.broadcast_to(top, tops.shape)
    decays[...] = jnp.broadcast_to(decay[:, length - 1 :], decays.shape)
    source_rows[...] = gate_in - decay
    decay_rows[...] = decay
    docs = ids.astype(F32) + 1.0
    docs_row[...] = docs
    filler = jnp.zeros((LANES - heads - 1, length), F32)
    columns[...] = jnp.concatenate([decay, docs, filler], axis=0).T


def state_kernel(heads, scalars, *refs):
    k_own, v_own, k_oth, v_oth, factors, tops, decays, docs_ref = refs[:8]
    outs = refs[8:]
    mine, core = scalars[0], scalars[1]
    tokens, key_width = k_own.shape[1:]
    length = 2 * tokens
    doc = jnp.broadcast_to(docs_ref[:, length - 1 :], (1, LANES))
    for slot in range(len(outs) - 1, -1, -1):
        out = outs[slot]
        local_head = jnp.bitwise_xor(mine, slot)
        head = (heads // 2) * core + local_head
        row = factors[pl.ds(head, 1), :]
        first, last = row[:, :tokens], row[:, tokens:]
        high, low, values, normal = [], [], [], None
        for k_ref, v_ref, f in (
            (k_own, v_own, jnp.where(core == 0, first, last)),
            (k_oth, v_oth, jnp.where(core == 0, last, first)),
        ):
            keys = k_ref[local_head]
            scaled = keys.astype(F32).T * f
            high.append(scaled.astype(BF16))
            low.append((scaled - high[-1].astype(F32)).astype(BF16))
            values.append(v_ref[local_head])
            pieces = jnp.concatenate(split3(f) + (jnp.zeros((META - 3, tokens), F32),), axis=0)
            sums = dot(pieces.astype(BF16), keys)
            line = (sums[2:3] + sums[1:2]) + sums[0:1]
            normal = line if normal is None else normal + line
        total = dot(jnp.concatenate(low + high, axis=1), jnp.concatenate(values * 2, axis=0))
        out[:key_width, :] = total.astype(BF16)
        out[key_width:, :] = meta_rows(
            normal, tops[pl.ds(head, 1), :], decays[pl.ds(head, 1), :], doc, out.shape[1]
        )


def decay_before(mine, place, decays):
    group = decays.shape[0]
    before = jnp.zeros_like(decays)
    for i in range(group):
        before = before + jnp.where(place > jnp.bitwise_xor(mine, i), decays[i : i + 1], 0.0)
    return before


def total_kernel(group, scalars, *refs):
    states, out = refs[:group], refs[group]
    mine = scalars[0]
    key_width, width = out.shape[0] - META, out.shape[1]
    normals, tops, decays, docs = read_meta(states)
    place = jnp.bitwise_xor(iota((group, LANES), 0), mine)
    whole_decay = jnp.sum(decays, axis=0, keepdims=True)
    after = whole_decay - decay_before(mine, place, decays) - decays
    doc = jnp.sum(jnp.where(place == group - 1, docs, 0.0), axis=0, keepdims=True)
    alive = docs == doc
    reached = jnp.where(alive, tops + after, FLOOR_NEG)
    top = jnp.max(reached, axis=0, keepdims=True)
    coefs = jnp.where(alive, jnp.exp(reached - top), 0.0)
    weighted(states, [out], [[coefs[i : i + 1] for i in range(group)]])
    normal = jnp.sum(wide(coefs, key_width) * normals, axis=0, keepdims=True)
    out[key_width:, :] = meta_rows(normal, top, whole_decay, doc, width)


def entering_kernel(group, reach, scalars, *refs):
    states, totals, outs = refs[:group], refs[group : group + reach], refs[group + reach :]
    mine = scalars[0]
    key_width, width = outs[0].shape[0] - META, outs[0].shape[1]
    normals, tops, decays, docs = read_meta(states)
    far_normals, far_tops, far_decays, far_docs = read_meta(totals)
    place = jnp.bitwise_xor(iota((group, LANES), 0), mine)
    before = decay_before(mine, place, decays)
    zero = jnp.zeros((1, LANES), F32)
    far_reached, passed, lines = [], zero, []
    for d in range(reach):
        far_reached.append(far_tops[d : d + 1] + passed)
        passed = passed + far_decays[d : d + 1]
    far_reached = jnp.concatenate(far_reached, axis=0)
    for r in range(group):
        here = jnp.bitwise_xor(mine, r)
        doc = jnp.sum(jnp.where(place == here - 1, docs, 0.0), axis=0, keepdims=True)
        doc = jnp.where(here == 0, far_docs[0:1], doc)
        mark = before[r : r + 1]
        alive = (place < here) & (docs == doc)
        reached = jnp.where(alive, tops + (mark - before - decays), FLOOR_NEG)
        far_alive = (far_docs == doc) & (far_docs > 0.5)
        far = jnp.where(far_alive, far_reached + mark, FLOOR_NEG)
        top = jnp.maximum(
            jnp.max(reached, axis=0, keepdims=True), jnp.max(far, axis=0, keepdims=True)
        )
        coefs = jnp.where(alive, jnp.exp(reached - top), 0.0)
        far_coefs = jnp.where(far_alive, jnp.exp(far - top), 0.0)
        lines.append(
            [None if i == r else coefs[i : i + 1] for i in range(group)]
            + [far_coefs[d : d + 1] for d in range(reach)]
        )
        normal = jnp.sum(wide(coefs, key_width) * normals, axis=0, keepdims=True)
        normal = normal + jnp.sum(wide(far_coefs, key_width) * far_normals, axis=0, keepdims=True)
        outs[r][key_width:, :] = meta_rows(normal, top, zero, doc, width)
    weighted(list(states) + list(totals), outs, lines)


def local_kernel(first_slot, heads, scalars, *refs):
    q_own, k_own, v_own, q_oth, k_oth, v_oth, source_rows, decay_rows, columns, docs_ref = refs[:10]
    numerators, stats = refs[-2:]
    mine, core = scalars[0], scalars[1]
    tokens, key_width = q_own.shape[1:]
    length = 2 * tokens
    scaling = key_width**-0.5
    is_first = core == 0
    lane = iota((length, LANES), 1)
    turned = columns[...]
    docs = turned[:, heads : heads + 1]
    source_docs = docs_ref[...]
    causal = iota((tokens, tokens), 0) >= iota((tokens, tokens), 1)
    for step in range(numerators.shape[0]):
        local_head = jnp.bitwise_xor(mine, first_slot + step)
        head = (heads // 2) * core + local_head
        source = source_rows[pl.ds(head, 1), :]
        decay = jnp.sum(jnp.where(lane == head, turned, 0.0), axis=1, keepdims=True)

        def ordered(own, other):
            own, other = own[local_head], other[local_head]
            return jnp.where(is_first, own, other), jnp.where(is_first, other, own)

        queries, keys, values = ordered(q_own, q_oth), ordered(k_own, k_oth), ordered(v_own, v_oth)
        for block in range(2):
            rows = slice(block * tokens, (block + 1) * tokens)
            exponents = []
            for s in range(block + 1):
                cols = slice(s * tokens, (s + 1) * tokens)
                allowed = docs[rows] == source_docs[:, cols]
                if s == block:
                    allowed = allowed & causal
                exponents.append(jnp.where(allowed, decay[rows] + source[:, cols], FLOOR_NEG))
            stabilizer = functools.reduce(
                jnp.maximum, [jnp.max(x, axis=1, keepdims=True) for x in exponents]
            )
            factors, sources, denominator = [], [], None
            for s in range(block + 1):
                weights = dot(queries[block], keys[s], NT) * scaling
                weights = weights * jnp.exp(exponents[s] - stabilizer)
                high = weights.astype(BF16)
                factors.append(high)
                sources.append(values[s])
                if s < block:
                    factors.append((weights - high.astype(F32)).astype(BF16))
                    sources.append(values[s])
                part = jnp.sum(weights, axis=1, keepdims=True)
                denominator = part if s == 0 else denominator + part
            numerator = dot(jnp.concatenate(factors, axis=1), jnp.concatenate(sources, axis=0))
            side = core if block == 0 else 1 - core
            numerators[step, side] = numerator
            first_lane = iota((tokens, LANES), 1) == 0
            pair = jnp.where(first_lane, stabilizer, denominator).T
            stats[step, side] = jnp.concatenate(
                [pair[:2], decay_rows[pl.ds(head, 1), rows], source_docs[:, rows], pair[4:8]], axis=0
            )


def output_kernel(first, count, scalars, q_own, q_oth, *refs):
    terms, entering, (keep, send) = refs[:4], refs[4 : 4 + count], refs[4 + count :]
    key_width = q_own.shape[2]
    scaling = key_width**-0.5
    early = terms[0].shape[0]
    for i, payload in enumerate(entering):
        slot = first + i
        numerators, stats = terms[:2] if slot < early else terms[2:]
        at = slot % early
        local_head = jnp.bitwise_xor(scalars[0], slot)
        normal, top, _, doc = read_meta([payload])
        pieces = split3(normal) + (jnp.zeros((META - 3, key_width), F32),)
        pieces = jnp.concatenate(pieces, axis=0).astype(BF16)
        memory = payload[:key_width, :]
        width = memory.shape[1]
        for side, (q_ref, out) in enumerate(((q_own, keep), (q_oth, send))):
            query = q_ref[local_head]
            tokens = query.shape[0]
            stat = stats[at, side]
            local = stat[0:1]
            alive = stat[3:4] == wide(doc, tokens)
            carried = jnp.where(alive, stat[2:3] + wide(top, tokens), FLOOR_NEG)
            stabilizer = jnp.maximum(local, carried)
            shrink = jnp.exp(local - stabilizer)
            retained = jnp.exp(carried - stabilizer) * scaling
            seen = dot(pieces, query, NT)
            seen = (seen[2:3] + seen[1:2]) + seen[0:1]
            denominator = shrink * stat[1:2] + retained * seen
            inverse = 1.0 / jnp.maximum(jnp.abs(denominator), 1.0)
            near = jnp.broadcast_to(shrink * inverse, (LANES, tokens)).T
            far = jnp.broadcast_to(retained * inverse, (LANES, tokens)).T
            result = wide(near, width) * numerators[at, side]
            out[i] = (result + wide(far, width) * dot(query, memory)).astype(BF16)


def merge_kernel(heads, scalars, *refs):
    stacks, (out, result, written) = refs[:-3], refs[-3:]
    half = heads // 2
    n = LAY // heads
    mine, core = scalars[0], scalars[1]
    into, given = iota((LAY, LAY), 0), iota((LAY, LAY), 1)
    index = given // n
    slot = jnp.bitwise_and(index, half - 1)
    side = jnp.where(index < half, core, 1 - core)
    head = side * half + jnp.bitwise_xor(slot, mine)
    order = ((into % heads == head) & (into // heads == given % n)).astype(BF16)
    _, tokens, width = stacks[0].shape
    copies = []
    for g in range(tokens // n):
        span = slice(g * n, (g + 1) * n)
        rows = jnp.concatenate([stack[:, span, :] for stack in stacks], axis=0)
        turned = dot(order, rows.reshape(LAY, width))
        result[span] = turned.reshape(n, heads, width).astype(BF16)
        copies.append(pltpu.make_async_copy(result.at[span], out.at[span], written.at[g]))
        copies[-1].start()
    for copy in copies:
        copy.wait()


def whole(shape):
    return pl.BlockSpec(shape, lambda *_: (0,) * len(shape))


def params():
    return pltpu.CompilerParams(vmem_limit_bytes=16 * 2**20)


SMEM = pl.BlockSpec(memory_space=pltpu.SMEM)
VMEM = pl.BlockSpec(memory_space=pltpu.VMEM)


def shape_of(*dims, dtype=BF16):
    return jax.ShapeDtypeStruct(dims, dtype)


def local(devices, queries, key_vectors, value_vectors, input_gate, forget_gate, doc_ids):
    tokens, heads, key_width = queries.shape
    value_width = value_vectors.shape[2]
    half = heads // 2
    group = half
    chips = devices // 2
    levels = chips // group
    reach = max(1, levels // 2)
    ctx, hv = lax.axis_index("ctx"), lax.axis_index("hv")
    chip = ctx * (lax.axis_size("hv") // 2) + hv // 2
    scalars = jnp.stack([chip % group, hv % 2]).astype(jnp.int32)
    ids = doc_ids[None, :]

    def swap_cores(x):
        return lax.ppermute(x, AXES, [(d, d ^ 1) for d in range(devices)])

    def in_group(x, r):
        pairs = [(d, d ^ (2 * r)) for d in range(devices)]
        return lax.ppermute(x, AXES, pairs)

    def to_next(x):
        jump = 2 * group
        return lax.ppermute(x, AXES, [(d, d + jump) for d in range(devices - jump)])

    rows = key_width + META
    state = (rows, value_width)
    sizes = {key_width: (half, tokens, key_width), value_width: (half, tokens, value_width)}

    def relayout(*sources):
        outs = [sizes[x.shape[2]] for x in sources] * 2
        return pl.pallas_call(
            functools.partial(relayout_kernel, half, len(sources)),
            in_specs=[whole(x.shape) for x in sources],
            out_specs=[VMEM] * len(outs),
            out_shape=[shape_of(*s) for s in outs],
            compiler_params=params(),
                name="relayout",
        )(*sources)

    gates = jnp.concatenate([input_gate.T, forget_gate.T], axis=0)
    gates, value_vectors = lax.optimization_barrier((gates, value_vectors))
    gates_oth = swap_cores(gates)
    v_keep, v_send = relayout(value_vectors)
    gates_oth, v_send = lax.optimization_barrier((gates_oth, v_send))
    v_oth = swap_cores(v_send)
    k_keep, k_send = relayout(key_vectors)
    k_oth = swap_cores(k_send)
    gate_shapes = [
        (heads, 2 * tokens),
        (heads, LANES),
        (heads, LANES),
        (heads, 2 * tokens),
        (heads, 2 * tokens),
        (2 * tokens, LANES),
        (1, 2 * tokens),
    ]
    factors, tops, decays, source_rows, decay_rows, columns, docs = pl.pallas_call(
        functools.partial(gates_kernel, heads),
        in_specs=[SMEM, VMEM, VMEM, VMEM],
        out_specs=[VMEM] * len(gate_shapes),
        out_shape=[shape_of(*s, dtype=F32) for s in gate_shapes],
        compiler_params=params(),
        name="gates",
    )(scalars, gates, gates_oth, ids)

    by_core = (k_keep, v_keep, k_oth, v_oth, factors, tops, decays, docs)
    made = pl.pallas_call(
        functools.partial(state_kernel, heads),
        in_specs=[SMEM] + [VMEM] * len(by_core),
        out_specs=[VMEM] * group,
        out_shape=[shape_of(*state)] * group,
        compiler_params=params(),
        name="states",
    )(scalars, *by_core)
    gathered = [made[0]] + [in_group(made[r], r) for r in range(1, group)]
    total = pl.pallas_call(
        functools.partial(total_kernel, group),
        in_specs=[SMEM] + [VMEM] * group,
        out_specs=VMEM,
        out_shape=shape_of(*state),
        compiler_params=params(),
        name="group_total",
    )(scalars, *gathered)
    queries, gathered[0] = lax.optimization_barrier((queries, gathered[0]))
    q_keep, q_send = relayout(queries)
    q_oth = swap_cores(q_send)
    small = (source_rows, decay_rows, columns, docs)
    early = half // 2

    def own_terms(first_slot, q_own):
        operands = (q_own, k_keep, v_keep, q_oth, k_oth, v_oth, *small)
        return pl.pallas_call(
            functools.partial(local_kernel, first_slot, heads),
            in_specs=[SMEM] + [VMEM] * len(operands),
            out_specs=[VMEM] * 2,
            out_shape=[
                shape_of(early, 2, tokens, value_width, dtype=F32),
                shape_of(early, 2, 8, tokens, dtype=F32),
            ],
            compiler_params=params(),
            name="own_terms",
        )(scalars, *operands)

    q_first, _ = lax.optimization_barrier((q_keep, total))
    first_terms = own_terms(0, q_first)
    totals = [to_next(total)]
    totals[0], first_terms = lax.optimization_barrier((totals[0], first_terms))
    while len(totals) < reach:
        totals.append(to_next(totals[-1]))
    q_last, _ = lax.optimization_barrier((q_keep, totals[0]))
    last_terms = own_terms(early, q_last)
    gathered[0], last_terms = lax.optimization_barrier((gathered[0], last_terms))
    terms = [*first_terms, *last_terms]

    leaving = pl.pallas_call(
        functools.partial(entering_kernel, group, reach),
        in_specs=[SMEM] + [VMEM] * (group + reach),
        out_specs=[VMEM] * group,
        out_shape=[shape_of(*state)] * group,
        compiler_params=params(),
        name="entering",
    )(scalars, *gathered, *totals)
    entering = [leaving[0]] + [in_group(leaving[r], r) for r in range(1, group)]

    def outputs(first, count):
        return pl.pallas_call(
            functools.partial(output_kernel, first, count),
            in_specs=[SMEM] + [VMEM] * (6 + count),
            out_specs=[VMEM] * 2,
            out_shape=[shape_of(count, tokens, value_width)] * 2,
            compiler_params=params(),
            name="outputs",
        )(scalars, q_keep, q_oth, *terms, *entering[first : first + count])

    kept, received = [], []
    for r in range(group):
        keep, send = outputs(r, 1)
        kept.append(keep)
        received.append(swap_cores(send))
        if r == 0:
            terms, received[0] = lax.optimization_barrier((terms, received[0]))
        else:
            terms, _ = lax.optimization_barrier((terms, send))
    return pl.pallas_call(
        functools.partial(merge_kernel, heads),
        in_specs=[SMEM] + [VMEM] * heads,
        out_specs=pl.BlockSpec(memory_space=pl.ANY),
        out_shape=shape_of(*value_vectors.shape),
        scratch_shapes=[
            pltpu.VMEM(value_vectors.shape, BF16),
            pltpu.SemaphoreType.DMA((tokens // (LAY // heads),)),
        ],
        compiler_params=params(),
        name="merge",
    )(scalars, *kept, *received)


def solution(mesh):
    return jax.shard_map(
        functools.partial(local, mesh.size),
        mesh=mesh,
        in_specs=(
            P(AXES, None, None),
            P(AXES, None, None),
            P(AXES, None, None),
            P(AXES, None),
            P(AXES, None),
            P("ctx"),
        ),
        out_specs=P(AXES, None, None),
        check_vma=False,
    )
```

```python
import functools

import jax
import jax.numpy as jnp
from jax import lax
from jax.experimental import pallas as pl
from jax.experimental.pallas import tpu as pltpu
from jax.sharding import PartitionSpec as P

AXES = ("ctx", "hv")
FLOOR_NEG = -1e30
META = 8
PAD = 16
LANES = 128
LAY = 256
F32, BF16 = jnp.float32, jnp.bfloat16

NN = (((1,), (0,)), ((), ()))
NT = (((1,), (1,)), ((), ()))


def dot(a, b, dims=NN):
    return lax.dot_general(a, b, dims, preferred_element_type=F32)


def split3(x):
    hi = x.astype(BF16).astype(F32)
    mid = (x - hi).astype(BF16).astype(F32)
    return hi, mid, (x - hi - mid).astype(BF16).astype(F32)


def iota(shape, dim):
    return lax.broadcasted_iota(jnp.int32, shape, dim)


def meta_rows(normalizer, top, decay, doc, width):
    used = normalizer.shape[1]
    row = iota((META, used), 0)
    rows = jnp.where(row == 6, wide(doc, used), 0.0)
    lines = split3(normalizer) + split3(jnp.concatenate([top, decay], axis=1))
    for index, line in enumerate(lines):
        rows = jnp.where(row == index, line, rows)
    spare = jnp.zeros((META, width - used), F32)
    return jnp.concatenate([rows, spare], axis=1).astype(BF16)


def read_meta(refs):
    key_width = refs[0].shape[0] - META
    rows = [ref[key_width:, : 2 * LANES].astype(F32) for ref in refs]
    normals = jnp.concatenate([(x[2:3] + x[1:2]) + x[0:1] for x in rows], axis=0)
    line = jnp.concatenate([(x[5:6] + x[4:5]) + x[3:4] for x in rows], axis=0)
    docs = jnp.concatenate([x[6:7, :LANES] for x in rows], axis=0)
    return normals, line[:, :LANES], line[:, LANES:], docs


def wide(x, width):
    return jnp.concatenate([x] * (width // LANES), axis=1)


CHUNK = 32


def weighted(refs, outs, coefs):
    key_width, width = refs[0].shape[0] - META, refs[0].shape[1]
    coefs = [[None if c is None else wide(c, width) for c in line] for line in coefs]
    for start in range(0, key_width, CHUNK):
        rows = slice(start, start + CHUNK)
        parts = [ref[rows, :].astype(F32) for ref in refs]
        for out, line in zip(outs, coefs, strict=True):
            terms = [c * part for c, part in zip(line, parts, strict=True) if c is not None]
            out[rows, :] = functools.reduce(jnp.add, terms).astype(BF16)


def gate_rows(core, own_ref, other_ref, heads):
    own, other = own_ref[...].astype(F32), other_ref[...].astype(F32)
    both = jnp.concatenate(
        [jnp.where(core == 0, own, other), jnp.where(core == 0, other, own)], axis=1
    )
    gate_in, forget = both[:heads], both[heads:]
    log_forget = jnp.minimum(forget, 0.0) - jnp.log1p(jnp.exp(-jnp.abs(forget)))
    length = both.shape[1]
    upto = (iota((length, length), 0) <= iota((length, length), 1)).astype(BF16)
    pieces = dot(jnp.concatenate(split3(log_forget), axis=0).astype(BF16), upto)
    decay = (pieces[2 * heads :] + pieces[heads : 2 * heads]) + pieces[:heads]
    return gate_in, decay


def by_head_order(heads):
    n = LAY // heads
    out, inside = iota((LAY, LAY), 0), iota((LAY, LAY), 1)
    return ((inside % heads == out // n) & (inside // heads == out % n)).astype(BF16)


def relayout_kernel(half, source, keep, send, held, landed):
    heads = 2 * half
    n = LAY // heads
    core = lax.axis_index("hv") % 2
    tokens, _, width = source.shape
    spans = [slice(g * n, (g + 1) * n) for g in range(tokens // n)]
    copies = [
        pltpu.make_async_copy(source.at[span], held.at[span], landed.at[g])
        for g, span in enumerate(spans)
    ]
    for copy in copies:
        copy.start()
    order = by_head_order(heads)
    for span, copy in zip(spans, copies, strict=True):
        copy.wait()
        rows = dot(order, held[span].reshape(LAY, width)).astype(BF16)
        rows = rows.reshape(heads, n, width)
        keep[:, span, :] = jnp.where(core == 0, rows[:half], rows[half:])
        send[:, span, :] = jnp.where(core == 0, rows[half:], rows[:half])


def gates_kernel(heads, scalars, g_own, g_oth, ids_ref, *outs):
    factors, tops, decays, source_rows, decay_rows, columns, docs_row = outs
    core = scalars[1]
    length = factors.shape[1]
    gate_in, decay = gate_rows(core, g_own, g_oth, heads)
    chip = lax.axis_index("hv") // 2
    ids = ids_ref[:, pl.ds(pl.multiple_of(chip * length, length), length)]
    exponent = decay[:, length - 1 :] - decay + gate_in
    exponent = jnp.where(ids == ids[:, length - 1 :], exponent, FLOOR_NEG)
    top = jnp.max(exponent, axis=1, keepdims=True)
    factors[...] = jnp.exp(exponent - top)
    tops[...] = jnp.broadcast_to(top, tops.shape)
    decays[...] = jnp.broadcast_to(decay[:, length - 1 :], decays.shape)
    source_rows[...] = gate_in - decay
    decay_rows[...] = decay
    docs = ids.astype(F32) + 1.0
    docs_row[...] = docs
    filler = jnp.zeros((LANES - heads - 1, length), F32)
    columns[...] = jnp.concatenate([decay, docs, filler], axis=0).T


def state_kernel(heads, scalars, *refs):
    k_own, v_own, k_oth, v_oth, factors, tops, decays, docs_ref = refs[:8]
    outs = refs[8:]
    mine, core = scalars[0], scalars[1]
    tokens, key_width = k_own.shape[1:]
    length = 2 * tokens
    doc = jnp.broadcast_to(docs_ref[:, length - 1 :], (1, LANES))
    for slot in range(len(outs) - 1, -1, -1):
        out = outs[slot]
        local_head = jnp.bitwise_xor(mine, slot)
        head = (heads // 2) * core + local_head
        row = factors[pl.ds(head, 1), :]
        first, last = row[:, :tokens], row[:, tokens:]
        high, low, values, normal = [], [], [], None
        for k_ref, v_ref, f in (
            (k_own, v_own, jnp.where(core == 0, first, last)),
            (k_oth, v_oth, jnp.where(core == 0, last, first)),
        ):
            keys = k_ref[local_head]
            scaled = keys.astype(F32).T * f
            high.append(scaled.astype(BF16))
            low.append((scaled - high[-1].astype(F32)).astype(BF16))
            values.append(v_ref[local_head])
            pieces = jnp.concatenate(split3(f) + (jnp.zeros((PAD - 3, tokens), F32),), axis=0)
            sums = dot(pieces.astype(BF16), keys)
            line = (sums[2:3] + sums[1:2]) + sums[0:1]
            normal = line if normal is None else normal + line
        total = dot(jnp.concatenate(low + high, axis=1), jnp.concatenate(values * 2, axis=0))
        out[:key_width, :] = total.astype(BF16)
        out[key_width:, :] = meta_rows(
            normal, tops[pl.ds(head, 1), :], decays[pl.ds(head, 1), :], doc, out.shape[1]
        )


def decay_before(mine, place, decays):
    group = decays.shape[0]
    before = jnp.zeros_like(decays)
    for i in range(group):
        before = before + jnp.where(place > jnp.bitwise_xor(mine, i), decays[i : i + 1], 0.0)
    return before


def total_kernel(group, scalars, *refs):
    states, out = refs[:group], refs[group]
    mine = scalars[0]
    key_width, width = out.shape[0] - META, out.shape[1]
    normals, tops, decays, docs = read_meta(states)
    place = jnp.bitwise_xor(iota((group, LANES), 0), mine)
    whole_decay = jnp.sum(decays, axis=0, keepdims=True)
    after = whole_decay - decay_before(mine, place, decays) - decays
    doc = jnp.sum(jnp.where(place == group - 1, docs, 0.0), axis=0, keepdims=True)
    alive = docs == doc
    reached = jnp.where(alive, tops + after, FLOOR_NEG)
    top = jnp.max(reached, axis=0, keepdims=True)
    coefs = jnp.where(alive, jnp.exp(reached - top), 0.0)
    weighted(states, [out], [[coefs[i : i + 1] for i in range(group)]])
    normal = jnp.sum(wide(coefs, key_width) * normals, axis=0, keepdims=True)
    out[key_width:, :] = meta_rows(normal, top, whole_decay, doc, width)


def entering_kernel(group, reach, scalars, *refs):
    states, totals, outs = refs[:group], refs[group : group + reach], refs[group + reach :]
    mine = scalars[0]
    key_width, width = outs[0].shape[0] - META, outs[0].shape[1]
    normals, tops, decays, docs = read_meta(states)
    far_normals, far_tops, far_decays, far_docs = read_meta(totals)
    place = jnp.bitwise_xor(iota((group, LANES), 0), mine)
    before = decay_before(mine, place, decays)
    zero = jnp.zeros((1, LANES), F32)
    far_reached, passed, lines = [], zero, []
    for d in range(reach):
        far_reached.append(far_tops[d : d + 1] + passed)
        passed = passed + far_decays[d : d + 1]
    far_reached = jnp.concatenate(far_reached, axis=0)
    for r in range(group):
        here = jnp.bitwise_xor(mine, r)
        doc = jnp.sum(jnp.where(place == here - 1, docs, 0.0), axis=0, keepdims=True)
        doc = jnp.where(here == 0, far_docs[0:1], doc)
        mark = before[r : r + 1]
        alive = (place < here) & (docs == doc)
        reached = jnp.where(alive, tops + (mark - before - decays), FLOOR_NEG)
        far_alive = (far_docs == doc) & (far_docs > 0.5)
        far = jnp.where(far_alive, far_reached + mark, FLOOR_NEG)
        top = jnp.maximum(
            jnp.max(reached, axis=0, keepdims=True), jnp.max(far, axis=0, keepdims=True)
        )
        coefs = jnp.where(alive, jnp.exp(reached - top), 0.0)
        far_coefs = jnp.where(far_alive, jnp.exp(far - top), 0.0)
        lines.append(
            [None if i == r else coefs[i : i + 1] for i in range(group)]
            + [far_coefs[d : d + 1] for d in range(reach)]
        )
        normal = jnp.sum(wide(coefs, key_width) * normals, axis=0, keepdims=True)
        normal = normal + jnp.sum(wide(far_coefs, key_width) * far_normals, axis=0, keepdims=True)
        outs[r][key_width:, :] = meta_rows(normal, top, zero, doc, width)
    weighted(list(states) + list(totals), outs, lines)


def local_kernel(first_slot, heads, scalars, *refs):
    q_own, k_own, v_own, q_oth, k_oth, v_oth, source_rows, decay_rows, columns, docs_ref = refs[:10]
    numerators, stats = refs[-2:]
    mine, core = scalars[0], scalars[1]
    tokens, key_width = q_own.shape[1:]
    length = 2 * tokens
    scaling = key_width**-0.5
    is_first = core == 0
    lane = iota((length, LANES), 1)
    turned = columns[...]
    docs = turned[:, heads : heads + 1]
    source_docs = docs_ref[...]
    causal = iota((tokens, tokens), 0) >= iota((tokens, tokens), 1)
    for step in range(numerators.shape[0]):
        local_head = jnp.bitwise_xor(mine, first_slot + step)
        head = (heads // 2) * core + local_head
        source = source_rows[pl.ds(head, 1), :]
        decay = jnp.sum(jnp.where(lane == head, turned, 0.0), axis=1, keepdims=True)

        def ordered(own, other):
            own, other = own[local_head], other[local_head]
            return jnp.where(is_first, own, other), jnp.where(is_first, other, own)

        queries, keys, values = ordered(q_own, q_oth), ordered(k_own, k_oth), ordered(v_own, v_oth)
        for block in range(2):
            rows = slice(block * tokens, (block + 1) * tokens)
            exponents = []
            for s in range(block + 1):
                cols = slice(s * tokens, (s + 1) * tokens)
                allowed = docs[rows] == source_docs[:, cols]
                if s == block:
                    allowed = allowed & causal
                exponents.append(jnp.where(allowed, decay[rows] + source[:, cols], FLOOR_NEG))
            stabilizer = functools.reduce(
                jnp.maximum, [jnp.max(x, axis=1, keepdims=True) for x in exponents]
            )
            factors, sources, denominator = [], [], None
            for s in range(block + 1):
                weights = dot(queries[block], keys[s], NT) * scaling
                weights = weights * jnp.exp(exponents[s] - stabilizer)
                high = weights.astype(BF16)
                factors.append(high)
                sources.append(values[s])
                if s < block:
                    factors.append((weights - high.astype(F32)).astype(BF16))
                    sources.append(values[s])
                part = jnp.sum(weights, axis=1, keepdims=True)
                denominator = part if s == 0 else denominator + part
            numerator = dot(jnp.concatenate(factors, axis=1), jnp.concatenate(sources, axis=0))
            side = core if block == 0 else 1 - core
            numerators[step, side] = numerator
            first_lane = iota((tokens, LANES), 1) == 0
            pair = jnp.where(first_lane, stabilizer, denominator).T
            stats[step, side] = jnp.concatenate(
                [pair[:2], decay_rows[pl.ds(head, 1), rows], source_docs[:, rows], pair[4:8]], axis=0
            )


def output_kernel(first, count, scalars, q_own, q_oth, *refs):
    terms, entering, (keep, send) = refs[:4], refs[4 : 4 + count], refs[4 + count :]
    key_width = q_own.shape[2]
    scaling = key_width**-0.5
    early = terms[0].shape[0]
    for i, payload in enumerate(entering):
        slot = first + i
        numerators, stats = terms[:2] if slot < early else terms[2:]
        at = slot % early
        local_head = jnp.bitwise_xor(scalars[0], slot)
        normal, top, _, doc = read_meta([payload])
        pieces = split3(normal) + (jnp.zeros((PAD - 3, key_width), F32),)
        pieces = jnp.concatenate(pieces, axis=0).astype(BF16)
        memory = payload[:key_width, :]
        width = memory.shape[1]
        for side, (q_ref, out) in enumerate(((q_own, keep), (q_oth, send))):
            query = q_ref[local_head]
            tokens = query.shape[0]
            stat = stats[at, side]
            local = stat[0:1]
            alive = stat[3:4] == wide(doc, tokens)
            carried = jnp.where(alive, stat[2:3] + wide(top, tokens), FLOOR_NEG)
            stabilizer = jnp.maximum(local, carried)
            shrink = jnp.exp(local - stabilizer)
            retained = jnp.exp(carried - stabilizer) * scaling
            seen = dot(pieces, query, NT)
            seen = (seen[2:3] + seen[1:2]) + seen[0:1]
            denominator = shrink * stat[1:2] + retained * seen
            inverse = 1.0 / jnp.maximum(jnp.abs(denominator), 1.0)
            near = jnp.broadcast_to(shrink * inverse, (LANES, tokens)).T
            far = jnp.broadcast_to(retained * inverse, (LANES, tokens)).T
            result = wide(near, width) * numerators[at, side]
            out[i] = (result + wide(far, width) * dot(query, memory)).astype(BF16)


def merge_kernel(heads, scalars, *refs):
    stacks, (out, result, written) = refs[:-3], refs[-3:]
    half = heads // 2
    n = LAY // heads
    mine, core = scalars[0], scalars[1]
    into, given = iota((LAY, LAY), 0), iota((LAY, LAY), 1)
    index = given // n
    slot = jnp.bitwise_and(index, half - 1)
    side = jnp.where(index < half, core, 1 - core)
    head = side * half + jnp.bitwise_xor(slot, mine)
    order = ((into % heads == head) & (into // heads == given % n)).astype(BF16)
    _, tokens, width = stacks[0].shape
    copies = []
    for g in range(tokens // n):
        span = slice(g * n, (g + 1) * n)
        rows = jnp.concatenate([stack[:, span, :] for stack in stacks], axis=0)
        turned = dot(order, rows.reshape(LAY, width))
        result[span] = turned.reshape(n, heads, width).astype(BF16)
        copies.append(pltpu.make_async_copy(result.at[span], out.at[span], written.at[g]))
        copies[-1].start()
    for copy in copies:
        copy.wait()


def whole(shape):
    return pl.BlockSpec(shape, lambda *_: (0,) * len(shape))


def params():
    return pltpu.CompilerParams(vmem_limit_bytes=16 * 2**20)


SMEM = pl.BlockSpec(memory_space=pltpu.SMEM)
VMEM = pl.BlockSpec(memory_space=pltpu.VMEM)


def shape_of(*dims, dtype=BF16):
    return jax.ShapeDtypeStruct(dims, dtype)


def local(devices, queries, key_vectors, value_vectors, input_gate, forget_gate, doc_ids):
    tokens, heads, key_width = queries.shape
    value_width = value_vectors.shape[2]
    half = heads // 2
    group = half
    chips = devices // 2
    levels = chips // group
    reach = max(1, levels // 2)
    ctx, hv = lax.axis_index("ctx"), lax.axis_index("hv")
    chip = ctx * (lax.axis_size("hv") // 2) + hv // 2
    scalars = jnp.stack([chip % group, hv % 2]).astype(jnp.int32)
    ids = doc_ids[None, :]

    def swap_cores(x):
        return lax.ppermute(x, AXES, [(d, d ^ 1) for d in range(devices)])

    def in_group(x, r):
        pairs = [(d, d ^ (2 * r)) for d in range(devices)]
        return lax.ppermute(x, AXES, pairs)

    def to_next(x):
        jump = 2 * group
        return lax.ppermute(x, AXES, [(d, d + jump) for d in range(devices - jump)])

    rows = key_width + META
    state = (rows, value_width)
    sizes = {key_width: (half, tokens, key_width), value_width: (half, tokens, value_width)}

    def relayout(source):
        size = sizes[source.shape[2]]
        return pl.pallas_call(
            functools.partial(relayout_kernel, half),
            in_specs=[pl.BlockSpec(memory_space=pl.ANY)],
            out_specs=[VMEM] * 2,
            out_shape=[shape_of(*size)] * 2,
            scratch_shapes=[
                pltpu.VMEM(source.shape, BF16),
                pltpu.SemaphoreType.DMA((tokens // (LAY // heads),)),
            ],
            compiler_params=params(),
            name="relayout",
        )(source)

    gates = jnp.concatenate([input_gate.T, forget_gate.T], axis=0)
    gates_oth = swap_cores(gates)
    v_keep, v_send = relayout(value_vectors)
    gates_oth, v_send = lax.optimization_barrier((gates_oth, v_send))
    v_oth = swap_cores(v_send)
    k_keep, k_send = relayout(key_vectors)
    k_oth = swap_cores(k_send)
    gate_shapes = [
        (heads, 2 * tokens),
        (heads, LANES),
        (heads, LANES),
        (heads, 2 * tokens),
        (heads, 2 * tokens),
        (2 * tokens, LANES),
        (1, 2 * tokens),
    ]
    factors, tops, decays, source_rows, decay_rows, columns, docs = pl.pallas_call(
        functools.partial(gates_kernel, heads),
        in_specs=[SMEM, VMEM, VMEM, VMEM],
        out_specs=[VMEM] * len(gate_shapes),
        out_shape=[shape_of(*s, dtype=F32) for s in gate_shapes],
        compiler_params=params(),
        name="gates",
    )(scalars, gates, gates_oth, ids)

    by_core = (k_keep, v_keep, k_oth, v_oth, factors, tops, decays, docs)
    made = pl.pallas_call(
        functools.partial(state_kernel, heads),
        in_specs=[SMEM] + [VMEM] * len(by_core),
        out_specs=[VMEM] * group,
        out_shape=[shape_of(*state)] * group,
        compiler_params=params(),
        name="states",
    )(scalars, *by_core)
    gathered = [made[0]] + [in_group(made[r], r) for r in range(1, group)]
    total = pl.pallas_call(
        functools.partial(total_kernel, group),
        in_specs=[SMEM] + [VMEM] * group,
        out_specs=VMEM,
        out_shape=shape_of(*state),
        compiler_params=params(),
        name="group_total",
    )(scalars, *gathered)
    queries, gathered[0] = lax.optimization_barrier((queries, gathered[0]))
    q_keep, q_send = relayout(queries)
    q_oth = swap_cores(q_send)
    small = (source_rows, decay_rows, columns, docs)
    early = half // 2

    def own_terms(first_slot, q_own):
        operands = (q_own, k_keep, v_keep, q_oth, k_oth, v_oth, *small)
        return pl.pallas_call(
            functools.partial(local_kernel, first_slot, heads),
            in_specs=[SMEM] + [VMEM] * len(operands),
            out_specs=[VMEM] * 2,
            out_shape=[
                shape_of(early, 2, tokens, value_width, dtype=F32),
                shape_of(early, 2, 8, tokens, dtype=F32),
            ],
            compiler_params=params(),
            name="own_terms",
        )(scalars, *operands)

    q_first, _ = lax.optimization_barrier((q_keep, total))
    first_terms = own_terms(0, q_first)
    totals = [to_next(total)]
    totals[0], first_terms = lax.optimization_barrier((totals[0], first_terms))
    while len(totals) < reach:
        totals.append(to_next(totals[-1]))
    q_last, _ = lax.optimization_barrier((q_keep, totals[0]))
    last_terms = own_terms(early, q_last)
    gathered[0], last_terms = lax.optimization_barrier((gathered[0], last_terms))
    terms = [*first_terms, *last_terms]

    leaving = pl.pallas_call(
        functools.partial(entering_kernel, group, reach),
        in_specs=[SMEM] + [VMEM] * (group + reach),
        out_specs=[VMEM] * group,
        out_shape=[shape_of(*state)] * group,
        compiler_params=params(),
        name="entering",
    )(scalars, *gathered, *totals)
    entering = [leaving[0]] + [in_group(leaving[r], r) for r in range(1, group)]

    def outputs(first, count):
        return pl.pallas_call(
            functools.partial(output_kernel, first, count),
            in_specs=[SMEM] + [VMEM] * (6 + count),
            out_specs=[VMEM] * 2,
            out_shape=[shape_of(count, tokens, value_width)] * 2,
            compiler_params=params(),
            name="outputs",
        )(scalars, q_keep, q_oth, *terms, *entering[first : first + count])

    kept, received = [], []
    for r in range(group):
        keep, send = outputs(r, 1)
        kept.append(keep)
        received.append(swap_cores(send))
        if r == 0:
            terms, received[0] = lax.optimization_barrier((terms, received[0]))
        else:
            terms, _ = lax.optimization_barrier((terms, send))
    return pl.pallas_call(
        functools.partial(merge_kernel, heads),
        in_specs=[SMEM] + [VMEM] * heads,
        out_specs=pl.BlockSpec(memory_space=pl.ANY),
        out_shape=shape_of(*value_vectors.shape),
        scratch_shapes=[
            pltpu.VMEM(value_vectors.shape, BF16),
            pltpu.SemaphoreType.DMA((tokens // (LAY // heads),)),
        ],
        compiler_params=params(),
        name="merge",
    )(scalars, *kept, *received)


def solution(mesh):
    return jax.shard_map(
        functools.partial(local, mesh.size),
        mesh=mesh,
        in_specs=(
            P(AXES, None, None),
            P(AXES, None, None),
            P(AXES, None, None),
            P(AXES, None),
            P(AXES, None),
            P("ctx"),
        ),
        out_specs=P(AXES, None, None),
        check_vma=False,
    )
```

```python
import functools

import jax
import jax.numpy as jnp
from jax import lax
from jax.experimental import pallas as pl
from jax.experimental.pallas import tpu as pltpu
from jax.sharding import PartitionSpec as P

AXES = ("ctx", "hv")
FLOOR_NEG = -1e30
META = 8
PAD = 16
LANES = 128
LAY = 256
F32, BF16 = jnp.float32, jnp.bfloat16

NN = (((1,), (0,)), ((), ()))
NT = (((1,), (1,)), ((), ()))


def dot(a, b, dims=NN):
    return lax.dot_general(a, b, dims, preferred_element_type=F32)


def split3(x):
    hi = x.astype(BF16).astype(F32)
    mid = (x - hi).astype(BF16).astype(F32)
    return hi, mid, (x - hi - mid).astype(BF16).astype(F32)


def iota(shape, dim):
    return lax.broadcasted_iota(jnp.int32, shape, dim)


def meta_rows(normalizer, top, decay, doc, width):
    used = normalizer.shape[1]
    row = iota((META, used), 0)
    rows = jnp.where(row == 6, wide(doc, used), 0.0)
    lines = split3(normalizer) + split3(jnp.concatenate([top, decay], axis=1))
    for index, line in enumerate(lines):
        rows = jnp.where(row == index, line, rows)
    spare = jnp.zeros((META, width - used), F32)
    return jnp.concatenate([rows, spare], axis=1).astype(BF16)


def read_meta(refs):
    key_width = refs[0].shape[0] - META
    rows = [ref[key_width:, : 2 * LANES].astype(F32) for ref in refs]
    normals = jnp.concatenate([(x[2:3] + x[1:2]) + x[0:1] for x in rows], axis=0)
    line = jnp.concatenate([(x[5:6] + x[4:5]) + x[3:4] for x in rows], axis=0)
    docs = jnp.concatenate([x[6:7, :LANES] for x in rows], axis=0)
    return normals, line[:, :LANES], line[:, LANES:], docs


def wide(x, width):
    return jnp.concatenate([x] * (width // LANES), axis=1)


CHUNK = 32


def weighted(refs, outs, coefs):
    key_width, width = refs[0].shape[0] - META, refs[0].shape[1]
    coefs = [[None if c is None else wide(c, width) for c in line] for line in coefs]
    for start in range(0, key_width, CHUNK):
        rows = slice(start, start + CHUNK)
        parts = [ref[rows, :].astype(F32) for ref in refs]
        for out, line in zip(outs, coefs, strict=True):
            terms = [c * part for c, part in zip(line, parts, strict=True) if c is not None]
            out[rows, :] = functools.reduce(jnp.add, terms).astype(BF16)


def gate_rows(core, own_ref, other_ref, heads):
    own, other = own_ref[...].astype(F32), other_ref[...].astype(F32)
    both = jnp.concatenate(
        [jnp.where(core == 0, own, other), jnp.where(core == 0, other, own)], axis=1
    )
    gate_in, forget = both[:heads], both[heads:]
    log_forget = jnp.minimum(forget, 0.0) - jnp.log1p(jnp.exp(-jnp.abs(forget)))
    length = both.shape[1]
    upto = (iota((length, length), 0) <= iota((length, length), 1)).astype(BF16)
    pieces = dot(jnp.concatenate(split3(log_forget), axis=0).astype(BF16), upto)
    decay = (pieces[2 * heads :] + pieces[heads : 2 * heads]) + pieces[:heads]
    return gate_in, decay


def by_head_order(heads):
    n = LAY // heads
    out, inside = iota((LAY, LAY), 0), iota((LAY, LAY), 1)
    return ((inside % heads == out // n) & (inside // heads == out % n)).astype(BF16)


def relayout_kernel(half, count, *refs):
    sources, outs = refs[:count], refs[count:]
    heads = 2 * half
    n = LAY // heads
    core = lax.axis_index("hv") % 2
    order = by_head_order(heads)
    for index, source in enumerate(sources):
        keep, send = outs[index], outs[count + index]
        tokens, _, width = source.shape
        for g in range(tokens // n):
            span = slice(g * n, (g + 1) * n)
            rows = dot(order, source[span].reshape(LAY, width)).astype(BF16)
            rows = rows.reshape(heads, n, width)
            keep[:, span, :] = jnp.where(core == 0, rows[:half], rows[half:])
            send[:, span, :] = jnp.where(core == 0, rows[half:], rows[:half])


def gates_kernel(heads, scalars, g_own, g_oth, ids_ref, *outs):
    factors, tops, decays, source_rows, decay_rows, columns, docs_row = outs
    core = scalars[1]
    length = factors.shape[1]
    gate_in, decay = gate_rows(core, g_own, g_oth, heads)
    chip = lax.axis_index("hv") // 2
    ids = ids_ref[:, pl.ds(pl.multiple_of(chip * length, length), length)]
    exponent = decay[:, length - 1 :] - decay + gate_in
    exponent = jnp.where(ids == ids[:, length - 1 :], exponent, FLOOR_NEG)
    top = jnp.max(exponent, axis=1, keepdims=True)
    factors[...] = jnp.exp(exponent - top)
    tops[...] = jnp.broadcast_to(top, tops.shape)
    decays[...] = jnp.broadcast_to(decay[:, length - 1 :], decays.shape)
    source_rows[...] = gate_in - decay
    decay_rows[...] = decay
    docs = ids.astype(F32) + 1.0
    docs_row[...] = docs
    filler = jnp.zeros((LANES - heads - 1, length), F32)
    columns[...] = jnp.concatenate([decay, docs, filler], axis=0).T


def state_kernel(heads, scalars, *refs):
    k_own, v_own, k_oth, v_oth, factors, tops, decays, docs_ref = refs[:8]
    outs = refs[8:]
    mine, core = scalars[0], scalars[1]
    tokens, key_width = k_own.shape[1:]
    length = 2 * tokens
    doc = jnp.broadcast_to(docs_ref[:, length - 1 :], (1, LANES))
    for slot in range(len(outs) - 1, -1, -1):
        out = outs[slot]
        local_head = jnp.bitwise_xor(mine, slot)
        head = (heads // 2) * core + local_head
        row = factors[pl.ds(head, 1), :]
        first, last = row[:, :tokens], row[:, tokens:]
        high, low, values, normal = [], [], [], None
        for k_ref, v_ref, f in (
            (k_own, v_own, jnp.where(core == 0, first, last)),
            (k_oth, v_oth, jnp.where(core == 0, last, first)),
        ):
            keys = k_ref[local_head]
            scaled = keys.astype(F32).T * f
            high.append(scaled.astype(BF16))
            low.append((scaled - high[-1].astype(F32)).astype(BF16))
            values.append(v_ref[local_head])
            pieces = jnp.concatenate(split3(f) + (jnp.zeros((PAD - 3, tokens), F32),), axis=0)
            sums = dot(pieces.astype(BF16), keys)
            line = (sums[2:3] + sums[1:2]) + sums[0:1]
            normal = line if normal is None else normal + line
        total = dot(jnp.concatenate(low + high, axis=1), jnp.concatenate(values * 2, axis=0))
        out[:key_width, :] = total.astype(BF16)
        out[key_width:, :] = meta_rows(
            normal, tops[pl.ds(head, 1), :], decays[pl.ds(head, 1), :], doc, out.shape[1]
        )


def decay_before(mine, place, decays):
    group = decays.shape[0]
    before = jnp.zeros_like(decays)
    for i in range(group):
        before = before + jnp.where(place > jnp.bitwise_xor(mine, i), decays[i : i + 1], 0.0)
    return before


def total_kernel(group, scalars, *refs):
    states, out = refs[:group], refs[group]
    mine = scalars[0]
    key_width, width = out.shape[0] - META, out.shape[1]
    normals, tops, decays, docs = read_meta(states)
    place = jnp.bitwise_xor(iota((group, LANES), 0), mine)
    whole_decay = jnp.sum(decays, axis=0, keepdims=True)
    after = whole_decay - decay_before(mine, place, decays) - decays
    doc = jnp.sum(jnp.where(place == group - 1, docs, 0.0), axis=0, keepdims=True)
    alive = docs == doc
    reached = jnp.where(alive, tops + after, FLOOR_NEG)
    top = jnp.max(reached, axis=0, keepdims=True)
    coefs = jnp.where(alive, jnp.exp(reached - top), 0.0)
    weighted(states, [out], [[coefs[i : i + 1] for i in range(group)]])
    normal = jnp.sum(wide(coefs, key_width) * normals, axis=0, keepdims=True)
    out[key_width:, :] = meta_rows(normal, top, whole_decay, doc, width)


def entering_kernel(group, reach, scalars, *refs):
    states, totals, outs = refs[:group], refs[group : group + reach], refs[group + reach :]
    mine = scalars[0]
    key_width, width = outs[0].shape[0] - META, outs[0].shape[1]
    normals, tops, decays, docs = read_meta(states)
    far_normals, far_tops, far_decays, far_docs = read_meta(totals)
    place = jnp.bitwise_xor(iota((group, LANES), 0), mine)
    before = decay_before(mine, place, decays)
    zero = jnp.zeros((1, LANES), F32)
    far_reached, passed, lines = [], zero, []
    for d in range(reach):
        far_reached.append(far_tops[d : d + 1] + passed)
        passed = passed + far_decays[d : d + 1]
    far_reached = jnp.concatenate(far_reached, axis=0)
    for r in range(group):
        here = jnp.bitwise_xor(mine, r)
        doc = jnp.sum(jnp.where(place == here - 1, docs, 0.0), axis=0, keepdims=True)
        doc = jnp.where(here == 0, far_docs[0:1], doc)
        mark = before[r : r + 1]
        alive = (place < here) & (docs == doc)
        reached = jnp.where(alive, tops + (mark - before - decays), FLOOR_NEG)
        far_alive = (far_docs == doc) & (far_docs > 0.5)
        far = jnp.where(far_alive, far_reached + mark, FLOOR_NEG)
        top = jnp.maximum(
            jnp.max(reached, axis=0, keepdims=True), jnp.max(far, axis=0, keepdims=True)
        )
        coefs = jnp.where(alive, jnp.exp(reached - top), 0.0)
        far_coefs = jnp.where(far_alive, jnp.exp(far - top), 0.0)
        lines.append(
            [None if i == r else coefs[i : i + 1] for i in range(group)]
            + [far_coefs[d : d + 1] for d in range(reach)]
        )
        normal = jnp.sum(wide(coefs, key_width) * normals, axis=0, keepdims=True)
        normal = normal + jnp.sum(wide(far_coefs, key_width) * far_normals, axis=0, keepdims=True)
        outs[r][key_width:, :] = meta_rows(normal, top, zero, doc, width)
    weighted(list(states) + list(totals), outs, lines)


def local_kernel(first_slot, heads, scalars, *refs):
    q_own, k_own, v_own, q_oth, k_oth, v_oth, source_rows, decay_rows, columns, docs_ref = refs[:10]
    numerators, stats = refs[-2:]
    mine, core = scalars[0], scalars[1]
    tokens, key_width = q_own.shape[1:]
    length = 2 * tokens
    scaling = key_width**-0.5
    is_first = core == 0
    lane = iota((length, LANES), 1)
    turned = columns[...]
    docs = turned[:, heads : heads + 1]
    source_docs = docs_ref[...]
    causal = iota((tokens, tokens), 0) >= iota((tokens, tokens), 1)
    for step in range(numerators.shape[0]):
        local_head = jnp.bitwise_xor(mine, first_slot + step)
        head = (heads // 2) * core + local_head
        source = source_rows[pl.ds(head, 1), :]
        decay = jnp.sum(jnp.where(lane == head, turned, 0.0), axis=1, keepdims=True)

        def ordered(own, other):
            own, other = own[local_head], other[local_head]
            return jnp.where(is_first, own, other), jnp.where(is_first, other, own)

        queries, keys, values = ordered(q_own, q_oth), ordered(k_own, k_oth), ordered(v_own, v_oth)
        for block in range(2):
            rows = slice(block * tokens, (block + 1) * tokens)
            exponents = []
            for s in range(block + 1):
                cols = slice(s * tokens, (s + 1) * tokens)
                allowed = docs[rows] == source_docs[:, cols]
                if s == block:
                    allowed = allowed & causal
                exponents.append(jnp.where(allowed, decay[rows] + source[:, cols], FLOOR_NEG))
            stabilizer = functools.reduce(
                jnp.maximum, [jnp.max(x, axis=1, keepdims=True) for x in exponents]
            )
            factors, sources, denominator = [], [], None
            for s in range(block + 1):
                weights = dot(queries[block], keys[s], NT) * scaling
                weights = weights * jnp.exp(exponents[s] - stabilizer)
                high = weights.astype(BF16)
                factors.append(high)
                sources.append(values[s])
                if s < block:
                    factors.append((weights - high.astype(F32)).astype(BF16))
                    sources.append(values[s])
                part = jnp.sum(weights, axis=1, keepdims=True)
                denominator = part if s == 0 else denominator + part
            numerator = dot(jnp.concatenate(factors, axis=1), jnp.concatenate(sources, axis=0))
            side = core if block == 0 else 1 - core
            numerators[step, side] = numerator
            first_lane = iota((tokens, LANES), 1) == 0
            pair = jnp.where(first_lane, stabilizer, denominator).T
            stats[step, side] = jnp.concatenate(
                [pair[:2], decay_rows[pl.ds(head, 1), rows], source_docs[:, rows], pair[4:8]], axis=0
            )


def output_kernel(first, count, scalars, q_own, q_oth, *refs):
    terms, entering, (keep, send) = refs[:4], refs[4 : 4 + count], refs[4 + count :]
    key_width = q_own.shape[2]
    scaling = key_width**-0.5
    early = terms[0].shape[0]
    for i, payload in enumerate(entering):
        slot = first + i
        numerators, stats = terms[:2] if slot < early else terms[2:]
        at = slot % early
        local_head = jnp.bitwise_xor(scalars[0], slot)
        normal, top, _, doc = read_meta([payload])
        pieces = split3(normal) + (jnp.zeros((PAD - 3, key_width), F32),)
        pieces = jnp.concatenate(pieces, axis=0).astype(BF16)
        memory = payload[:key_width, :]
        width = memory.shape[1]
        for side, (q_ref, out) in enumerate(((q_own, keep), (q_oth, send))):
            query = q_ref[local_head]
            tokens = query.shape[0]
            stat = stats[at, side]
            local = stat[0:1]
            alive = stat[3:4] == wide(doc, tokens)
            carried = jnp.where(alive, stat[2:3] + wide(top, tokens), FLOOR_NEG)
            stabilizer = jnp.maximum(local, carried)
            shrink = jnp.exp(local - stabilizer)
            retained = jnp.exp(carried - stabilizer) * scaling
            seen = dot(pieces, query, NT)
            seen = (seen[2:3] + seen[1:2]) + seen[0:1]
            denominator = shrink * stat[1:2] + retained * seen
            inverse = 1.0 / jnp.maximum(jnp.abs(denominator), 1.0)
            near = jnp.broadcast_to(shrink * inverse, (LANES, tokens)).T
            far = jnp.broadcast_to(retained * inverse, (LANES, tokens)).T
            result = wide(near, width) * numerators[at, side]
            out[i] = (result + wide(far, width) * dot(query, memory)).astype(BF16)


def merge_kernel(heads, scalars, *refs):
    stacks, (out, result, written) = refs[:-3], refs[-3:]
    half = heads // 2
    n = LAY // heads
    mine, core = scalars[0], scalars[1]
    into, given = iota((LAY, LAY), 0), iota((LAY, LAY), 1)
    index = given // n
    slot = jnp.bitwise_and(index, half - 1)
    side = jnp.where(index < half, core, 1 - core)
    head = side * half + jnp.bitwise_xor(slot, mine)
    order = ((into % heads == head) & (into // heads == given % n)).astype(BF16)
    _, tokens, width = stacks[0].shape
    copies = []
    for g in range(tokens // n):
        span = slice(g * n, (g + 1) * n)
        rows = jnp.concatenate([stack[:, span, :] for stack in stacks], axis=0)
        turned = dot(order, rows.reshape(LAY, width))
        result[span] = turned.reshape(n, heads, width).astype(BF16)
        copies.append(pltpu.make_async_copy(result.at[span], out.at[span], written.at[g]))
        copies[-1].start()
    for copy in copies:
        copy.wait()


def whole(shape):
    return pl.BlockSpec(shape, lambda *_: (0,) * len(shape))


def params():
    return pltpu.CompilerParams(vmem_limit_bytes=16 * 2**20)


SMEM = pl.BlockSpec(memory_space=pltpu.SMEM)
VMEM = pl.BlockSpec(memory_space=pltpu.VMEM)


def shape_of(*dims, dtype=BF16):
    return jax.ShapeDtypeStruct(dims, dtype)


def local(devices, queries, key_vectors, value_vectors, input_gate, forget_gate, doc_ids):
    tokens, heads, key_width = queries.shape
    value_width = value_vectors.shape[2]
    half = heads // 2
    group = half
    chips = devices // 2
    levels = chips // group
    reach = max(1, levels // 2)
    ctx, hv = lax.axis_index("ctx"), lax.axis_index("hv")
    chip = ctx * (lax.axis_size("hv") // 2) + hv // 2
    scalars = jnp.stack([chip % group, hv % 2]).astype(jnp.int32)
    ids = doc_ids[None, :]

    def swap_cores(x):
        return lax.ppermute(x, AXES, [(d, d ^ 1) for d in range(devices)])

    def in_group(x, r):
        pairs = [(d, d ^ (2 * r)) for d in range(devices)]
        return lax.ppermute(x, AXES, pairs)

    def to_next(x):
        jump = 2 * group
        return lax.ppermute(x, AXES, [(d, d + jump) for d in range(devices - jump)])

    rows = key_width + META
    state = (rows, value_width)
    sizes = {key_width: (half, tokens, key_width), value_width: (half, tokens, value_width)}

    def relayout(*sources):
        outs = [sizes[x.shape[2]] for x in sources] * 2
        return pl.pallas_call(
            functools.partial(relayout_kernel, half, len(sources)),
            in_specs=[whole(x.shape) for x in sources],
            out_specs=[VMEM] * len(outs),
            out_shape=[shape_of(*s) for s in outs],
            compiler_params=params(),
                name="relayout",
        )(*sources)

    gates = jnp.concatenate([input_gate.T, forget_gate.T], axis=0)
    gates, value_vectors = lax.optimization_barrier((gates, value_vectors))
    gates_oth = swap_cores(gates)
    v_keep, v_send = relayout(value_vectors)
    gates_oth, v_send = lax.optimization_barrier((gates_oth, v_send))
    v_oth = swap_cores(v_send)
    k_keep, k_send = relayout(key_vectors)
    k_oth = swap_cores(k_send)
    gate_shapes = [
        (heads, 2 * tokens),
        (heads, LANES),
        (heads, LANES),
        (heads, 2 * tokens),
        (heads, 2 * tokens),
        (2 * tokens, LANES),
        (1, 2 * tokens),
    ]
    factors, tops, decays, source_rows, decay_rows, columns, docs = pl.pallas_call(
        functools.partial(gates_kernel, heads),
        in_specs=[SMEM, VMEM, VMEM, VMEM],
        out_specs=[VMEM] * len(gate_shapes),
        out_shape=[shape_of(*s, dtype=F32) for s in gate_shapes],
        compiler_params=params(),
        name="gates",
    )(scalars, gates, gates_oth, ids)

    by_core = (k_keep, v_keep, k_oth, v_oth, factors, tops, decays, docs)
    made = pl.pallas_call(
        functools.partial(state_kernel, heads),
        in_specs=[SMEM] + [VMEM] * len(by_core),
        out_specs=[VMEM] * group,
        out_shape=[shape_of(*state)] * group,
        compiler_params=params(),
        name="states",
    )(scalars, *by_core)
    gathered = [made[0]] + [in_group(made[r], r) for r in range(1, group)]
    total = pl.pallas_call(
        functools.partial(total_kernel, group),
        in_specs=[SMEM] + [VMEM] * group,
        out_specs=VMEM,
        out_shape=shape_of(*state),
        compiler_params=params(),
        name="group_total",
    )(scalars, *gathered)
    queries, gathered[0] = lax.optimization_barrier((queries, gathered[0]))
    q_keep, q_send = relayout(queries)
    q_oth = swap_cores(q_send)
    small = (source_rows, decay_rows, columns, docs)
    early = half // 2

    def own_terms(first_slot, q_own):
        operands = (q_own, k_keep, v_keep, q_oth, k_oth, v_oth, *small)
        return pl.pallas_call(
            functools.partial(local_kernel, first_slot, heads),
            in_specs=[SMEM] + [VMEM] * len(operands),
            out_specs=[VMEM] * 2,
            out_shape=[
                shape_of(early, 2, tokens, value_width, dtype=F32),
                shape_of(early, 2, 8, tokens, dtype=F32),
            ],
            compiler_params=params(),
            name="own_terms",
        )(scalars, *operands)

    q_first, _ = lax.optimization_barrier((q_keep, total))
    first_terms = own_terms(0, q_first)
    totals = [to_next(total)]
    totals[0], first_terms = lax.optimization_barrier((totals[0], first_terms))
    while len(totals) < reach:
        totals.append(to_next(totals[-1]))
    q_last, _ = lax.optimization_barrier((q_keep, totals[0]))
    last_terms = own_terms(early, q_last)
    gathered[0], last_terms = lax.optimization_barrier((gathered[0], last_terms))
    terms = [*first_terms, *last_terms]

    leaving = pl.pallas_call(
        functools.partial(entering_kernel, group, reach),
        in_specs=[SMEM] + [VMEM] * (group + reach),
        out_specs=[VMEM] * group,
        out_shape=[shape_of(*state)] * group,
        compiler_params=params(),
        name="entering",
    )(scalars, *gathered, *totals)
    entering = [leaving[0]] + [in_group(leaving[r], r) for r in range(1, group)]

    def outputs(first, count):
        return pl.pallas_call(
            functools.partial(output_kernel, first, count),
            in_specs=[SMEM] + [VMEM] * (6 + count),
            out_specs=[VMEM] * 2,
            out_shape=[shape_of(count, tokens, value_width)] * 2,
            compiler_params=params(),
            name="outputs",
        )(scalars, q_keep, q_oth, *terms, *entering[first : first + count])

    kept, received = [], []
    for r in range(group):
        keep, send = outputs(r, 1)
        kept.append(keep)
        received.append(swap_cores(send))
        if r == 0:
            terms, received[0] = lax.optimization_barrier((terms, received[0]))
        else:
            terms, _ = lax.optimization_barrier((terms, send))
    return pl.pallas_call(
        functools.partial(merge_kernel, heads),
        in_specs=[SMEM] + [VMEM] * heads,
        out_specs=pl.BlockSpec(memory_space=pl.ANY),
        out_shape=shape_of(*value_vectors.shape),
        scratch_shapes=[
            pltpu.VMEM(value_vectors.shape, BF16),
            pltpu.SemaphoreType.DMA((tokens // (LAY // heads),)),
        ],
        compiler_params=params(),
        name="merge",
    )(scalars, *kept, *received)


def solution(mesh):
    return jax.shard_map(
        functools.partial(local, mesh.size),
        mesh=mesh,
        in_specs=(
            P(AXES, None, None),
            P(AXES, None, None),
            P(AXES, None, None),
            P(AXES, None),
            P(AXES, None),
            P("ctx"),
        ),
        out_specs=P(AXES, None, None),
        check_vma=False,
    )
```

```python
import functools

import jax
import jax.numpy as jnp
from jax import lax
from jax.experimental import pallas as pl
from jax.experimental.pallas import tpu as pltpu
from jax.sharding import PartitionSpec as P

AXES = ("ctx", "hv")
FLOOR_NEG = -1e30
META = 8
PAD = 16
LANES = 128
LAY = 256
F32, BF16 = jnp.float32, jnp.bfloat16

NN = (((1,), (0,)), ((), ()))
NT = (((1,), (1,)), ((), ()))


def dot(a, b, dims=NN):
    return lax.dot_general(a, b, dims, preferred_element_type=F32)


def split3(x):
    hi = x.astype(BF16).astype(F32)
    mid = (x - hi).astype(BF16).astype(F32)
    return hi, mid, (x - hi - mid).astype(BF16).astype(F32)


def iota(shape, dim):
    return lax.broadcasted_iota(jnp.int32, shape, dim)


def meta_rows(normalizer, top, decay, doc, width):
    used = normalizer.shape[1]
    row = iota((META, used), 0)
    rows = jnp.where(row == 6, wide(doc, used), 0.0)
    lines = split3(normalizer) + split3(jnp.concatenate([top, decay], axis=1))
    for index, line in enumerate(lines):
        rows = jnp.where(row == index, line, rows)
    spare = jnp.zeros((META, width - used), F32)
    return jnp.concatenate([rows, spare], axis=1).astype(BF16)


def read_meta(refs):
    key_width = refs[0].shape[0] - META
    rows = [ref[key_width:, : 2 * LANES].astype(F32) for ref in refs]
    normals = jnp.concatenate([(x[2:3] + x[1:2]) + x[0:1] for x in rows], axis=0)
    line = jnp.concatenate([(x[5:6] + x[4:5]) + x[3:4] for x in rows], axis=0)
    docs = jnp.concatenate([x[6:7, :LANES] for x in rows], axis=0)
    return normals, line[:, :LANES], line[:, LANES:], docs


def wide(x, width):
    return jnp.concatenate([x] * (width // LANES), axis=1)


CHUNK = 32


def weighted(refs, outs, coefs):
    key_width, width = refs[0].shape[0] - META, refs[0].shape[1]
    coefs = [[None if c is None else wide(c, width) for c in line] for line in coefs]
    for start in range(0, key_width, CHUNK):
        rows = slice(start, start + CHUNK)
        parts = [ref[rows, :].astype(F32) for ref in refs]
        for out, line in zip(outs, coefs, strict=True):
            terms = [c * part for c, part in zip(line, parts, strict=True) if c is not None]
            out[rows, :] = functools.reduce(jnp.add, terms).astype(BF16)


def gate_rows(core, own_ref, other_ref, heads):
    own, other = own_ref[...].astype(F32), other_ref[...].astype(F32)
    both = jnp.concatenate(
        [jnp.where(core == 0, own, other), jnp.where(core == 0, other, own)], axis=1
    )
    gate_in, forget = both[:heads], both[heads:]
    log_forget = jnp.minimum(forget, 0.0) - jnp.log1p(jnp.exp(-jnp.abs(forget)))
    length = both.shape[1]
    upto = (iota((length, length), 0) <= iota((length, length), 1)).astype(BF16)
    pieces = dot(jnp.concatenate(split3(log_forget), axis=0).astype(BF16), upto)
    decay = (pieces[2 * heads :] + pieces[heads : 2 * heads]) + pieces[:heads]
    return gate_in, decay


def by_head_order(heads):
    n = LAY // heads
    out, inside = iota((LAY, LAY), 0), iota((LAY, LAY), 1)
    return ((inside % heads == out // n) & (inside // heads == out % n)).astype(BF16)


def relayout_kernel(half, count, *refs):
    sources, outs = refs[:count], refs[count:]
    heads = 2 * half
    n = LAY // heads
    core = lax.axis_index("hv") % 2
    order = by_head_order(heads)
    for index, source in enumerate(sources):
        keep, send = outs[index], outs[count + index]
        tokens, _, width = source.shape
        for g in range(tokens // n):
            span = slice(g * n, (g + 1) * n)
            rows = dot(order, source[span].reshape(LAY, width)).astype(BF16)
            rows = rows.reshape(heads, n, width)
            keep[:, span, :] = jnp.where(core == 0, rows[:half], rows[half:])
            send[:, span, :] = jnp.where(core == 0, rows[half:], rows[:half])


def gates_kernel(heads, scalars, g_own, g_oth, ids_ref, *outs):
    factors, tops, decays, source_rows, decay_rows, columns, docs_row = outs
    core = scalars[1]
    length = factors.shape[1]
    gate_in, decay = gate_rows(core, g_own, g_oth, heads)
    chip = lax.axis_index("hv") // 2
    ids = ids_ref[:, pl.ds(pl.multiple_of(chip * length, length), length)]
    exponent = decay[:, length - 1 :] - decay + gate_in
    exponent = jnp.where(ids == ids[:, length - 1 :], exponent, FLOOR_NEG)
    top = jnp.max(exponent, axis=1, keepdims=True)
    factors[...] = jnp.exp(exponent - top)
    tops[...] = jnp.broadcast_to(top, tops.shape)
    decays[...] = jnp.broadcast_to(decay[:, length - 1 :], decays.shape)
    source_rows[...] = gate_in - decay
    decay_rows[...] = decay
    docs = ids.astype(F32) + 1.0
    docs_row[...] = docs
    filler = jnp.zeros((LANES - heads - 1, length), F32)
    columns[...] = jnp.concatenate([decay, docs, filler], axis=0).T


def state_kernel(heads, slots, scalars, *refs):
    k_own, v_own, k_oth, v_oth, factors, tops, decays, docs_ref = refs[:8]
    outs = refs[8:]
    mine, core = scalars[0], scalars[1]
    tokens, key_width = k_own.shape[1:]
    length = 2 * tokens
    doc = jnp.broadcast_to(docs_ref[:, length - 1 :], (1, LANES))
    for slot, out in zip(slots, outs, strict=True):
        local_head = jnp.bitwise_xor(mine, slot)
        head = (heads // 2) * core + local_head
        row = factors[pl.ds(head, 1), :]
        first, last = row[:, :tokens], row[:, tokens:]
        high, low, values, normal = [], [], [], None
        for k_ref, v_ref, f in (
            (k_own, v_own, jnp.where(core == 0, first, last)),
            (k_oth, v_oth, jnp.where(core == 0, last, first)),
        ):
            keys = k_ref[local_head]
            scaled = keys.astype(F32).T * f
            high.append(scaled.astype(BF16))
            low.append((scaled - high[-1].astype(F32)).astype(BF16))
            values.append(v_ref[local_head])
            pieces = jnp.concatenate(split3(f) + (jnp.zeros((PAD - 3, tokens), F32),), axis=0)
            sums = dot(pieces.astype(BF16), keys)
            line = (sums[2:3] + sums[1:2]) + sums[0:1]
            normal = line if normal is None else normal + line
        total = dot(jnp.concatenate(low + high, axis=1), jnp.concatenate(values * 2, axis=0))
        out[:key_width, :] = total.astype(BF16)
        out[key_width:, :] = meta_rows(
            normal, tops[pl.ds(head, 1), :], decays[pl.ds(head, 1), :], doc, out.shape[1]
        )


def decay_before(mine, place, decays):
    group = decays.shape[0]
    before = jnp.zeros_like(decays)
    for i in range(group):
        before = before + jnp.where(place > jnp.bitwise_xor(mine, i), decays[i : i + 1], 0.0)
    return before


def total_kernel(group, scalars, *refs):
    states, out = refs[:group], refs[group]
    mine = scalars[0]
    key_width, width = out.shape[0] - META, out.shape[1]
    normals, tops, decays, docs = read_meta(states)
    place = jnp.bitwise_xor(iota((group, LANES), 0), mine)
    whole_decay = jnp.sum(decays, axis=0, keepdims=True)
    after = whole_decay - decay_before(mine, place, decays) - decays
    doc = jnp.sum(jnp.where(place == group - 1, docs, 0.0), axis=0, keepdims=True)
    alive = docs == doc
    reached = jnp.where(alive, tops + after, FLOOR_NEG)
    top = jnp.max(reached, axis=0, keepdims=True)
    coefs = jnp.where(alive, jnp.exp(reached - top), 0.0)
    weighted(states, [out], [[coefs[i : i + 1] for i in range(group)]])
    normal = jnp.sum(wide(coefs, key_width) * normals, axis=0, keepdims=True)
    out[key_width:, :] = meta_rows(normal, top, whole_decay, doc, width)


def entering_kernel(group, reach, scalars, *refs):
    states, totals, outs = refs[:group], refs[group : group + reach], refs[group + reach :]
    mine = scalars[0]
    key_width, width = outs[0].shape[0] - META, outs[0].shape[1]
    normals, tops, decays, docs = read_meta(states)
    far_normals, far_tops, far_decays, far_docs = read_meta(totals)
    place = jnp.bitwise_xor(iota((group, LANES), 0), mine)
    before = decay_before(mine, place, decays)
    zero = jnp.zeros((1, LANES), F32)
    far_reached, passed, lines = [], zero, []
    for d in range(reach):
        far_reached.append(far_tops[d : d + 1] + passed)
        passed = passed + far_decays[d : d + 1]
    far_reached = jnp.concatenate(far_reached, axis=0)
    for r in range(group):
        here = jnp.bitwise_xor(mine, r)
        doc = jnp.sum(jnp.where(place == here - 1, docs, 0.0), axis=0, keepdims=True)
        doc = jnp.where(here == 0, far_docs[0:1], doc)
        mark = before[r : r + 1]
        alive = (place < here) & (docs == doc)
        reached = jnp.where(alive, tops + (mark - before - decays), FLOOR_NEG)
        far_alive = (far_docs == doc) & (far_docs > 0.5)
        far = jnp.where(far_alive, far_reached + mark, FLOOR_NEG)
        top = jnp.maximum(
            jnp.max(reached, axis=0, keepdims=True), jnp.max(far, axis=0, keepdims=True)
        )
        coefs = jnp.where(alive, jnp.exp(reached - top), 0.0)
        far_coefs = jnp.where(far_alive, jnp.exp(far - top), 0.0)
        lines.append(
            [None if i == r else coefs[i : i + 1] for i in range(group)]
            + [far_coefs[d : d + 1] for d in range(reach)]
        )
        normal = jnp.sum(wide(coefs, key_width) * normals, axis=0, keepdims=True)
        normal = normal + jnp.sum(wide(far_coefs, key_width) * far_normals, axis=0, keepdims=True)
        outs[r][key_width:, :] = meta_rows(normal, top, zero, doc, width)
    weighted(list(states) + list(totals), outs, lines)


def local_kernel(first_slot, heads, scalars, *refs):
    q_own, k_own, v_own, q_oth, k_oth, v_oth, source_rows, decay_rows, columns, docs_ref = refs[:10]
    numerators, stats = refs[-2:]
    mine, core = scalars[0], scalars[1]
    tokens, key_width = q_own.shape[1:]
    length = 2 * tokens
    scaling = key_width**-0.5
    is_first = core == 0
    lane = iota((length, LANES), 1)
    turned = columns[...]
    docs = turned[:, heads : heads + 1]
    source_docs = docs_ref[...]
    causal = iota((tokens, tokens), 0) >= iota((tokens, tokens), 1)
    for step in range(numerators.shape[0]):
        local_head = jnp.bitwise_xor(mine, first_slot + step)
        head = (heads // 2) * core + local_head
        source = source_rows[pl.ds(head, 1), :]
        decay = jnp.sum(jnp.where(lane == head, turned, 0.0), axis=1, keepdims=True)

        def ordered(own, other):
            own, other = own[local_head], other[local_head]
            return jnp.where(is_first, own, other), jnp.where(is_first, other, own)

        queries, keys, values = ordered(q_own, q_oth), ordered(k_own, k_oth), ordered(v_own, v_oth)
        for block in range(2):
            rows = slice(block * tokens, (block + 1) * tokens)
            exponents = []
            for s in range(block + 1):
                cols = slice(s * tokens, (s + 1) * tokens)
                allowed = docs[rows] == source_docs[:, cols]
                if s == block:
                    allowed = allowed & causal
                exponents.append(jnp.where(allowed, decay[rows] + source[:, cols], FLOOR_NEG))
            stabilizer = functools.reduce(
                jnp.maximum, [jnp.max(x, axis=1, keepdims=True) for x in exponents]
            )
            factors, sources, denominator = [], [], None
            for s in range(block + 1):
                weights = dot(queries[block], keys[s], NT) * scaling
                weights = weights * jnp.exp(exponents[s] - stabilizer)
                high = weights.astype(BF16)
                factors.append(high)
                sources.append(values[s])
                if s < block:
                    factors.append((weights - high.astype(F32)).astype(BF16))
                    sources.append(values[s])
                part = jnp.sum(weights, axis=1, keepdims=True)
                denominator = part if s == 0 else denominator + part
            numerator = dot(jnp.concatenate(factors, axis=1), jnp.concatenate(sources, axis=0))
            side = core if block == 0 else 1 - core
            numerators[step, side] = numerator
            first_lane = iota((tokens, LANES), 1) == 0
            pair = jnp.where(first_lane, stabilizer, denominator).T
            stats[step, side] = jnp.concatenate(
                [pair[:2], decay_rows[pl.ds(head, 1), rows], source_docs[:, rows], pair[4:8]], axis=0
            )


def output_kernel(first, count, scalars, q_own, q_oth, *refs):
    terms, entering, (keep, send) = refs[:4], refs[4 : 4 + count], refs[4 + count :]
    key_width = q_own.shape[2]
    scaling = key_width**-0.5
    early = terms[0].shape[0]
    for i, payload in enumerate(entering):
        slot = first + i
        numerators, stats = terms[:2] if slot < early else terms[2:]
        at = slot % early
        local_head = jnp.bitwise_xor(scalars[0], slot)
        normal, top, _, doc = read_meta([payload])
        pieces = split3(normal) + (jnp.zeros((PAD - 3, key_width), F32),)
        pieces = jnp.concatenate(pieces, axis=0).astype(BF16)
        memory = payload[:key_width, :]
        width = memory.shape[1]
        for side, (q_ref, out) in enumerate(((q_own, keep), (q_oth, send))):
            query = q_ref[local_head]
            tokens = query.shape[0]
            stat = stats[at, side]
            local = stat[0:1]
            alive = stat[3:4] == wide(doc, tokens)
            carried = jnp.where(alive, stat[2:3] + wide(top, tokens), FLOOR_NEG)
            stabilizer = jnp.maximum(local, carried)
            shrink = jnp.exp(local - stabilizer)
            retained = jnp.exp(carried - stabilizer) * scaling
            seen = dot(pieces, query, NT)
            seen = (seen[2:3] + seen[1:2]) + seen[0:1]
            denominator = shrink * stat[1:2] + retained * seen
            inverse = 1.0 / jnp.maximum(jnp.abs(denominator), 1.0)
            near = jnp.broadcast_to(shrink * inverse, (LANES, tokens)).T
            far = jnp.broadcast_to(retained * inverse, (LANES, tokens)).T
            result = wide(near, width) * numerators[at, side]
            out[i] = (result + wide(far, width) * dot(query, memory)).astype(BF16)


def merge_kernel(heads, scalars, *refs):
    stacks, (out, result, written) = refs[:-3], refs[-3:]
    half = heads // 2
    n = LAY // heads
    mine, core = scalars[0], scalars[1]
    into, given = iota((LAY, LAY), 0), iota((LAY, LAY), 1)
    index = given // n
    slot = jnp.bitwise_and(index, half - 1)
    side = jnp.where(index < half, core, 1 - core)
    head = side * half + jnp.bitwise_xor(slot, mine)
    order = ((into % heads == head) & (into // heads == given % n)).astype(BF16)
    _, tokens, width = stacks[0].shape
    copies = []
    for g in range(tokens // n):
        span = slice(g * n, (g + 1) * n)
        rows = jnp.concatenate([stack[:, span, :] for stack in stacks], axis=0)
        turned = dot(order, rows.reshape(LAY, width))
        result[span] = turned.reshape(n, heads, width).astype(BF16)
        copies.append(pltpu.make_async_copy(result.at[span], out.at[span], written.at[g]))
        copies[-1].start()
    for copy in copies:
        copy.wait()


def whole(shape):
    return pl.BlockSpec(shape, lambda *_: (0,) * len(shape))


def params():
    return pltpu.CompilerParams(vmem_limit_bytes=16 * 2**20)


SMEM = pl.BlockSpec(memory_space=pltpu.SMEM)
VMEM = pl.BlockSpec(memory_space=pltpu.VMEM)


def shape_of(*dims, dtype=BF16):
    return jax.ShapeDtypeStruct(dims, dtype)


def local(devices, queries, key_vectors, value_vectors, input_gate, forget_gate, doc_ids):
    tokens, heads, key_width = queries.shape
    value_width = value_vectors.shape[2]
    half = heads // 2
    group = half
    chips = devices // 2
    levels = chips // group
    reach = max(1, levels // 2)
    ctx, hv = lax.axis_index("ctx"), lax.axis_index("hv")
    chip = ctx * (lax.axis_size("hv") // 2) + hv // 2
    scalars = jnp.stack([chip % group, hv % 2]).astype(jnp.int32)
    ids = doc_ids[None, :]

    def swap_cores(x):
        return lax.ppermute(x, AXES, [(d, d ^ 1) for d in range(devices)])

    def in_group(x, r):
        pairs = [(d, d ^ (2 * r)) for d in range(devices)]
        return lax.ppermute(x, AXES, pairs)

    def to_next(x):
        jump = 2 * group
        return lax.ppermute(x, AXES, [(d, d + jump) for d in range(devices - jump)])

    rows = key_width + META
    state = (rows, value_width)
    sizes = {key_width: (half, tokens, key_width), value_width: (half, tokens, value_width)}

    def relayout(*sources):
        outs = [sizes[x.shape[2]] for x in sources] * 2
        return pl.pallas_call(
            functools.partial(relayout_kernel, half, len(sources)),
            in_specs=[whole(x.shape) for x in sources],
            out_specs=[VMEM] * len(outs),
            out_shape=[shape_of(*s) for s in outs],
            compiler_params=params(),
                name="relayout",
        )(*sources)

    gates = jnp.concatenate([input_gate.T, forget_gate.T], axis=0)
    gates, value_vectors = lax.optimization_barrier((gates, value_vectors))
    gates_oth = swap_cores(gates)
    v_keep, v_send = relayout(value_vectors)
    gates_oth, v_send = lax.optimization_barrier((gates_oth, v_send))
    v_oth = swap_cores(v_send)
    k_keep, k_send = relayout(key_vectors)
    k_oth = swap_cores(k_send)
    gate_shapes = [
        (heads, 2 * tokens),
        (heads, LANES),
        (heads, LANES),
        (heads, 2 * tokens),
        (heads, 2 * tokens),
        (2 * tokens, LANES),
        (1, 2 * tokens),
    ]
    factors, tops, decays, source_rows, decay_rows, columns, docs = pl.pallas_call(
        functools.partial(gates_kernel, heads),
        in_specs=[SMEM, VMEM, VMEM, VMEM],
        out_specs=[VMEM] * len(gate_shapes),
        out_shape=[shape_of(*s, dtype=F32) for s in gate_shapes],
        compiler_params=params(),
        name="gates",
    )(scalars, gates, gates_oth, ids)

    by_core = (k_keep, v_keep, k_oth, v_oth, factors, tops, decays, docs)
    def states_of(slots):
        return pl.pallas_call(
            functools.partial(state_kernel, heads, slots),
            in_specs=[SMEM] + [VMEM] * len(by_core),
            out_specs=[VMEM] * len(slots),
            out_shape=[shape_of(*state)] * len(slots),
            compiler_params=params(),
            name="states",
        )(scalars, *by_core)
    made = [None] * group
    for first in (1, 0):
        slots = tuple(range(first, group, 2))
        for slot, out in zip(slots, states_of(slots), strict=True):
            made[slot] = out
    gathered = [made[0]] + [in_group(made[r], r) for r in range(1, group)]
    total = pl.pallas_call(
        functools.partial(total_kernel, group),
        in_specs=[SMEM] + [VMEM] * group,
        out_specs=VMEM,
        out_shape=shape_of(*state),
        compiler_params=params(),
        name="group_total",
    )(scalars, *gathered)
    queries, gathered[0] = lax.optimization_barrier((queries, gathered[0]))
    q_keep, q_send = relayout(queries)
    q_oth = swap_cores(q_send)
    small = (source_rows, decay_rows, columns, docs)
    early = half // 2

    def own_terms(first_slot, q_own):
        operands = (q_own, k_keep, v_keep, q_oth, k_oth, v_oth, *small)
        return pl.pallas_call(
            functools.partial(local_kernel, first_slot, heads),
            in_specs=[SMEM] + [VMEM] * len(operands),
            out_specs=[VMEM] * 2,
            out_shape=[
                shape_of(early, 2, tokens, value_width, dtype=F32),
                shape_of(early, 2, 8, tokens, dtype=F32),
            ],
            compiler_params=params(),
            name="own_terms",
        )(scalars, *operands)

    q_first, _ = lax.optimization_barrier((q_keep, total))
    first_terms = own_terms(0, q_first)
    totals = [to_next(total)]
    totals[0], first_terms = lax.optimization_barrier((totals[0], first_terms))
    while len(totals) < reach:
        totals.append(to_next(totals[-1]))
    q_last, _ = lax.optimization_barrier((q_keep, totals[0]))
    last_terms = own_terms(early, q_last)
    gathered[0], last_terms = lax.optimization_barrier((gathered[0], last_terms))
    terms = [*first_terms, *last_terms]

    leaving = pl.pallas_call(
        functools.partial(entering_kernel, group, reach),
        in_specs=[SMEM] + [VMEM] * (group + reach),
        out_specs=[VMEM] * group,
        out_shape=[shape_of(*state)] * group,
        compiler_params=params(),
        name="entering",
    )(scalars, *gathered, *totals)
    entering = [leaving[0]] + [in_group(leaving[r], r) for r in range(1, group)]

    def outputs(first, count):
        return pl.pallas_call(
            functools.partial(output_kernel, first, count),
            in_specs=[SMEM] + [VMEM] * (6 + count),
            out_specs=[VMEM] * 2,
            out_shape=[shape_of(count, tokens, value_width)] * 2,
            compiler_params=params(),
            name="outputs",
        )(scalars, q_keep, q_oth, *terms, *entering[first : first + count])

    kept, received = [], []
    for r in range(group):
        keep, send = outputs(r, 1)
        kept.append(keep)
        received.append(swap_cores(send))
        if r == 0:
            terms, received[0] = lax.optimization_barrier((terms, received[0]))
        else:
            terms, _ = lax.optimization_barrier((terms, send))
    return pl.pallas_call(
        functools.partial(merge_kernel, heads),
        in_specs=[SMEM] + [VMEM] * heads,
        out_specs=pl.BlockSpec(memory_space=pl.ANY),
        out_shape=shape_of(*value_vectors.shape),
        scratch_shapes=[
            pltpu.VMEM(value_vectors.shape, BF16),
            pltpu.SemaphoreType.DMA((tokens // (LAY // heads),)),
        ],
        compiler_params=params(),
        name="merge",
    )(scalars, *kept, *received)


def solution(mesh):
    return jax.shard_map(
        functools.partial(local, mesh.size),
        mesh=mesh,
        in_specs=(
            P(AXES, None, None),
            P(AXES, None, None),
            P(AXES, None, None),
            P(AXES, None),
            P(AXES, None),
            P("ctx"),
        ),
        out_specs=P(AXES, None, None),
        check_vma=False,
    )
```
